128 devices in a mesh: dp: 4 (over z), shard: 32 (over y, x, core).
Axes of the slice: x: 4, y: 4, z: 4, core: 2. Of those that a mesh axis runs over, the one named last changes fastest.
Arguments:
- gradients: bfloat16 [4, 8, 512, 16, 512], P('dp', None, 'shard'), may hold values from -6 to 6
- owner_list: int32 [128], replicated, may hold values from 0 to 127, as said below
- row_offset: int32 [128], replicated, may hold values from 0 to 3584, as said below
- col_offset: int32 [128], replicated, may hold values from 0 to 7680, as said below
- left_factor: float32 [256, 512, 512], P(('dp', 'shard')), may hold values from -32 to 32, as said below
- right_factor: float32 [256, 512, 512], P(('dp', 'shard')), may hold values from -32 to 32, as said below
- left_root: float32 [256, 512, 512], P(('dp', 'shard')), may hold values from -2 to 2, as said below
- right_root: float32 [256, 512, 512], P(('dp', 'shard')), may hold values from -2 to 2, as said below
Outputs:
- update: bfloat16 [8, 512, 16, 512], P(None, 'shard', None, 'dp')
- new_left_factor: float32 [256, 512, 512], P(('dp', 'shard'))
- new_right_factor: float32 [256, 512, 512], P(('dp', 'shard'))
- new_left_root: float32 [256, 512, 512], P(('dp', 'shard'))
- new_right_root: float32 [256, 512, 512], P(('dp', 'shard'))
The draws below stay inside these ranges and needn't reach their ends.
Inputs may be any that keep to these rules, and one draw needn't show every extreme that they name: `owner_list`: no owner is named by more than 2 entries, and some owner by exactly 2. `row_offset`: multiples of 512; with col_offset, every block of the 8 x 16 grid is named exactly once. `col_offset`: multiples of 512; with row_offset, every block of the grid is named exactly once. `left_factor`: each slot symmetric positive definite. `right_factor`: each slot symmetric positive definite. `left_root`: each slot symmetric. `right_root`: each slot symmetric.
All inputs are finite; a program needn't handle non-finite values.
Results may differ from the reference program's by a relative error of at most 0.012.
Values may be sent and summed in bfloat16 or wider, within the bound.
No kernel may reach another device: no remote copies, remote signals or barrier semaphores. Data moves between devices by JAX's collectives and lax.ppermute only.
A program may use at most 128 MiB of HBM per device.

```python
import jax
import jax.numpy as jnp
from jax import lax

BLOCK = 512
SLOTS = 2
REPLICAS = 4
BC = 16
BR = 8
BLOCKS = 128
SLOTS_ALL = 256


def draw_owner_list(key, part):
    base = jax.random.fold_in(key, 7)
    first_key, second_key, third_key = jax.random.split(base, 3)
    owner_count = SLOTS_ALL // SLOTS
    starred = jax.random.randint(first_key, (), 0, owner_count)
    others = jax.random.permutation(second_key, SLOTS_ALL - SLOTS).astype(jnp.int32)
    others = others + SLOTS * (others >= SLOTS * starred).astype(jnp.int32)
    rest = others[:BLOCKS - SLOTS] // SLOTS
    owners = jnp.concatenate([jnp.full((SLOTS,), starred, jnp.int32), rest.astype(jnp.int32)])
    shuffle = jax.random.permutation(third_key, BLOCKS)
    return owners[shuffle].astype(jnp.int32)


def grid_order(key):
    return jax.random.permutation(jax.random.fold_in(key, 11), BLOCKS).astype(jnp.int32)


def draw_row_offset(key, part):
    return (grid_order(key) // BC * BLOCK).astype(jnp.int32)


def draw_col_offset(key, part):
    return (grid_order(key) % BC * BLOCK).astype(jnp.int32)


def factor_draw(key):
    first_key = jax.random.fold_in(key, 0)
    noise = jax.random.normal(first_key, (SLOTS_ALL, BLOCK, BLOCK), jnp.float32)
    gram = jnp.einsum('nij,nkj->nik', noise, noise, precision=lax.Precision.HIGHEST) / BLOCK
    return gram + 0.5 * jnp.eye(BLOCK, dtype=jnp.float32)[None]


def draw_left_factor(key, part):
    return factor_draw(jax.random.fold_in(key, 3))


def draw_right_factor(key, part):
    return factor_draw(jax.random.fold_in(key, 5))


def root_draw(key):
    noise = jax.random.normal(key, (SLOTS_ALL, BLOCK, BLOCK), jnp.float32)
    symmetric = (noise + jnp.swapaxes(noise, 1, 2)) / (2.0 * BLOCK ** 0.5)
    return jnp.eye(BLOCK, dtype=jnp.float32)[None] + 0.3 * symmetric


def draw_left_root(key, part):
    return root_draw(jax.random.fold_in(key, 13))


def draw_right_root(key, part):
    return root_draw(jax.random.fold_in(key, 17))


def level_of(stream_key, shape, cuts, smallest, largest):
    loudness = 1.0
    for axis_at, shards_of in cuts:
        draws = jax.random.uniform(jax.random.fold_in(jax.random.fold_in(stream_key, 6), axis_at), (shards_of,), jnp.float32, smallest / len(cuts), largest / len(cuts))
        loudness = loudness * jnp.repeat(jnp.exp(draws), shape[axis_at] // shards_of).reshape((-1,) + (1,) * (len(shape) - 1 - axis_at))
    return loudness


def centred(own_key, shape, scale, reach, cuts=(), kind=jnp.bfloat16):
    loudness = level_of(own_key, shape, cuts, -0.22, 0.18) if cuts else 1.0
    drawn = jax.random.normal(own_key, shape, jnp.float32) * scale * loudness
    return jnp.minimum(jnp.maximum(drawn, -reach), reach).astype(kind)


def setup_inputs(seed: int = 0) -> dict:
    splits = jax.random.split(jax.random.key(seed), 9)
    gradients = centred(splits[0], (REPLICAS, BR, BLOCK, BC, BLOCK), 0.5, 6.0, ((0, 4), (2, 32)))
    owner_list = draw_owner_list(jax.random.fold_in(splits[8], 71), 0)
    row_offset = draw_row_offset(jax.random.fold_in(splits[8], 71), 0)
    col_offset = draw_col_offset(jax.random.fold_in(splits[8], 71), 0)
    left_factor = draw_left_factor(jax.random.fold_in(splits[8], 71), 0)
    right_factor = draw_right_factor(jax.random.fold_in(splits[8], 71), 0)
    left_root = draw_left_root(jax.random.fold_in(splits[8], 71), 0)
    right_root = draw_right_root(jax.random.fold_in(splits[8], 71), 0)
    return {"gradients": gradients, "owner_list": owner_list, "row_offset": row_offset, "col_offset": col_offset, "left_factor": left_factor, "right_factor": right_factor, "left_root": left_root, "right_root": right_root}


decay_rate = 0.9
highest = lax.Precision.HIGHEST


def newton_root(factor, old_root):
    identity = jnp.eye(factor.shape[0], dtype=factor.dtype)
    normed = factor * (factor.shape[0] / jnp.trace(factor))
    root_sq = jnp.dot(old_root, old_root, precision=highest)
    root_quad = jnp.dot(root_sq, root_sq, precision=highest)
    coupled = jnp.dot(root_quad, normed, precision=highest)
    newton_t = (5.0 * identity - coupled) / 4.0
    return jnp.dot(old_root, newton_t, precision=highest)


def per_block(inputs):
    g_block, left_old, right_old, left_prev, right_prev = inputs
    gram_left = jnp.dot(g_block, g_block.T, preferred_element_type=jnp.float32)
    gram_right = jnp.dot(g_block.T, g_block, preferred_element_type=jnp.float32)
    left_new = decay_rate * left_old + ((1.0 - decay_rate) / BLOCK) * gram_left
    right_new = decay_rate * right_old + ((1.0 - decay_rate) / BLOCK) * gram_right
    left_next = newton_root(left_new, left_prev)
    right_next = newton_root(right_new, right_prev)
    g_float = g_block.astype(jnp.float32)
    result = jnp.dot(jnp.dot(left_next, g_float, precision=highest), right_next, precision=highest)
    return result.astype(jnp.bfloat16), left_new, right_new, left_next, right_next


def reference(gradients, owner_list, row_offset, col_offset, left_factor, right_factor, left_root, right_root):
    summed = jnp.sum(gradients.astype(jnp.float32), axis=0).astype(jnp.bfloat16)
    block_row = (row_offset // BLOCK).astype(jnp.int32)
    block_col = (col_offset // BLOCK).astype(jnp.int32)
    entry_index = jnp.arange(BLOCKS, dtype=jnp.int32)
    same_owner = owner_list[None, :] == owner_list[:, None]
    earlier = jnp.sum(same_owner & (entry_index[None, :] < entry_index[:, None]), axis=1).astype(jnp.int32)
    slot_of = (owner_list * SLOTS + earlier).astype(jnp.int32)
    pieces = summed[block_row, :, block_col, :]
    outputs = lax.map(per_block, (pieces, left_factor[slot_of], right_factor[slot_of], left_root[slot_of], right_root[slot_of]))
    blocks_out, left_new, right_new, left_next, right_next = outputs
    update = jnp.zeros((BR, BLOCK, BC, BLOCK), jnp.bfloat16).at[block_row, :, block_col, :].set(blocks_out)
    new_left_factor = left_factor.at[slot_of].set(left_new)
    new_right_factor = right_factor.at[slot_of].set(right_new)
    new_left_root = left_root.at[slot_of].set(left_next)
    new_right_root = right_root.at[slot_of].set(right_next)
    return update, new_left_factor, new_right_factor, new_left_root, new_right_root
```

```python
import functools

import jax
import jax.numpy as jnp
from jax import lax
from jax.experimental import pallas as pl
from jax.experimental.pallas import tpu as pltpu
from jax.sharding import PartitionSpec as P

decay_rate = 0.9
f32 = jnp.float32
bf16 = jnp.bfloat16
MIB = 1 << 20


def params(mib):
    return pltpu.CompilerParams(vmem_limit_bytes=mib * MIB)


def halves(x):
    high = x.astype(bf16)
    return high, (x - high.astype(f32)).astype(bf16)


def mul(a, b):
    return jnp.dot(a, b, preferred_element_type=f32)


def mul_t(a, b):
    return lax.dot_general(a, b, (((1,), (1,)), ((), ())), preferred_element_type=f32)


def t_mul(a, b):
    return lax.dot_general(a, b, (((0,), (0,)), ((), ())), preferred_element_type=f32)


def mul3(a, b):
    return mul(a[0], b[0]) + (mul(a[0], b[1]) + mul(a[1], b[0]))


def gather_kernel(per_step, rows, cols, table, own, one, two, three, out, held):
    step = pl.program_id(0)

    @pl.when(step == 0)
    def _():
        out[...] = jnp.zeros_like(out)

    for b in range(per_step):
        total = own[b].astype(f32) + one[b].astype(f32)
        total = total + (two[b].astype(f32) + three[b].astype(f32))
        held[b] = total.reshape(rows * cols, total.shape[-1])
        for c in range(cols):
            piece = held[b, pl.ds(c, rows, stride=cols), :]
            slot = table[(step * per_step + b) * cols + c]
            out[slot] = piece.astype(out.dtype)


def gather_pieces(table, me, own, arrived, slots):
    row_blocks, rows, cols, width = arrived[0].shape
    per_step = 2
    spec = pl.BlockSpec((per_step, rows, cols, width), lambda i, *_: (i, 0, 0, 0))

    def kernel(table_ref, me_ref, *refs):
        gather_kernel(per_step, rows, cols, table_ref, *refs)

    return pl.pallas_call(
        kernel,
        out_shape=jax.ShapeDtypeStruct((slots, rows, width), bf16),
        grid_spec=pltpu.PrefetchScalarGridSpec(
            num_scalar_prefetch=2,
            grid=(row_blocks // per_step,),
            in_specs=[
                pl.BlockSpec(
                    (per_step, rows, cols, width), lambda i, t, m: (i, 0, 0, m[0])
                ),
                spec,
                spec,
                spec,
            ],
            out_specs=pl.BlockSpec((slots, rows, width), lambda i, *_: (0, 0, 0)),
            scratch_shapes=[pltpu.VMEM((per_step, rows * cols, width), f32)],
        ),
        compiler_params=params(16),
        name="sum_and_gather",
    )(table, me, own, *arrived)


def place_kernel(per_step, rows, cols, table, arrived, out, held):
    step = pl.program_id(0)
    for b in range(per_step):
        for c in range(cols):
            slot = table[(step * per_step + b) * cols + c]
            held[b, pl.ds(c, rows, stride=cols), :] = arrived[slot].astype(f32)
        out[b] = held[b].reshape(rows, cols, held.shape[-1]).astype(out.dtype)


def place_pieces(table, arrived, row_blocks, cols):
    slots, rows, width = arrived.shape
    per_step = 4
    return pl.pallas_call(
        functools.partial(place_kernel, per_step, rows, cols),
        out_shape=jax.ShapeDtypeStruct((row_blocks, rows, cols, width), bf16),
        grid_spec=pltpu.PrefetchScalarGridSpec(
            num_scalar_prefetch=1,
            grid=(row_blocks // per_step,),
            in_specs=[pl.BlockSpec((slots, rows, width), lambda i, t: (0, 0, 0))],
            out_specs=pl.BlockSpec(
                (per_step, rows, cols, width), lambda i, t: (i, 0, 0, 0)
            ),
            scratch_shapes=[pltpu.VMEM((per_step, rows * cols, width), f32)],
        ),
        compiler_params=params(16),
        name="place_pieces",
    )(table, arrived)


def early_kernel(count, root, factor, five_high, five_low, product):
    @pl.when(pl.program_id(0) < count[0])
    def _():
        x = halves(root[0])
        square = halves(mul3(x, x))
        fourth = halves(mul3(square, square))
        fifth = halves(mul3(x, fourth))
        five_high[0], five_low[0] = fifth
        product[0] = decay_rate * mul3(fifth, halves(factor[0]))


def early(count, root, factor):
    slots, n, _ = root.shape
    spec = pl.BlockSpec((1, n, n), lambda i, c: (i, 0, 0))
    return pl.pallas_call(
        early_kernel,
        out_shape=(
            jax.ShapeDtypeStruct((slots, n, n), bf16),
            jax.ShapeDtypeStruct((slots, n, n), bf16),
            jax.ShapeDtypeStruct((slots, n, n), f32),
        ),
        grid_spec=pltpu.PrefetchScalarGridSpec(
            num_scalar_prefetch=1,
            grid=(slots,),
            in_specs=[spec, spec],
            out_specs=(spec, spec, spec),
        ),
        compiler_params=params(32),
        cost_estimate=pl.CostEstimate(
            flops=slots * 12 * 2 * n**3,
            bytes_accessed=slots * 16 * n * n,
            transcendentals=0,
        ),
        name="early_products",
    )(count, root, factor)


def assembled(pieces, block):
    parts, shards, _, rows, width = pieces.shape
    for z in range(parts):
        block[:, z * width : (z + 1) * width] = pieces[z, :, 0].reshape(
            shards * rows, width
        )
    return block[...]


def scale_of(trace, block, gain):
    g = block.astype(f32)
    n = block.shape[0]
    return n / (decay_rate * trace + gain * jnp.sum(g * g))


def update_kernel(
    gain, count, traces, pieces, xl, xr, pl_, pr, fl, fr, out, block
):
    t = pl.program_id(0)

    @pl.when(t < count[0])
    def _():
        g = assembled(pieces, block)
        slots = pl.num_programs(0)
        left_scale = scale_of(traces[t], g, gain)
        right_scale = scale_of(traces[slots + t], g, gain)
        m = mul_t(mul(fl[0], g).astype(bf16), g)
        left = 1.25 * xl[0] - (0.25 * left_scale) * (pl_[0] + gain * m)
        m = mul(mul_t(fr[0], g).astype(bf16), g)
        right = 1.25 * xr[0] - (0.25 * right_scale) * (pr[0] + gain * m)
        half = mul(left.astype(bf16), g).astype(bf16)
        done = mul(half, right.astype(bf16)).astype(bf16)
        parts, shards, _, rows, width = out.shape
        for z in range(parts):
            out[z, :, 0] = done[:, z * width : (z + 1) * width].reshape(
                shards, rows, width
            )

    @pl.when(t >= count[0])
    def _():
        out[...] = jnp.zeros_like(out)


def update_pieces(gain, count, traces, pieces, xl, xr, pl_, pr, fl, fr):
    parts, shards, slots, rows, width = pieces.shape
    n = xl.shape[1]
    piece_spec = pl.BlockSpec(
        (parts, shards, 1, rows, width), lambda i, *_: (0, 0, i, 0, 0)
    )
    spec = pl.BlockSpec((1, n, n), lambda i, *_: (i, 0, 0))
    return pl.pallas_call(
        functools.partial(update_kernel, gain),
        out_shape=jax.ShapeDtypeStruct(pieces.shape, bf16),
        grid_spec=pltpu.PrefetchScalarGridSpec(
            num_scalar_prefetch=2,
            grid=(slots,),
            in_specs=[piece_spec] + [spec] * 6,
            out_specs=piece_spec,
            scratch_shapes=[pltpu.VMEM((n, n), bf16)],
        ),
        compiler_params=params(32),
        name="update_pieces",
    )(count, traces, pieces, xl, xr, pl_, pr, fl, fr)


def state_kernel(
    gain, count, traces, pieces,
    xl, xr, pl_, pr, flh, fll, frh, frl, left, right,
    new_left, new_right, new_xl, new_xr, block,
):
    t = pl.program_id(0)

    @pl.when(t < count[0])
    def _():
        g = assembled(pieces, block)
        slots = pl.num_programs(0)
        left_scale = scale_of(traces[t], g, gain)
        right_scale = scale_of(traces[slots + t], g, gain)
        new_left[0] = decay_rate * left[0] + gain * mul_t(g, g)
        new_right[0] = decay_rate * right[0] + gain * t_mul(g, g)
        high, low = halves(mul(flh[0], g) + mul(fll[0], g))
        m = mul_t(high, g) + mul_t(low, g)
        new_xl[0] = 1.25 * xl[0] - (0.25 * left_scale) * (pl_[0] + gain * m)
        high, low = halves(mul_t(frh[0], g) + mul_t(frl[0], g))
        m = mul(high, g) + mul(low, g)
        new_xr[0] = 1.25 * xr[0] - (0.25 * right_scale) * (pr[0] + gain * m)

    @pl.when(t >= count[0])
    def _():
        new_left[...] = left[...]
        new_right[...] = right[...]
        new_xl[...] = xl[...]
        new_xr[...] = xr[...]


def new_state(gain, count, traces, pieces, *arrays):
    parts, shards, slots, rows, width = pieces.shape
    n = arrays[0].shape[1]
    spec = pl.BlockSpec((1, n, n), lambda i, *_: (i, 0, 0))
    return pl.pallas_call(
        functools.partial(state_kernel, gain),
        out_shape=(jax.ShapeDtypeStruct((slots, n, n), f32),) * 4,
        grid_spec=pltpu.PrefetchScalarGridSpec(
            num_scalar_prefetch=2,
            grid=(slots,),
            in_specs=[
                pl.BlockSpec(
                    (parts, shards, 1, rows, width), lambda i, *_: (0, 0, i, 0, 0)
                )
            ]
            + [spec] * len(arrays),
            out_specs=(spec,) * 4,
            scratch_shapes=[pltpu.VMEM((n, n), bf16)],
        ),
        compiler_params=params(48),
        cost_estimate=pl.CostEstimate(
            flops=slots * 10 * 2 * n**3,
            bytes_accessed=slots * 44 * n * n,
            transcendentals=0,
        ),
        name="new_state",
    )(count, traces, pieces, *arrays)


def body(
    gradients, owner_list, row_offset, col_offset, left_factor, right_factor, left_root, right_root
):
    replicas = lax.axis_size("dp")
    shards = lax.axis_size("shard")
    slots, n, _ = left_factor.shape
    _, row_blocks, rows, cols, _ = gradients.shape
    width = n // replicas
    gain = (1.0 - decay_rate) / n
    me = lax.axis_index("dp")
    mine = gradients[0]

    arrived = []
    for hop in (2, 1, 3):
        to = lax.rem(me + hop, replicas)
        part = lax.dynamic_slice_in_dim(mine, to * width, width, axis=3)
        pairs = [(i, (i + hop) % replicas) for i in range(replicas)]
        arrived.append(lax.ppermute(part, "dp", pairs))

    entries = jnp.arange(owner_list.shape[0], dtype=jnp.int32)
    same = owner_list[None, :] == owner_list[:, None]
    earlier = jnp.sum(same & (entries[None, :] < entries[:, None]), axis=1)
    slot_of = owner_list * slots + earlier.astype(jnp.int32)
    block_of = row_offset // n * cols + col_offset // n
    table = jnp.sum(
        jnp.where(block_of[None, :] == entries[:, None], slot_of[None, :], 0), axis=1
    ).astype(jnp.int32)
    owner = lax.axis_index(("dp", "shard"))
    count = jnp.sum((owner_list == owner).astype(jnp.int32)).reshape(1)

    flh, fll, pl_ = early(count, left_root, left_factor)
    frh, frl, pr = early(count, right_root, right_factor)
    traces = jnp.concatenate(
        [jnp.trace(left_factor, axis1=1, axis2=2), jnp.trace(right_factor, axis1=1, axis2=2)]
    )

    all_slots = replicas * shards * slots
    outgoing = gather_pieces(table, me.reshape(1).astype(jnp.int32), mine, arrived, all_slots)
    incoming = lax.all_to_all(outgoing, ("dp", "shard"), split_axis=0, concat_axis=0, tiled=True)
    pieces = incoming.reshape(replicas, shards, slots, rows, width)
    outbound = update_pieces(
        gain, count, traces, pieces, left_root, right_root, pl_, pr, flh, frh
    )
    returned = lax.all_to_all(
        outbound.reshape(all_slots, rows, width),
        ("dp", "shard"), split_axis=0, concat_axis=0, tiled=True,
    )
    new_left, new_right, new_xl, new_xr = new_state(
        gain, count, traces, pieces,
        left_root, right_root, pl_, pr, flh, fll, frh, frl, left_factor, right_factor,
    )
    update = place_pieces(table, returned, row_blocks, cols)
    return update, new_left, new_right, new_xl, new_xr


def solution(mesh):
    slots = P(("dp", "shard"), None, None)
    in_specs = (P("dp", None, "shard", None, None), P(), P(), P(), slots, slots, slots, slots)
    out_specs = (P(None, "shard", None, "dp"), slots, slots, slots, slots)
    return jax.shard_map(body, mesh=mesh, in_specs=in_specs, out_specs=out_specs, check_vma=False)
```

```python
import functools

import jax
import jax.numpy as jnp
from jax import lax
from jax.experimental import pallas as pl
from jax.experimental.pallas import tpu as pltpu
from jax.sharding import PartitionSpec as P

decay_rate = 0.9
f32 = jnp.float32
bf16 = jnp.bfloat16
MIB = 1 << 20


def params(mib):
    return pltpu.CompilerParams(vmem_limit_bytes=mib * MIB)


def halves(x):
    high = x.astype(bf16)
    return high, (x - high.astype(f32)).astype(bf16)


def mul(a, b):
    return jnp.dot(a, b, preferred_element_type=f32)


def mul_t(a, b):
    return lax.dot_general(a, b, (((1,), (1,)), ((), ())), preferred_element_type=f32)


def t_mul(a, b):
    return lax.dot_general(a, b, (((0,), (0,)), ((), ())), preferred_element_type=f32)


def mul3(a, b):
    return mul(a[0], b[0]) + (mul(a[0], b[1]) + mul(a[1], b[0]))


def vmem(x):
    return pltpu.with_memory_space_constraint(x, pltpu.VMEM)


def hbm(x):
    return pltpu.with_memory_space_constraint(x, pltpu.HBM)


def stored(*shape, dtype=f32):
    return pltpu.HBM(shape, dtype)


whole = pl.BlockSpec(memory_space=pltpu.VMEM)
scalars = pl.BlockSpec(memory_space=pltpu.SMEM)
in_place = pl.BlockSpec(memory_space=pl.ANY)


def window_kernel(at, mine, *refs):
    outs, sem = refs[:-1], refs[-1]
    copies = []
    for k, out in enumerate(outs):
        height, rows, cols, width = out.shape
        column = pl.multiple_of(at[2 * k + 1] * width, width)
        copy = pltpu.make_async_copy(
            mine.at[pl.ds(at[2 * k], height), :, :, pl.ds(column, width)],
            out,
            sem.at[k],
        )
        copy.start()
        copies.append(copy)
    for copy in copies:
        copy.wait()


def windows(mine, width, pairs, name):
    row_blocks, rows, cols, _ = mine.shape
    at = jnp.stack([jnp.asarray(v, jnp.int32) for pair in pairs for v in pair])
    return pl.pallas_call(
        window_kernel,
        out_shape=(stored(row_blocks // 2, rows, cols, width, dtype=bf16),) * len(pairs),
        in_specs=[scalars, in_place],
        out_specs=(in_place,) * len(pairs),
        scratch_shapes=[pltpu.SemaphoreType.DMA((len(pairs),))],
        compiler_params=params(2),
        name=name,
    )(at, hbm(mine))


def merge_kernel(at, mine, low_in, high_in, low_out, high_out):
    half, rows, cols, width = low_in.shape
    for k, (came, out) in enumerate(((low_in, low_out), (high_in, high_out))):
        column = pl.ds(pl.multiple_of(at[k] * width, width), width)
        for b in range(half):
            own = mine[k * half + b, :, :, column].astype(f32)
            out[b] = (own + came[b].astype(f32)).astype(bf16)


def merged(mine, at, low_in, high_in):
    return pl.pallas_call(
        merge_kernel,
        out_shape=(jax.ShapeDtypeStruct(low_in.shape, bf16),) * 2,
        in_specs=[scalars] + [whole] * 3,
        out_specs=(whole, whole),
        compiler_params=params(4),
        name="merge_far_part",
    )(at, mine, vmem(low_in), vmem(high_in))


def gather_kernel(table, me, mine, ups, downs, ups_more, downs_more, out, held):
    row_blocks, rows, cols, _ = mine.shape
    width = ups.shape[-1]
    half = row_blocks // 2
    column = pl.ds(pl.multiple_of(me[0] * width, width), width)
    out[...] = jnp.zeros_like(out)
    for b in range(row_blocks):
        near, far = (downs, ups_more) if b < half else (ups, downs_more)
        total = mine[b, :, :, column].astype(f32) + near[b % half].astype(f32)
        total = total + far[b % half].astype(f32)
        held[b] = total.reshape(rows * cols, width)
        for c in range(cols):
            piece = held[b, pl.ds(c, rows, stride=cols), :]
            out[table[b * cols + c]] = piece.astype(out.dtype)


def gather_pieces(table, me, mine, arrived, slots):
    half, rows, cols, width = arrived[0].shape
    return pl.pallas_call(
        gather_kernel,
        out_shape=jax.ShapeDtypeStruct((slots, rows, width), bf16),
        in_specs=[scalars, scalars] + [whole] * 5,
        out_specs=whole,
        scratch_shapes=[pltpu.VMEM((2 * half, rows * cols, width), f32)],
        compiler_params=params(6),
        name="sum_and_gather",
    )(table, me, mine, *[vmem(a) for a in arrived])


def place_kernel(per_step, rows, cols, table, arrived, out, held):
    step = pl.program_id(0)
    for b in range(per_step):
        for c in range(cols):
            slot = table[(step * per_step + b) * cols + c]
            held[b, pl.ds(c, rows, stride=cols), :] = arrived[slot].astype(f32)
        out[b] = held[b].reshape(rows, cols, held.shape[-1]).astype(out.dtype)


def place_pieces(table, arrived, row_blocks, cols):
    slots, rows, width = arrived.shape
    per_step = 4
    return pl.pallas_call(
        functools.partial(place_kernel, per_step, rows, cols),
        out_shape=jax.ShapeDtypeStruct((row_blocks, rows, cols, width), bf16),
        grid=(row_blocks // per_step,),
        in_specs=[scalars, whole],
        out_specs=pl.BlockSpec((per_step, rows, cols, width), lambda i: (i, 0, 0, 0)),
        scratch_shapes=[pltpu.VMEM((per_step, rows * cols, width), f32)],
        compiler_params=params(4),
        name="place_pieces",
    )(table, vmem(arrived))


def early_kernel(t, sides, count, *refs):
    ins, outs = refs[: 2 * sides], refs[2 * sides : 6 * sides]
    roots, factors, highs, lows, products, in_sem, out_sem = refs[6 * sides :]

    @pl.when(t < count[0])
    def _():
        coming, going = [], []
        for k in range(sides):
            for i, held in enumerate((roots, factors)):
                copy = pltpu.make_async_copy(
                    ins[2 * k + i].at[t], held.at[k], in_sem.at[2 * k + i]
                )
                copy.start()
                coming.append(copy)
        for k in range(sides):
            coming[2 * k].wait()
            x = halves(roots[k])
            square = halves(mul3(x, x))
            fourth = halves(mul3(square, square))
            fifth = halves(mul3(x, fourth))
            highs[k], lows[k] = fifth
            coming[2 * k + 1].wait()
            n = roots.shape[1]
            total = jnp.zeros((128, 128), f32)
            on = lax.broadcasted_iota(jnp.int32, (128, 128), 0)
            on = on == lax.broadcasted_iota(jnp.int32, (128, 128), 1)
            for d in range(0, n, 128):
                total += factors[k, d : d + 128, d : d + 128]
            outs[4 * k + 3][0] = jnp.sum(jnp.where(on, total, 0.0))
            products[k] = decay_rate * mul3(fifth, halves(factors[k]))
            for i, held in enumerate((highs, lows, products)):
                copy = pltpu.make_async_copy(
                    held.at[k], outs[4 * k + i], out_sem.at[3 * k + i]
                )
                copy.start()
                going.append(copy)
        for copy in going:
            copy.wait()

    @pl.when(t >= count[0])
    def _():
        for k in range(sides):
            outs[4 * k + 3][0] = jnp.float32(0.0)


def early(t, count, *pairs):
    n = pairs[0].shape[1]
    sides = len(pairs) // 2
    made = pl.pallas_call(
        functools.partial(early_kernel, t, sides),
        out_shape=(
            stored(n, n, dtype=bf16),
            stored(n, n, dtype=bf16),
            stored(n, n),
            jax.ShapeDtypeStruct((1,), f32),
        )
        * sides,
        in_specs=[scalars] + [in_place] * len(pairs),
        out_specs=(in_place, in_place, in_place, scalars) * sides,
        scratch_shapes=[
            pltpu.VMEM((sides, n, n), f32),
            pltpu.VMEM((sides, n, n), f32),
            pltpu.VMEM((sides, n, n), bf16),
            pltpu.VMEM((sides, n, n), bf16),
            pltpu.VMEM((sides, n, n), f32),
            pltpu.SemaphoreType.DMA((2 * sides,)),
            pltpu.SemaphoreType.DMA((3 * sides,)),
        ],
        compiler_params=params(24),
        cost_estimate=pl.CostEstimate(
            flops=sides * 12 * 2 * n**3,
            bytes_accessed=sides * 16 * n * n,
            transcendentals=0,
        ),
        name="early_products",
    )(count, *[hbm(x) for x in pairs])
    return [made[4 * k : 4 * k + 4] for k in range(sides)]


def assembled(pieces, t, block):
    parts, shards, _, rows, width = pieces.shape
    for z in range(parts):
        block[:, z * width : (z + 1) * width] = pieces[z, :, t].reshape(
            shards * rows, width
        )
    return block[...]


def scale_of(trace, square, gain, n):
    return n / (decay_rate * trace + gain * square)


def update_kernel(gain, slots, count, pieces, xl, xr, *refs):
    ready, refs = refs[: 6 * slots], refs[6 * slots :]
    out, block, fives, singles, made, in_sem, out_sem = refs
    parts, shards, rows, width = made.shape[1:]
    n = xl.shape[1]

    def arrivals(t):
        fl, pl_, _, fr, pr, _ = ready[6 * t : 6 * t + 6]
        sources = (
            (fl, fives.at[t, 0]),
            (xl.at[t], singles.at[t, 0]),
            (pl_, singles.at[t, 1]),
            (fr, fives.at[t, 1]),
            (xr.at[t], singles.at[t, 2]),
            (pr, singles.at[t, 3]),
        )
        return [
            pltpu.make_async_copy(a, b, in_sem.at[t, k]) for k, (a, b) in enumerate(sources)
        ]

    def departure(t):
        return pltpu.make_async_copy(made.at[t], out.at[:, :, t], out_sem.at[t])

    for t in range(slots):

        @pl.when(t < count[0])
        def _():
            for copy in arrivals(t):
                copy.start()

    for t in range(slots):

        @pl.when(t < count[0])
        def _():
            copies = arrivals(t)
            g = assembled(pieces, t, block)
            wide = g.astype(f32)
            square = jnp.sum(wide * wide)
            left_scale = scale_of(ready[6 * t + 2][0], square, gain, n)
            right_scale = scale_of(ready[6 * t + 5][0], square, gain, n)
            copies[0].wait()
            m = mul_t(mul(fives[t, 0], g).astype(bf16), g)
            copies[1].wait()
            copies[2].wait()
            left = 1.25 * singles[t, 0] - (0.25 * left_scale) * (singles[t, 1] + gain * m)
            part = mul(left.astype(bf16), g).astype(bf16)
            copies[3].wait()
            m = mul(mul_t(fives[t, 1], g).astype(bf16), g)
            copies[4].wait()
            copies[5].wait()
            right = 1.25 * singles[t, 2] - (0.25 * right_scale) * (singles[t, 3] + gain * m)
            done = mul(part, right.astype(bf16)).astype(bf16)
            for z in range(parts):
                made[t, z] = done[:, z * width : (z + 1) * width].reshape(
                    shards, rows, width
                )

        @pl.when(t >= count[0])
        def _():
            made[t] = jnp.zeros_like(made[t])

        departure(t).start()
    for t in range(slots):
        departure(t).wait()


def update_pieces(gain, count, pieces, xl, xr, ready):
    parts, shards, slots, rows, width = pieces.shape
    n = xl.shape[1]
    inputs, specs = [], []
    for left, right in ready:
        for high, _, product, trace in (left, right):
            inputs += [hbm(high), hbm(product), trace]
            specs += [in_place, in_place, scalars]
    return pl.pallas_call(
        functools.partial(update_kernel, gain, slots),
        out_shape=stored(*pieces.shape, dtype=bf16),
        in_specs=[scalars, whole, in_place, in_place] + specs,
        out_specs=in_place,
        scratch_shapes=[
            pltpu.VMEM((n, n), bf16),
            pltpu.VMEM((slots, 2, n, n), bf16),
            pltpu.VMEM((slots, 4, n, n), f32),
            pltpu.VMEM((slots, parts, shards, rows, width), bf16),
            pltpu.SemaphoreType.DMA((slots, 6)),
            pltpu.SemaphoreType.DMA((slots,)),
        ],
        compiler_params=params(28),
        name="update_pieces",
    )(count, vmem(pieces), hbm(xl), hbm(xr), *inputs)


def state_kernel(gain, slots, count, pieces, left, right, xl, xr, *refs):
    ready, refs = refs[: 8 * slots], refs[8 * slots :]
    outs, refs = refs[:4], refs[4:]
    block, fives, singles, made, in_sem, out_sem = refs
    n = xl.shape[1]
    olds = (left, right, xl, xr)

    def arrivals(t):
        flh, fll, pl_, _, frh, frl, pr, _ = ready[8 * t : 8 * t + 8]
        sources = [(a, fives.at[t, k]) for k, a in enumerate((flh, fll, frh, frl))]
        sources += [(a.at[t], singles.at[t, k]) for k, a in enumerate(olds)]
        sources += [(a, singles.at[t, 4 + k]) for k, a in enumerate((pl_, pr))]
        return [
            pltpu.make_async_copy(a, b, in_sem.at[t, k]) for k, (a, b) in enumerate(sources)
        ]

    def departures(t):
        return [
            pltpu.make_async_copy(made.at[t, k], out.at[t], out_sem.at[t, k])
            for k, out in enumerate(outs)
        ]

    def carried(t):
        return [
            pltpu.make_async_copy(old.at[t], out.at[t], out_sem.at[t, k])
            for k, (old, out) in enumerate(zip(olds, outs))
        ]

    for t in range(slots):

        @pl.when(t < count[0])
        def _():
            for copy in arrivals(t):
                copy.start()

        @pl.when(t >= count[0])
        def _():
            for copy in carried(t):
                copy.start()

    for t in range(slots):

        @pl.when(t < count[0])
        def _():
            copies, leaving = arrivals(t), departures(t)
            g = assembled(pieces, t, block)
            wide = g.astype(f32)
            square = jnp.sum(wide * wide)
            left_scale = scale_of(ready[8 * t + 3][0], square, gain, n)
            right_scale = scale_of(ready[8 * t + 7][0], square, gain, n)
            for copy in copies:
                copy.wait()
            made[t, 0] = decay_rate * singles[t, 0] + gain * mul_t(g, g)
            leaving[0].start()
            made[t, 1] = decay_rate * singles[t, 1] + gain * t_mul(g, g)
            leaving[1].start()
            high, low = halves(mul(fives[t, 0], g) + mul(fives[t, 1], g))
            m = mul_t(high, g) + mul_t(low, g)
            made[t, 2] = 1.25 * singles[t, 2] - (0.25 * left_scale) * (singles[t, 4] + gain * m)
            leaving[2].start()
            high, low = halves(mul_t(fives[t, 2], g) + mul_t(fives[t, 3], g))
            m = mul(high, g) + mul(low, g)
            made[t, 3] = 1.25 * singles[t, 3] - (0.25 * right_scale) * (singles[t, 5] + gain * m)
            leaving[3].start()

    for t in range(slots):

        @pl.when(t < count[0])
        def _():
            for copy in departures(t):
                copy.wait()

        @pl.when(t >= count[0])
        def _():
            for copy in carried(t):
                copy.wait()


def new_state(gain, count, pieces, left, right, xl, xr, ready):
    slots, n, _ = left.shape
    inputs, specs = [], []
    for sides in ready:
        for high, low, product, trace in sides:
            inputs += [hbm(high), hbm(low), hbm(product), trace]
            specs += [in_place, in_place, in_place, scalars]
    return pl.pallas_call(
        functools.partial(state_kernel, gain, slots),
        out_shape=(stored(slots, n, n),) * 4,
        in_specs=[scalars, whole] + [in_place] * 4 + specs,
        out_specs=(in_place,) * 4,
        scratch_shapes=[
            pltpu.VMEM((n, n), bf16),
            pltpu.VMEM((slots, 4, n, n), bf16),
            pltpu.VMEM((slots, 6, n, n), f32),
            pltpu.VMEM((slots, 4, n, n), f32),
            pltpu.SemaphoreType.DMA((slots, 10)),
            pltpu.SemaphoreType.DMA((slots, 4)),
        ],
        compiler_params=params(40),
        cost_estimate=pl.CostEstimate(
            flops=slots * 10 * 2 * n**3,
            bytes_accessed=slots * 48 * n * n,
            transcendentals=0,
        ),
        name="new_state",
    )(count, vmem(pieces), *[hbm(x) for x in (left, right, xl, xr)], *inputs)


def body(
    gradients, owner_list, row_offset, col_offset, left_factor, right_factor, left_root, right_root
):
    replicas = lax.axis_size("dp")
    shards = lax.axis_size("shard")
    slots, n, _ = left_factor.shape
    _, row_blocks, rows, cols, _ = gradients.shape
    width = n // replicas
    gain = (1.0 - decay_rate) / n
    me = lax.axis_index("dp")
    mine = gradients[0]

    def hop(x, step):
        return lax.ppermute(x, "dp", [(i, (i + step) % replicas) for i in range(replicas)])

    def column(step):
        return lax.rem(me + step, replicas).astype(jnp.int32)

    half = row_blocks // 2
    far_low, far_high = windows(mine, width, ((0, column(2)), (half, column(2))), "far_parts")
    far_low, far_high = hop(far_low, 1), hop(far_high, -1)
    near_high, near_low = windows(
        mine, width, ((half, column(1)), (0, column(3))), "near_parts"
    )
    near_high, near_low = hop(near_high, 1), hop(near_low, -1)

    entries = jnp.arange(owner_list.shape[0], dtype=jnp.int32)
    same = owner_list[None, :] == owner_list[:, None]
    earlier = jnp.sum(same & (entries[None, :] < entries[:, None]), axis=1)
    slot_of = owner_list * slots + earlier.astype(jnp.int32)
    block_of = row_offset // n * cols + col_offset // n
    table = jnp.sum(
        jnp.where(block_of[None, :] == entries[:, None], slot_of[None, :], 0), axis=1
    ).astype(jnp.int32)
    owner = lax.axis_index(("dp", "shard"))
    count = jnp.sum((owner_list == owner).astype(jnp.int32)).reshape(1)

    (left_ready,) = early(0, count, left_root, left_factor)
    far_low, far_high, left_ready = lax.optimization_barrier((far_low, far_high, left_ready))
    far_low, far_high = merged(mine, jnp.stack([column(1), column(3)]), far_low, far_high)
    far_low, far_high = hop(far_low, 1), hop(far_high, -1)
    (right_ready,) = early(0, count, right_root, right_factor)
    arrived = (near_high, near_low, far_low, far_high)
    arrived, left_ready, right_ready = lax.optimization_barrier(
        (arrived, left_ready, right_ready)
    )
    ready = [(left_ready, right_ready)]

    all_slots = replicas * shards * slots
    outgoing = gather_pieces(
        table, me.reshape(1).astype(jnp.int32), mine, arrived, all_slots
    )
    incoming = lax.all_to_all(outgoing, ("dp", "shard"), split_axis=0, concat_axis=0, tiled=True)
    for t in range(1, slots):
        ready.append(early(t, count, left_root, left_factor, right_root, right_factor))
    incoming, ready = lax.optimization_barrier((incoming, ready))
    pieces = incoming.reshape(replicas, shards, slots, rows, width)
    outbound = update_pieces(gain, count, pieces, left_root, right_root, ready)
    returned = lax.all_to_all(
        outbound.reshape(all_slots, rows, width),
        ("dp", "shard"), split_axis=0, concat_axis=0, tiled=True,
    )
    new_left, new_right, new_xl, new_xr = new_state(
        gain, count, pieces, left_factor, right_factor, left_root, right_root, ready
    )
    update = place_pieces(table, returned, row_blocks, cols)
    return update, new_left, new_right, new_xl, new_xr


def solution(mesh):
    slots = P(("dp", "shard"), None, None)
    in_specs = (P("dp", None, "shard", None, None), P(), P(), P(), slots, slots, slots, slots)
    out_specs = (P(None, "shard", None, "dp"), slots, slots, slots, slots)
    return jax.shard_map(body, mesh=mesh, in_specs=in_specs, out_specs=out_specs, check_vma=False)
```

```python
import functools

import jax
import jax.numpy as jnp
from jax import lax
from jax.experimental import pallas as pl
from jax.experimental.pallas import tpu as pltpu
from jax.sharding import PartitionSpec as P

decay_rate = 0.9
f32 = jnp.float32
bf16 = jnp.bfloat16
MIB = 1 << 20


def params(mib):
    return pltpu.CompilerParams(vmem_limit_bytes=mib * MIB)


def halves(x):
    high = x.astype(bf16)
    return high, (x - high.astype(f32)).astype(bf16)


def mul(a, b):
    return jnp.dot(a, b, preferred_element_type=f32)


def mul_t(a, b):
    return lax.dot_general(a, b, (((1,), (1,)), ((), ())), preferred_element_type=f32)


def t_mul(a, b):
    return lax.dot_general(a, b, (((0,), (0,)), ((), ())), preferred_element_type=f32)


def mul3(a, b):
    return mul(a[0], b[0]) + (mul(a[0], b[1]) + mul(a[1], b[0]))


def vmem(x):
    return pltpu.with_memory_space_constraint(x, pltpu.VMEM)


def hbm(x):
    return pltpu.with_memory_space_constraint(x, pltpu.HBM)


def stored(*shape, dtype=f32):
    return pltpu.HBM(shape, dtype)


whole = pl.BlockSpec(memory_space=pltpu.VMEM)
scalars = pl.BlockSpec(memory_space=pltpu.SMEM)
in_place = pl.BlockSpec(memory_space=pl.ANY)


def window_kernel(at, mine, *outs):
    for k, out in enumerate(outs):
        half, width = out.shape[0], out.shape[-1]
        column = pl.ds(pl.multiple_of(at[2 * k + 1] * width, width), width)
        for b in range(half):
            out[b] = mine[at[2 * k] + b, :, :, column]


def windows(mine, width, pairs):
    row_blocks, rows, cols, _ = mine.shape
    at = jnp.stack([jnp.asarray(v, jnp.int32) for pair in pairs for v in pair])
    return pl.pallas_call(
        window_kernel,
        out_shape=(jax.ShapeDtypeStruct((row_blocks // 2, rows, cols, width), bf16),)
        * len(pairs),
        in_specs=[scalars, whole],
        out_specs=(whole,) * len(pairs),
        compiler_params=params(6),
        name="windows",
    )(at, vmem(mine))


def merge_kernel(at, mine, low_in, high_in, low_out, high_out):
    half, rows, cols, width = low_in.shape
    for k, (came, out) in enumerate(((low_in, low_out), (high_in, high_out))):
        column = pl.ds(pl.multiple_of(at[k] * width, width), width)
        for b in range(half):
            own = mine[k * half + b, :, :, column].astype(f32)
            out[b] = (own + came[b].astype(f32)).astype(bf16)


def merged(mine, at, low_in, high_in):
    return pl.pallas_call(
        merge_kernel,
        out_shape=(jax.ShapeDtypeStruct(low_in.shape, bf16),) * 2,
        in_specs=[scalars] + [whole] * 3,
        out_specs=(whole, whole),
        compiler_params=params(4),
        name="merge_far_part",
    )(at, vmem(mine), vmem(low_in), vmem(high_in))


def gather_kernel(table, me, mine, ups, downs, ups_more, downs_more, out, held):
    row_blocks, rows, cols, _ = mine.shape
    width = ups.shape[-1]
    half = row_blocks // 2
    column = pl.ds(pl.multiple_of(me[0] * width, width), width)
    out[...] = jnp.zeros_like(out)
    for b in range(row_blocks):
        near, far = (downs, ups_more) if b < half else (ups, downs_more)
        total = mine[b, :, :, column].astype(f32) + near[b % half].astype(f32)
        total = total + far[b % half].astype(f32)
        held[b] = total.reshape(rows * cols, width)
        for c in range(cols):
            piece = held[b, pl.ds(c, rows, stride=cols), :]
            out[table[b * cols + c]] = piece.astype(out.dtype)


def gather_pieces(table, me, mine, arrived, slots):
    half, rows, cols, width = arrived[0].shape
    return pl.pallas_call(
        gather_kernel,
        out_shape=jax.ShapeDtypeStruct((slots, rows, width), bf16),
        in_specs=[scalars, scalars] + [whole] * 5,
        out_specs=whole,
        scratch_shapes=[pltpu.VMEM((2 * half, rows * cols, width), f32)],
        compiler_params=params(6),
        name="sum_and_gather",
    )(table, me, vmem(mine), *[vmem(a) for a in arrived])


def place_kernel(per_step, rows, cols, table, arrived, out, held):
    step = pl.program_id(0)
    for b in range(per_step):
        for c in range(cols):
            slot = table[(step * per_step + b) * cols + c]
            held[b, pl.ds(c, rows, stride=cols), :] = arrived[slot].astype(f32)
        out[b] = held[b].reshape(rows, cols, held.shape[-1]).astype(out.dtype)


def place_pieces(table, arrived, row_blocks, cols):
    slots, rows, width = arrived.shape
    per_step = 4
    return pl.pallas_call(
        functools.partial(place_kernel, per_step, rows, cols),
        out_shape=jax.ShapeDtypeStruct((row_blocks, rows, cols, width), bf16),
        grid=(row_blocks // per_step,),
        in_specs=[scalars, whole],
        out_specs=pl.BlockSpec((per_step, rows, cols, width), lambda i: (i, 0, 0, 0)),
        scratch_shapes=[pltpu.VMEM((per_step, rows * cols, width), f32)],
        compiler_params=params(4),
        name="place_pieces",
    )(table, vmem(arrived))


def early_kernel(slots, count, *refs):
    items = len(slots)
    ins, outs = refs[: 2 * items], refs[2 * items : 6 * items]
    roots, factors, highs, lows, products, in_sem, out_sem = refs[6 * items :]
    n = roots.shape[1]

    def arrivals(k):
        return [
            pltpu.make_async_copy(
                ins[2 * k + i].at[slots[k]], held.at[k], in_sem.at[k, i]
            )
            for i, held in enumerate((roots, factors))
        ]

    def departures(k):
        return [
            pltpu.make_async_copy(held.at[k], outs[4 * k + i], out_sem.at[k, i])
            for i, held in enumerate((highs, lows, products))
        ]

    for k in range(items):

        @pl.when(slots[k] < count[0])
        def _():
            for copy in arrivals(k):
                copy.start()

    for k in range(items):

        @pl.when(slots[k] < count[0])
        def _():
            coming, going = arrivals(k), departures(k)
            coming[0].wait()
            x = halves(roots[k])
            square = halves(mul3(x, x))
            fourth = halves(mul3(square, square))
            fifth = halves(mul3(x, fourth))
            highs[k], lows[k] = fifth
            going[0].start()
            going[1].start()
            coming[1].wait()
            total = jnp.zeros((128, 128), f32)
            on = lax.broadcasted_iota(jnp.int32, (128, 128), 0)
            on = on == lax.broadcasted_iota(jnp.int32, (128, 128), 1)
            for d in range(0, n, 128):
                total += factors[k, d : d + 128, d : d + 128]
            outs[4 * k + 3][0] = jnp.sum(jnp.where(on, total, 0.0))
            products[k] = decay_rate * mul3(fifth, halves(factors[k]))
            going[2].start()

        @pl.when(slots[k] >= count[0])
        def _():
            outs[4 * k + 3][0] = jnp.float32(0.0)

    for k in range(items):

        @pl.when(slots[k] < count[0])
        def _():
            for copy in departures(k):
                copy.wait()


def early(count, *items):
    n = items[0][1].shape[1]
    many = len(items)
    made = pl.pallas_call(
        functools.partial(early_kernel, [t for t, _, _ in items]),
        out_shape=(
            stored(n, n, dtype=bf16),
            stored(n, n, dtype=bf16),
            stored(n, n),
            jax.ShapeDtypeStruct((1,), f32),
        )
        * many,
        in_specs=[scalars] + [in_place] * (2 * many),
        out_specs=(in_place, in_place, in_place, scalars) * many,
        scratch_shapes=[
            pltpu.VMEM((many, n, n), f32),
            pltpu.VMEM((many, n, n), f32),
            pltpu.VMEM((many, n, n), bf16),
            pltpu.VMEM((many, n, n), bf16),
            pltpu.VMEM((many, n, n), f32),
            pltpu.SemaphoreType.DMA((many, 2)),
            pltpu.SemaphoreType.DMA((many, 3)),
        ],
        compiler_params=params(28),
        cost_estimate=pl.CostEstimate(
            flops=many * 12 * 2 * n**3,
            bytes_accessed=many * 16 * n * n,
            transcendentals=0,
        ),
        name="early_products",
    )(count, *[hbm(x) for _, *pair in items for x in pair])
    return [made[4 * k : 4 * k + 4] for k in range(many)]


def assembled(pieces, t, block):
    parts, shards, _, rows, width = pieces.shape
    for z in range(parts):
        block[:, z * width : (z + 1) * width] = pieces[z, :, t].reshape(
            shards * rows, width
        )
    return block[...]


def scale_of(trace, square, gain, n):
    return n / (decay_rate * trace + gain * square)


def update_kernel(gain, slots, count, pieces, xl, xr, *refs):
    ready, refs = refs[: 6 * slots], refs[6 * slots :]
    out, block, fives, singles, in_sem = refs
    parts, shards, _, rows, width = out.shape
    n = xl.shape[1]

    def arrivals(t):
        fl, pl_, _, fr, pr, _ = ready[6 * t : 6 * t + 6]
        sources = (
            (fl, fives.at[t, 0]),
            (xl.at[t], singles.at[t, 0]),
            (pl_, singles.at[t, 1]),
            (fr, fives.at[t, 1]),
            (xr.at[t], singles.at[t, 2]),
            (pr, singles.at[t, 3]),
        )
        return [
            pltpu.make_async_copy(a, b, in_sem.at[t, k]) for k, (a, b) in enumerate(sources)
        ]

    for t in range(slots):

        @pl.when(t < count[0])
        def _():
            for copy in arrivals(t):
                copy.start()

    for t in range(slots):

        @pl.when(t < count[0])
        def _():
            copies = arrivals(t)
            g = assembled(pieces, t, block)
            wide = g.astype(f32)
            square = jnp.sum(wide * wide)
            left_scale = scale_of(ready[6 * t + 2][0], square, gain, n)
            right_scale = scale_of(ready[6 * t + 5][0], square, gain, n)
            copies[0].wait()
            m = mul_t(mul(fives[t, 0], g).astype(bf16), g)
            copies[1].wait()
            copies[2].wait()
            left = 1.25 * singles[t, 0] - (0.25 * left_scale) * (singles[t, 1] + gain * m)
            part = mul(left.astype(bf16), g).astype(bf16)
            copies[3].wait()
            m = mul(mul_t(fives[t, 1], g).astype(bf16), g)
            copies[4].wait()
            copies[5].wait()
            right = 1.25 * singles[t, 2] - (0.25 * right_scale) * (singles[t, 3] + gain * m)
            done = mul(part, right.astype(bf16)).astype(bf16)
            for z in range(parts):
                out[z, :, t] = done[:, z * width : (z + 1) * width].reshape(
                    shards, rows, width
                )

        @pl.when(t >= count[0])
        def _():
            out[:, :, t] = jnp.zeros_like(out[:, :, t])


def update_pieces(gain, count, pieces, xl, xr, ready):
    slots = pieces.shape[2]
    n = xl.shape[1]
    inputs, specs = [], []
    for left, right in ready:
        for high, _, product, trace in (left, right):
            inputs += [hbm(high), hbm(product), trace]
            specs += [in_place, in_place, scalars]
    return pl.pallas_call(
        functools.partial(update_kernel, gain, slots),
        out_shape=jax.ShapeDtypeStruct(pieces.shape, bf16),
        in_specs=[scalars, whole, in_place, in_place] + specs,
        out_specs=whole,
        scratch_shapes=[
            pltpu.VMEM((n, n), bf16),
            pltpu.VMEM((slots, 2, n, n), bf16),
            pltpu.VMEM((slots, 4, n, n), f32),
            pltpu.SemaphoreType.DMA((slots, 6)),
        ],
        compiler_params=params(28),
        name="update_pieces",
    )(count, vmem(pieces), hbm(xl), hbm(xr), *inputs)


def state_kernel(gain, slots, count, pieces, left, right, xl, xr, *refs):
    ready, refs = refs[: 8 * slots], refs[8 * slots :]
    outs, refs = refs[:4], refs[4:]
    block, fives, singles, made, in_sem, out_sem = refs
    n = xl.shape[1]
    olds = (left, right, xl, xr)

    def arrivals(t):
        flh, fll, pl_, _, frh, frl, pr, _ = ready[8 * t : 8 * t + 8]
        sources = [(a, fives.at[t, k]) for k, a in enumerate((flh, fll, frh, frl))]
        sources += [(a.at[t], singles.at[t, k]) for k, a in enumerate(olds)]
        sources += [(a, singles.at[t, 4 + k]) for k, a in enumerate((pl_, pr))]
        return [
            pltpu.make_async_copy(a, b, in_sem.at[t, k]) for k, (a, b) in enumerate(sources)
        ]

    def departures(t):
        return [
            pltpu.make_async_copy(made.at[t, k], out.at[t], out_sem.at[t, k])
            for k, out in enumerate(outs)
        ]

    def carried(t):
        return [
            pltpu.make_async_copy(old.at[t], made.at[t, k], in_sem.at[t, k])
            for k, old in enumerate(olds)
        ]

    for t in range(slots):

        @pl.when(t < count[0])
        def _():
            for copy in arrivals(t):
                copy.start()

        @pl.when(t >= count[0])
        def _():
            for copy in carried(t):
                copy.start()

    for t in range(slots):

        @pl.when(t < count[0])
        def _():
            copies, leaving = arrivals(t), departures(t)
            g = assembled(pieces, t, block)
            wide = g.astype(f32)
            square = jnp.sum(wide * wide)
            left_scale = scale_of(ready[8 * t + 3][0], square, gain, n)
            right_scale = scale_of(ready[8 * t + 7][0], square, gain, n)
            for copy in copies:
                copy.wait()
            made[t, 0] = decay_rate * singles[t, 0] + gain * mul_t(g, g)
            leaving[0].start()
            made[t, 1] = decay_rate * singles[t, 1] + gain * t_mul(g, g)
            leaving[1].start()
            high, low = halves(mul(fives[t, 0], g) + mul(fives[t, 1], g))
            m = mul_t(high, g) + mul_t(low, g)
            made[t, 2] = 1.25 * singles[t, 2] - (0.25 * left_scale) * (singles[t, 4] + gain * m)
            leaving[2].start()
            high, low = halves(mul_t(fives[t, 2], g) + mul_t(fives[t, 3], g))
            m = mul(high, g) + mul(low, g)
            made[t, 3] = 1.25 * singles[t, 3] - (0.25 * right_scale) * (singles[t, 5] + gain * m)
            leaving[3].start()

        @pl.when(t >= count[0])
        def _():
            for came, leaves in zip(carried(t), departures(t)):
                came.wait()
                leaves.start()

    for t in range(slots):
        for copy in departures(t):
            copy.wait()


def new_state(gain, count, pieces, left, right, xl, xr, ready):
    slots, n, _ = left.shape
    inputs, specs = [], []
    for sides in ready:
        for high, low, product, trace in sides:
            inputs += [hbm(high), hbm(low), hbm(product), trace]
            specs += [in_place, in_place, in_place, scalars]
    return pl.pallas_call(
        functools.partial(state_kernel, gain, slots),
        out_shape=(stored(slots, n, n),) * 4,
        in_specs=[scalars, whole] + [in_place] * 4 + specs,
        out_specs=(in_place,) * 4,
        scratch_shapes=[
            pltpu.VMEM((n, n), bf16),
            pltpu.VMEM((slots, 4, n, n), bf16),
            pltpu.VMEM((slots, 6, n, n), f32),
            pltpu.VMEM((slots, 4, n, n), f32),
            pltpu.SemaphoreType.DMA((slots, 10)),
            pltpu.SemaphoreType.DMA((slots, 4)),
        ],
        compiler_params=params(40),
        cost_estimate=pl.CostEstimate(
            flops=slots * 10 * 2 * n**3,
            bytes_accessed=slots * 48 * n * n,
            transcendentals=0,
        ),
        name="new_state",
    )(count, vmem(pieces), *[hbm(x) for x in (left, right, xl, xr)], *inputs)


def body(
    gradients, owner_list, row_offset, col_offset, left_factor, right_factor, left_root, right_root
):
    replicas = lax.axis_size("dp")
    shards = lax.axis_size("shard")
    slots, n, _ = left_factor.shape
    _, row_blocks, rows, cols, _ = gradients.shape
    width = n // replicas
    gain = (1.0 - decay_rate) / n
    me = lax.axis_index("dp")
    mine = gradients[0]

    def hop(x, step):
        return lax.ppermute(x, "dp", [(i, (i + step) % replicas) for i in range(replicas)])

    def column(step):
        return lax.rem(me + step, replicas).astype(jnp.int32)

    half = row_blocks // 2
    far_low, far_high, near_high, near_low = windows(
        mine,
        width,
        ((0, column(2)), (half, column(2)), (half, column(1)), (0, column(3))),
    )
    far_low, far_high = hop(far_low, 1), hop(far_high, -1)
    near_high, near_low = hop(near_high, 1), hop(near_low, -1)

    entries = jnp.arange(owner_list.shape[0], dtype=jnp.int32)
    same = owner_list[None, :] == owner_list[:, None]
    earlier = jnp.sum(same & (entries[None, :] < entries[:, None]), axis=1)
    slot_of = owner_list * slots + earlier.astype(jnp.int32)
    block_of = row_offset // n * cols + col_offset // n
    table = jnp.sum(
        jnp.where(block_of[None, :] == entries[:, None], slot_of[None, :], 0), axis=1
    ).astype(jnp.int32)
    owner = lax.axis_index(("dp", "shard"))
    count = jnp.sum((owner_list == owner).astype(jnp.int32)).reshape(1)

    far_low, far_high = merged(mine, jnp.stack([column(1), column(3)]), far_low, far_high)
    far_low, far_high = hop(far_low, 1), hop(far_high, -1)
    (first,) = early(count, (0, left_root, left_factor))
    arrived = (near_high, near_low, far_low, far_high)
    arrived, first = lax.optimization_barrier((arrived, first))

    all_slots = replicas * shards * slots
    outgoing = gather_pieces(
        table, me.reshape(1).astype(jnp.int32), mine, arrived, all_slots
    )
    incoming = lax.all_to_all(outgoing, ("dp", "shard"), split_axis=0, concat_axis=0, tiled=True)
    sides = ((left_root, left_factor), (right_root, right_factor))
    rest = [(t, *side) for t in range(slots) for side in sides][1:]
    ready = [first, *early(count, *rest)]
    incoming, ready = lax.optimization_barrier((incoming, ready))
    ready = [ready[2 * t : 2 * t + 2] for t in range(slots)]
    pieces = incoming.reshape(replicas, shards, slots, rows, width)
    outbound = update_pieces(gain, count, pieces, left_root, right_root, ready)
    returned = lax.all_to_all(
        outbound.reshape(all_slots, rows, width),
        ("dp", "shard"), split_axis=0, concat_axis=0, tiled=True,
    )
    new_left, new_right, new_xl, new_xr = new_state(
        gain, count, pieces, left_factor, right_factor, left_root, right_root, ready
    )
    update = place_pieces(table, returned, row_blocks, cols)
    return update, new_left, new_right, new_xl, new_xr


def solution(mesh):
    slots = P(("dp", "shard"), None, None)
    in_specs = (P("dp", None, "shard", None, None), P(), P(), P(), slots, slots, slots, slots)
    out_specs = (P(None, "shard", None, "dp"), slots, slots, slots, slots)
    return jax.shard_map(body, mesh=mesh, in_specs=in_specs, out_specs=out_specs, check_vma=False)
```

```python
import functools

import jax
import jax.numpy as jnp
from jax import lax
from jax.experimental import pallas as pl
from jax.experimental.pallas import tpu as pltpu
from jax.sharding import PartitionSpec as P

decay_rate = 0.9
f32 = jnp.float32
bf16 = jnp.bfloat16
MIB = 1 << 20


def params(mib):
    return pltpu.CompilerParams(vmem_limit_bytes=mib * MIB)


def halves(x):
    high = x.astype(bf16)
    return high, (x - high.astype(f32)).astype(bf16)


def mul(a, b):
    return jnp.dot(a, b, preferred_element_type=f32)


def mul_t(a, b):
    return lax.dot_general(a, b, (((1,), (1,)), ((), ())), preferred_element_type=f32)


def t_mul(a, b):
    return lax.dot_general(a, b, (((0,), (0,)), ((), ())), preferred_element_type=f32)


def mul3(a, b):
    return mul(a[0], b[0]) + (mul(a[0], b[1]) + mul(a[1], b[0]))


def vmem(x):
    return pltpu.with_memory_space_constraint(x, pltpu.VMEM)


def hbm(x):
    return pltpu.with_memory_space_constraint(x, pltpu.HBM)


def stored(*shape, dtype=f32):
    return pltpu.HBM(shape, dtype)


whole = pl.BlockSpec(memory_space=pltpu.VMEM)
scalars = pl.BlockSpec(memory_space=pltpu.SMEM)
in_place = pl.BlockSpec(memory_space=pl.ANY)


def column_at(hop, width):
    replicas = lax.axis_size("dp")
    z = lax.rem(lax.axis_index("dp").astype(jnp.int32) + hop, replicas)
    return pl.ds(pl.multiple_of(z * width, width), width)


def window_kernel(parts, mine, *refs):
    outs, sem = refs[:-1], refs[-1]
    copies = []
    for k, ((low, hop), out) in enumerate(zip(parts, outs)):
        half, width = out.shape[0], out.shape[-1]
        source = mine.at[low : low + half, :, :, column_at(hop, width)]
        copies.append(pltpu.make_async_copy(source, out, sem.at[k]))
    for copy in copies:
        copy.start()
    for copy in copies:
        copy.wait()


def windows(mine, width, parts):
    row_blocks, rows, cols, _ = mine.shape
    return pl.pallas_call(
        functools.partial(window_kernel, parts),
        out_shape=(pltpu.VMEM((row_blocks // 2, rows, cols, width), bf16),) * len(parts),
        in_specs=[in_place],
        out_specs=(whole,) * len(parts),
        scratch_shapes=[pltpu.SemaphoreType.DMA((len(parts),))],
        compiler_params=params(4),
        name="windows",
    )(hbm(mine))


def merge_kernel(hops, mine, low_in, high_in, low_out, high_out):
    half, width = low_in.shape[0], low_in.shape[-1]
    for k, (came, out) in enumerate(((low_in, low_out), (high_in, high_out))):
        column = column_at(hops[k], width)
        for b in range(half):
            own = mine[k * half + b, :, :, column].astype(f32)
            out[b] = (own + came[b].astype(f32)).astype(bf16)


def merged(mine, hops, low_in, high_in):
    return pl.pallas_call(
        functools.partial(merge_kernel, hops),
        out_shape=(pltpu.VMEM(low_in.shape, bf16),) * 2,
        in_specs=[whole] * 3,
        out_specs=(whole, whole),
        compiler_params=params(4),
        name="merge_far_part",
    )(vmem(mine), vmem(low_in), vmem(high_in))


def gather_kernel(table, mine, ups, downs, ups_more, downs_more, out, held):
    row_blocks, rows, cols, _ = mine.shape
    width = ups.shape[-1]
    half = row_blocks // 2
    column = column_at(0, width)
    out[...] = jnp.zeros_like(out)
    for b in range(row_blocks):
        near, far = (downs, ups_more) if b < half else (ups, downs_more)
        total = mine[b, :, :, column].astype(f32) + near[b % half].astype(f32)
        total = total + far[b % half].astype(f32)
        held[b] = total.reshape(rows * cols, width)
        for c in range(cols):
            piece = held[b, pl.ds(c, rows, stride=cols), :]
            out[table[b * cols + c]] = piece.astype(out.dtype)


def gather_pieces(table, mine, arrived, slots):
    half, rows, cols, width = arrived[0].shape
    return pl.pallas_call(
        gather_kernel,
        out_shape=jax.ShapeDtypeStruct((slots, rows, width), bf16),
        in_specs=[scalars] + [whole] * 5,
        out_specs=whole,
        scratch_shapes=[pltpu.VMEM((2 * half, rows * cols, width), f32)],
        compiler_params=params(6),
        name="sum_and_gather",
    )(table, vmem(mine), *[vmem(a) for a in arrived])


def place_kernel(per_step, rows, cols, table, arrived, out, held):
    step = pl.program_id(0)
    for b in range(per_step):
        for c in range(cols):
            slot = table[(step * per_step + b) * cols + c]
            held[b, pl.ds(c, rows, stride=cols), :] = arrived[slot].astype(f32)
        out[b] = held[b].reshape(rows, cols, held.shape[-1]).astype(out.dtype)


def place_pieces(table, arrived, row_blocks, cols):
    slots, rows, width = arrived.shape
    per_step = 4
    return pl.pallas_call(
        functools.partial(place_kernel, per_step, rows, cols),
        out_shape=jax.ShapeDtypeStruct((row_blocks, rows, cols, width), bf16),
        grid=(row_blocks // per_step,),
        in_specs=[scalars, whole],
        out_specs=pl.BlockSpec((per_step, rows, cols, width), lambda i: (i, 0, 0, 0)),
        scratch_shapes=[pltpu.VMEM((per_step, rows * cols, width), f32)],
        compiler_params=params(4),
        name="place_pieces",
    )(table, vmem(arrived))


def early_kernel(slots, count, *refs):
    items = len(slots)
    ins, outs = refs[: 2 * items], refs[2 * items : 6 * items]
    roots, factors, highs, lows, products, traces, in_sem, out_sem = refs[6 * items :]
    n = roots.shape[1]

    def arrivals(k):
        return [
            pltpu.make_async_copy(
                ins[2 * k + i].at[slots[k]], held.at[k], in_sem.at[k, i]
            )
            for i, held in enumerate((roots, factors))
        ]

    def departures(k):
        return [
            pltpu.make_async_copy(held.at[k], outs[4 * k + i], out_sem.at[k, i])
            for i, held in enumerate((highs, lows, products, traces))
        ]

    for k in range(items):

        @pl.when(slots[k] < count[0])
        def _():
            for copy in arrivals(k):
                copy.start()

    for k in range(items):

        @pl.when(slots[k] < count[0])
        def _():
            coming, going = arrivals(k), departures(k)
            coming[0].wait()
            x = halves(roots[k])
            square = halves(mul3(x, x))
            fourth = halves(mul3(square, square))
            fifth = halves(mul3(x, fourth))
            highs[k], lows[k] = fifth
            going[0].start()
            going[1].start()
            coming[1].wait()
            total = jnp.zeros((128, 128), f32)
            on = lax.broadcasted_iota(jnp.int32, (128, 128), 0)
            on = on == lax.broadcasted_iota(jnp.int32, (128, 128), 1)
            for d in range(0, n, 128):
                total += factors[k, d : d + 128, d : d + 128]
            traces[k] = jnp.full(traces.shape[1:], jnp.sum(jnp.where(on, total, 0.0)))
            products[k] = decay_rate * mul3(fifth, halves(factors[k]))
            going[2].start()
            going[3].start()

    for k in range(items):

        @pl.when(slots[k] < count[0])
        def _():
            for copy in departures(k):
                copy.wait()


def early(count, *items):
    n = items[0][1].shape[1]
    many = len(items)
    made = pl.pallas_call(
        functools.partial(early_kernel, [t for t, _, _ in items]),
        out_shape=(
            stored(n, n, dtype=bf16),
            stored(n, n, dtype=bf16),
            stored(n, n),
            stored(8, 128),
        )
        * many,
        in_specs=[scalars] + [in_place] * (2 * many),
        out_specs=(in_place,) * (4 * many),
        scratch_shapes=[
            pltpu.VMEM((many, n, n), f32),
            pltpu.VMEM((many, n, n), f32),
            pltpu.VMEM((many, n, n), bf16),
            pltpu.VMEM((many, n, n), bf16),
            pltpu.VMEM((many, n, n), f32),
            pltpu.VMEM((many, 8, 128), f32),
            pltpu.SemaphoreType.DMA((many, 2)),
            pltpu.SemaphoreType.DMA((many, 4)),
        ],
        compiler_params=params(28),
        cost_estimate=pl.CostEstimate(
            flops=many * 12 * 2 * n**3,
            bytes_accessed=many * 16 * n * n,
            transcendentals=0,
        ),
        name="early_products",
    )(count, *[hbm(x) for _, *pair in items for x in pair])
    return [made[4 * k : 4 * k + 4] for k in range(many)]


def assembled(pieces, t, block):
    parts, shards, _, rows, width = pieces.shape
    for z in range(parts):
        block[:, z * width : (z + 1) * width] = pieces[z, :, t].reshape(
            shards * rows, width
        )
    return block[...]


def quarter_scale(trace, block, gain):
    wide = block.astype(f32)
    square = jnp.sum(wide * wide)
    total = decay_rate * trace[0:1, 0:1] + gain * square
    return (0.25 * block.shape[0]) / total


def update_kernel(gain, slots, count, pieces, xl, xr, *refs):
    ready, refs = refs[: 6 * slots], refs[6 * slots :]
    out, blocks, fives, singles, traces, in_sem = refs
    parts, shards, _, rows, width = out.shape

    def arrivals(t):
        fl, pl_, tl, fr, pr, tr = ready[6 * t : 6 * t + 6]
        sources = (
            (fl, fives.at[t, 0]),
            (tl, traces.at[t, 0]),
            (xl.at[t], singles.at[t, 0]),
            (pl_, singles.at[t, 1]),
            (fr, fives.at[t, 1]),
            (tr, traces.at[t, 1]),
            (xr.at[t], singles.at[t, 2]),
            (pr, singles.at[t, 3]),
        )
        return [
            pltpu.make_async_copy(a, b, in_sem.at[t, k]) for k, (a, b) in enumerate(sources)
        ]

    def work(ts):
        copies = {t: arrivals(t) for t in ts}
        for t in ts:
            for copy in copies[t]:
                copy.start()
        g, side, part = {}, {}, {}
        for t in ts:
            g[t] = assembled(pieces, t, blocks.at[t])
        for t in ts:
            copies[t][0].wait()
        for t in ts:
            side[t] = mul_t(mul(fives[t, 0], g[t]).astype(bf16), g[t])
        for t in ts:
            for copy in copies[t][1:4]:
                copy.wait()
        for t in ts:
            scale = quarter_scale(traces[t, 0], g[t], gain)
            side[t] = 1.25 * singles[t, 0] - scale * (singles[t, 1] + gain * side[t])
            part[t] = mul(side[t].astype(bf16), g[t]).astype(bf16)
        for t in ts:
            copies[t][4].wait()
        for t in ts:
            side[t] = mul(mul_t(fives[t, 1], g[t]).astype(bf16), g[t])
        for t in ts:
            for copy in copies[t][5:]:
                copy.wait()
        for t in ts:
            scale = quarter_scale(traces[t, 1], g[t], gain)
            side[t] = 1.25 * singles[t, 2] - scale * (singles[t, 3] + gain * side[t])
            done = mul(part[t], side[t].astype(bf16)).astype(bf16)
            for z in range(parts):
                out[z, :, t] = done[:, z * width : (z + 1) * width].reshape(
                    shards, rows, width
                )

    for live in range(slots + 1):

        @pl.when(count[0] == live)
        def _():
            work(range(live))
            for t in range(live, slots):
                out[:, :, t] = jnp.zeros_like(out[:, :, t])


def update_pieces(gain, count, pieces, xl, xr, ready):
    slots = pieces.shape[2]
    n = xl.shape[1]
    inputs = []
    for sides in ready:
        for high, _, product, trace in sides:
            inputs += [hbm(high), hbm(product), hbm(trace)]
    return pl.pallas_call(
        functools.partial(update_kernel, gain, slots),
        out_shape=jax.ShapeDtypeStruct(pieces.shape, bf16),
        in_specs=[scalars, whole] + [in_place] * (2 + len(inputs)),
        out_specs=whole,
        scratch_shapes=[
            pltpu.VMEM((slots, n, n), bf16),
            pltpu.VMEM((slots, 2, n, n), bf16),
            pltpu.VMEM((slots, 4, n, n), f32),
            pltpu.VMEM((slots, 2, 8, 128), f32),
            pltpu.SemaphoreType.DMA((slots, 8)),
        ],
        compiler_params=params(32),
        name="update_pieces",
    )(count, vmem(pieces), hbm(xl), hbm(xr), *inputs)


def state_kernel(gain, slots, count, pieces, left, right, xl, xr, *refs):
    ready, refs = refs[: 8 * slots], refs[8 * slots :]
    outs, refs = refs[:4], refs[4:]
    block, fives, singles, traces, made, in_sem, out_sem = refs
    n = xl.shape[1]
    olds = (left, right, xl, xr)

    def arrivals(t):
        flh, fll, pl_, tl, frh, frl, pr, tr = ready[8 * t : 8 * t + 8]
        sources = [(a, fives.at[t, k]) for k, a in enumerate((flh, fll, frh, frl))]
        sources += [(a.at[t], singles.at[t, k]) for k, a in enumerate(olds)]
        sources += [(a, singles.at[t, 4 + k]) for k, a in enumerate((pl_, pr))]
        sources += [(a, traces.at[t, k]) for k, a in enumerate((tl, tr))]
        return [
            pltpu.make_async_copy(a, b, in_sem.at[t, k]) for k, (a, b) in enumerate(sources)
        ]

    def departures(t):
        return [
            pltpu.make_async_copy(made.at[t, k], out.at[t], out_sem.at[t, k])
            for k, out in enumerate(outs)
        ]

    def carried(t):
        return [
            pltpu.make_async_copy(old.at[t], made.at[t, k], in_sem.at[t, k])
            for k, old in enumerate(olds)
        ]

    for t in range(slots):

        @pl.when(t < count[0])
        def _():
            for copy in arrivals(t):
                copy.start()

        @pl.when(t >= count[0])
        def _():
            for copy in carried(t):
                copy.start()

    for t in range(slots):

        @pl.when(t < count[0])
        def _():
            copies, leaving = arrivals(t), departures(t)
            g = assembled(pieces, t, block)
            for copy in copies:
                copy.wait()
            left_scale = quarter_scale(traces[t, 0], g, gain)
            right_scale = quarter_scale(traces[t, 1], g, gain)
            made[t, 0] = decay_rate * singles[t, 0] + gain * mul_t(g, g)
            leaving[0].start()
            made[t, 1] = decay_rate * singles[t, 1] + gain * t_mul(g, g)
            leaving[1].start()
            high, low = halves(mul(fives[t, 0], g) + mul(fives[t, 1], g))
            m = mul_t(high, g) + mul_t(low, g)
            made[t, 2] = 1.25 * singles[t, 2] - left_scale * (singles[t, 4] + gain * m)
            leaving[2].start()
            high, low = halves(mul_t(fives[t, 2], g) + mul_t(fives[t, 3], g))
            m = mul(high, g) + mul(low, g)
            made[t, 3] = 1.25 * singles[t, 3] - right_scale * (singles[t, 5] + gain * m)
            leaving[3].start()

        @pl.when(t >= count[0])
        def _():
            for came, leaves in zip(carried(t), departures(t)):
                came.wait()
                leaves.start()

    for t in range(slots):
        for copy in departures(t):
            copy.wait()


def new_state(gain, count, pieces, left, right, xl, xr, ready):
    slots, n, _ = left.shape
    inputs = [hbm(x) for sides in ready for made in sides for x in made]
    return pl.pallas_call(
        functools.partial(state_kernel, gain, slots),
        out_shape=(stored(slots, n, n),) * 4,
        in_specs=[scalars, whole] + [in_place] * (4 + len(inputs)),
        out_specs=(in_place,) * 4,
        scratch_shapes=[
            pltpu.VMEM((n, n), bf16),
            pltpu.VMEM((slots, 4, n, n), bf16),
            pltpu.VMEM((slots, 6, n, n), f32),
            pltpu.VMEM((slots, 2, 8, 128), f32),
            pltpu.VMEM((slots, 4, n, n), f32),
            pltpu.SemaphoreType.DMA((slots, 12)),
            pltpu.SemaphoreType.DMA((slots, 4)),
        ],
        compiler_params=params(40),
        cost_estimate=pl.CostEstimate(
            flops=slots * 10 * 2 * n**3,
            bytes_accessed=slots * 48 * n * n,
            transcendentals=0,
        ),
        name="new_state",
    )(count, vmem(pieces), *[hbm(x) for x in (left, right, xl, xr)], *inputs)


def body(
    gradients, owner_list, row_offset, col_offset, left_factor, right_factor, left_root, right_root
):
    replicas = lax.axis_size("dp")
    shards = lax.axis_size("shard")
    slots, n, _ = left_factor.shape
    _, row_blocks, rows, cols, _ = gradients.shape
    width = n // replicas
    gain = (1.0 - decay_rate) / n
    mine = gradients[0]

    def hop(x, step):
        return lax.ppermute(x, "dp", [(i, (i + step) % replicas) for i in range(replicas)])

    half = row_blocks // 2
    far_low, far_high, near_high, near_low = windows(
        mine, width, ((0, 2), (half, 2), (half, 1), (0, 3))
    )
    far_low, far_high = hop(far_low, 1), hop(far_high, -1)
    near_high, near_low = hop(near_high, 1), hop(near_low, -1)

    entries = jnp.arange(owner_list.shape[0], dtype=jnp.int32)
    same = owner_list[None, :] == owner_list[:, None]
    earlier = jnp.sum(same & (entries[None, :] < entries[:, None]), axis=1)
    slot_of = owner_list * slots + earlier.astype(jnp.int32)
    block_of = row_offset // n * cols + col_offset // n
    table = jnp.sum(
        jnp.where(block_of[None, :] == entries[:, None], slot_of[None, :], 0), axis=1
    ).astype(jnp.int32)
    owner = lax.axis_index(("dp", "shard"))
    count = jnp.sum((owner_list == owner).astype(jnp.int32)).reshape(1)

    far_low, far_high = merged(mine, (1, 3), far_low, far_high)
    far_low, far_high = hop(far_low, 1), hop(far_high, -1)
    (first,) = early(count, (0, left_root, left_factor))
    arrived = (near_high, near_low, far_low, far_high)
    arrived, first = lax.optimization_barrier((arrived, first))

    all_slots = replicas * shards * slots
    outgoing = gather_pieces(table, mine, arrived, all_slots)
    incoming = lax.all_to_all(outgoing, ("dp", "shard"), split_axis=0, concat_axis=0, tiled=True)
    sides = ((left_root, left_factor), (right_root, right_factor))
    rest = [(t, *side) for t in range(slots) for side in sides][1:]
    ready = [first, *early(count, *rest)]
    incoming, ready = lax.optimization_barrier((incoming, ready))
    ready = [ready[2 * t : 2 * t + 2] for t in range(slots)]
    pieces = incoming.reshape(replicas, shards, slots, rows, width)
    outbound = update_pieces(gain, count, pieces, left_root, right_root, ready)
    returned = lax.all_to_all(
        outbound.reshape(all_slots, rows, width),
        ("dp", "shard"), split_axis=0, concat_axis=0, tiled=True,
    )
    new_left, new_right, new_xl, new_xr = new_state(
        gain, count, pieces, left_factor, right_factor, left_root, right_root, ready
    )
    update = place_pieces(table, returned, row_blocks, cols)
    return update, new_left, new_right, new_xl, new_xr


def solution(mesh):
    slots = P(("dp", "shard"), None, None)
    in_specs = (P("dp", None, "shard", None, None), P(), P(), P(), slots, slots, slots, slots)
    out_specs = (P(None, "shard", None, "dp"), slots, slots, slots, slots)
    return jax.shard_map(body, mesh=mesh, in_specs=in_specs, out_specs=out_specs, check_vma=False)
```

```python
import functools

import jax
import jax.numpy as jnp
from jax import lax
from jax.experimental import pallas as pl
from jax.experimental.pallas import tpu as pltpu
from jax.sharding import PartitionSpec as P

decay_rate = 0.9
f32 = jnp.float32
bf16 = jnp.bfloat16
MIB = 1 << 20


def params(mib):
    return pltpu.CompilerParams(vmem_limit_bytes=mib * MIB)


def halves(x):
    high = x.astype(bf16)
    return high, (x - high.astype(f32)).astype(bf16)


def mul(a, b):
    return jnp.dot(a, b, preferred_element_type=f32)


def mul_t(a, b):
    return lax.dot_general(a, b, (((1,), (1,)), ((), ())), preferred_element_type=f32)


def t_mul(a, b):
    return lax.dot_general(a, b, (((0,), (0,)), ((), ())), preferred_element_type=f32)


def mul3(a, b):
    return mul(a[0], b[0]) + (mul(a[0], b[1]) + mul(a[1], b[0]))


def vmem(x):
    return pltpu.with_memory_space_constraint(x, pltpu.VMEM)


def hbm(x):
    return pltpu.with_memory_space_constraint(x, pltpu.HBM)


def stored(*shape, dtype=f32):
    return pltpu.HBM(shape, dtype)


whole = pl.BlockSpec(memory_space=pltpu.VMEM)
scalars = pl.BlockSpec(memory_space=pltpu.SMEM)
in_place = pl.BlockSpec(memory_space=pl.ANY)


def column_at(hop, width):
    replicas = lax.axis_size("dp")
    z = lax.rem(lax.axis_index("dp").astype(jnp.int32) + hop, replicas)
    return pl.ds(pl.multiple_of(z * width, width), width)


def window_kernel(parts, mine, *refs):
    outs, sem = refs[:-1], refs[-1]
    copies = []
    for k, ((low, hop), out) in enumerate(zip(parts, outs)):
        half, width = out.shape[0], out.shape[-1]
        source = mine.at[low : low + half, :, :, column_at(hop, width)]
        copies.append(pltpu.make_async_copy(source, out, sem.at[k]))
    for copy in copies:
        copy.start()
    for copy in copies:
        copy.wait()


def windows(mine, width, parts):
    row_blocks, rows, cols, _ = mine.shape
    return pl.pallas_call(
        functools.partial(window_kernel, parts),
        out_shape=(pltpu.VMEM((row_blocks // 2, rows, cols, width), bf16),) * len(parts),
        in_specs=[in_place],
        out_specs=(whole,) * len(parts),
        scratch_shapes=[pltpu.SemaphoreType.DMA((len(parts),))],
        compiler_params=params(4),
        name="windows",
    )(hbm(mine))


def merge_kernel(hops, mine, low_in, high_in, low_out, high_out):
    half, width = low_in.shape[0], low_in.shape[-1]
    for k, (came, out) in enumerate(((low_in, low_out), (high_in, high_out))):
        column = column_at(hops[k], width)
        for b in range(half):
            own = mine[k * half + b, :, :, column].astype(f32)
            out[b] = (own + came[b].astype(f32)).astype(bf16)


def merged(mine, hops, low_in, high_in):
    return pl.pallas_call(
        functools.partial(merge_kernel, hops),
        out_shape=(pltpu.VMEM(low_in.shape, bf16),) * 2,
        in_specs=[whole] * 3,
        out_specs=(whole, whole),
        compiler_params=params(4),
        name="merge_far_part",
    )(vmem(mine), vmem(low_in), vmem(high_in))


def gather_kernel(table, mine, ups, downs, ups_more, downs_more, out, held):
    row_blocks, rows, cols, _ = mine.shape
    width = ups.shape[-1]
    half = row_blocks // 2
    column = column_at(0, width)
    out[...] = jnp.zeros_like(out)
    for b in range(row_blocks):
        near, far = (downs, ups_more) if b < half else (ups, downs_more)
        total = mine[b, :, :, column].astype(f32) + near[b % half].astype(f32)
        total = total + far[b % half].astype(f32)
        held[b] = total.reshape(rows * cols, width)
        for c in range(cols):
            piece = held[b, pl.ds(c, rows, stride=cols), :]
            out[table[b * cols + c]] = piece.astype(out.dtype)


def gather_pieces(table, mine, arrived, slots):
    half, rows, cols, width = arrived[0].shape
    return pl.pallas_call(
        gather_kernel,
        out_shape=jax.ShapeDtypeStruct((slots, rows, width), bf16),
        in_specs=[scalars] + [whole] * 5,
        out_specs=whole,
        scratch_shapes=[pltpu.VMEM((2 * half, rows * cols, width), f32)],
        compiler_params=params(6),
        name="sum_and_gather",
    )(table, vmem(mine), *[vmem(a) for a in arrived])


def place_kernel(per_step, rows, cols, table, arrived, out, held):
    step = pl.program_id(0)
    for b in range(per_step):
        for c in range(cols):
            slot = table[(step * per_step + b) * cols + c]
            held[b, pl.ds(c, rows, stride=cols), :] = arrived[slot].astype(f32)
        out[b] = held[b].reshape(rows, cols, held.shape[-1]).astype(out.dtype)


def place_pieces(table, arrived, row_blocks, cols):
    slots, rows, width = arrived.shape
    per_step = 4
    return pl.pallas_call(
        functools.partial(place_kernel, per_step, rows, cols),
        out_shape=jax.ShapeDtypeStruct((row_blocks, rows, cols, width), bf16),
        grid=(row_blocks // per_step,),
        in_specs=[scalars, whole],
        out_specs=pl.BlockSpec((per_step, rows, cols, width), lambda i: (i, 0, 0, 0)),
        scratch_shapes=[pltpu.VMEM((per_step, rows * cols, width), f32)],
        compiler_params=params(4),
        name="place_pieces",
    )(table, vmem(arrived))


def early_kernel(slots, count, *refs):
    items = len(slots)
    ins, outs = refs[: 2 * items], refs[2 * items : 6 * items]
    roots, factors, lows, products, traces, in_sem, out_sem = refs[6 * items :]
    n = roots.shape[1]

    def arrivals(k):
        return [
            pltpu.make_async_copy(
                ins[2 * k + i].at[slots[k]], held.at[k], in_sem.at[k, i]
            )
            for i, held in enumerate((roots, factors))
        ]

    def departures(k):
        return [
            pltpu.make_async_copy(held.at[k], outs[4 * k + 1 + i], out_sem.at[k, i])
            for i, held in enumerate((lows, products, traces))
        ]

    @pl.when(slots[0] < count[0])
    def _():
        arrivals(0)[0].start()

    for k in range(items):

        @pl.when(slots[k] < count[0])
        def _():
            coming, going = arrivals(k), departures(k)
            coming[0].wait()
            coming[1].start()
            if k + 1 < items:

                @pl.when(slots[k + 1] < count[0])
                def _():
                    arrivals(k + 1)[0].start()

            x = halves(roots[k])
            square = halves(mul3(x, x))
            fourth = halves(mul3(square, square))
            fifth = halves(mul3(x, fourth))
            outs[4 * k][...], lows[k] = fifth
            going[0].start()
            coming[1].wait()
            total = jnp.zeros((128, 128), f32)
            on = lax.broadcasted_iota(jnp.int32, (128, 128), 0)
            on = on == lax.broadcasted_iota(jnp.int32, (128, 128), 1)
            for d in range(0, n, 128):
                total += factors[k, d : d + 128, d : d + 128]
            traces[k] = jnp.full(traces.shape[1:], jnp.sum(jnp.where(on, total, 0.0)))
            products[k] = decay_rate * mul3(fifth, halves(factors[k]))
            going[1].start()
            going[2].start()

    for k in range(items):

        @pl.when(slots[k] < count[0])
        def _():
            for copy in departures(k):
                copy.wait()


def early(count, *items):
    n = items[0][1].shape[1]
    many = len(items)
    made = pl.pallas_call(
        functools.partial(early_kernel, [t for t, _, _ in items]),
        out_shape=(
            pltpu.VMEM((n, n), bf16),
            stored(n, n, dtype=bf16),
            stored(n, n),
            stored(8, 128),
        )
        * many,
        in_specs=[scalars] + [in_place] * (2 * many),
        out_specs=(whole, in_place, in_place, in_place) * many,
        scratch_shapes=[
            pltpu.VMEM((many, n, n), f32),
            pltpu.VMEM((many, n, n), f32),
            pltpu.VMEM((many, n, n), bf16),
            pltpu.VMEM((many, n, n), f32),
            pltpu.VMEM((many, 8, 128), f32),
            pltpu.SemaphoreType.DMA((many, 2)),
            pltpu.SemaphoreType.DMA((many, 3)),
        ],
        compiler_params=params(28),
        cost_estimate=pl.CostEstimate(
            flops=many * 12 * 2 * n**3,
            bytes_accessed=many * 16 * n * n,
            transcendentals=0,
        ),
        name="early_products",
    )(count, *[hbm(x) for _, *pair in items for x in pair])
    return [made[4 * k : 4 * k + 4] for k in range(many)]


def assembled(pieces, t, block):
    parts, shards, _, rows, width = pieces.shape
    for z in range(parts):
        block[:, z * width : (z + 1) * width] = pieces[z, :, t].reshape(
            shards * rows, width
        )
    return block[...]


def square_sum(block):
    wide = block.astype(f32)
    return jnp.sum(wide * wide)


def quarter_scale(trace, square, gain, n):
    return (0.25 * n) / (decay_rate * trace[0:1, 0:1] + gain * square)


def update_kernel(gain, slots, count, pieces, xl, xr, *refs):
    ready, refs = refs[: 6 * slots], refs[6 * slots :]
    out, blocks, singles, traces, made, in_sem, out_sem = refs
    parts, shards, _, rows, width = made.shape
    n = parts * width

    def arrivals(t):
        _, pl_, tl, _, pr, tr = ready[6 * t : 6 * t + 6]
        sources = (
            (tl, traces.at[t, 0]),
            (xl.at[t], singles.at[t, 0]),
            (pl_, singles.at[t, 1]),
            (tr, traces.at[t, 1]),
            (xr.at[t], singles.at[t, 2]),
            (pr, singles.at[t, 3]),
        )
        return [
            pltpu.make_async_copy(a, b, in_sem.at[t, k]) for k, (a, b) in enumerate(sources)
        ]

    def departure(h):
        span = pl.ds(h * parts // 2, parts // 2)
        return pltpu.make_async_copy(made.at[span], out.at[span], out_sem.at[h])

    def work(ts):
        copies = {t: arrivals(t) for t in ts}
        for t in ts:
            for copy in copies[t]:
                copy.start()
        g, left, right, part, square = {}, {}, {}, {}, {}
        for t in ts:
            g[t] = assembled(pieces, t, blocks.at[t])
            square[t] = square_sum(g[t])
        for t in ts:
            left[t] = mul_t(mul(ready[6 * t][...], g[t]).astype(bf16), g[t])
        for t in ts:
            right[t] = mul(mul_t(ready[6 * t + 3][...], g[t]).astype(bf16), g[t])
        for t in ts:
            for copy in copies[t][:3]:
                copy.wait()
            scale = quarter_scale(traces[t, 0], square[t], gain, n)
            left[t] = 1.25 * singles[t, 0] - scale * (singles[t, 1] + gain * left[t])
            part[t] = mul(left[t].astype(bf16), g[t]).astype(bf16)
        for t in ts:
            for copy in copies[t][3:]:
                copy.wait()
            scale = quarter_scale(traces[t, 1], square[t], gain, n)
            right[t] = 1.25 * singles[t, 2] - scale * (singles[t, 3] + gain * right[t])
            right[t] = right[t].astype(bf16)
        for h in range(2):
            for t in ts:
                done = mul(part[t], right[t][:, h * n // 2 : (h + 1) * n // 2]).astype(bf16)
                for k in range(parts // 2):
                    made[h * parts // 2 + k, :, t] = done[
                        :, k * width : (k + 1) * width
                    ].reshape(shards, rows, width)
            departure(h).start()

    for live in range(slots + 1):

        @pl.when(count[0] == live)
        def _():
            for t in range(live, slots):
                made[:, :, t] = jnp.zeros_like(made[:, :, t])
            if live:
                work(range(live))
            else:
                departure(0).start()
                departure(1).start()

    departure(0).wait()
    departure(1).wait()


def update_pieces(gain, count, pieces, xl, xr, ready):
    slots = pieces.shape[2]
    n = xl.shape[1]
    inputs = []
    for sides in ready:
        for high, _, product, trace in sides:
            inputs += [vmem(high), hbm(product), hbm(trace)]
    return pl.pallas_call(
        functools.partial(update_kernel, gain, slots),
        out_shape=stored(*pieces.shape, dtype=bf16),
        in_specs=[scalars, whole] + [in_place] * 2
        + [whole, in_place, in_place] * (len(inputs) // 3),
        out_specs=in_place,
        scratch_shapes=[
            pltpu.VMEM((slots, n, n), bf16),
            pltpu.VMEM((slots, 4, n, n), f32),
            pltpu.VMEM((slots, 2, 8, 128), f32),
            pltpu.VMEM(pieces.shape, bf16),
            pltpu.SemaphoreType.DMA((slots, 6)),
            pltpu.SemaphoreType.DMA((2,)),
        ],
        compiler_params=params(32),
        name="update_pieces",
    )(count, vmem(pieces), hbm(xl), hbm(xr), *inputs)


def state_kernel(gain, slots, count, pieces, left, right, xl, xr, *refs):
    ready, refs = refs[: 8 * slots], refs[8 * slots :]
    outs, refs = refs[:4], refs[4:]
    block, fives, singles, traces, made, in_sem, out_sem = refs
    n = xl.shape[1]
    olds = (left, right, xl, xr)

    def arrivals(t):
        flh, fll, pl_, tl, frh, frl, pr, tr = ready[8 * t : 8 * t + 8]
        sources = [(a, fives.at[t, k]) for k, a in enumerate((flh, fll, frh, frl))]
        sources += [(a.at[t], singles.at[t, k]) for k, a in enumerate(olds)]
        sources += [(a, singles.at[t, 4 + k]) for k, a in enumerate((pl_, pr))]
        sources += [(a, traces.at[t, k]) for k, a in enumerate((tl, tr))]
        return [
            pltpu.make_async_copy(a, b, in_sem.at[t, k]) for k, (a, b) in enumerate(sources)
        ]

    def departures(t):
        return [
            pltpu.make_async_copy(made.at[t, k], out.at[t], out_sem.at[t, k])
            for k, out in enumerate(outs)
        ]

    def carried(t):
        return [
            pltpu.make_async_copy(old.at[t], made.at[t, k], in_sem.at[t, k])
            for k, old in enumerate(olds)
        ]

    for t in range(slots):

        @pl.when(t < count[0])
        def _():
            for copy in arrivals(t):
                copy.start()

        @pl.when(t >= count[0])
        def _():
            for copy in carried(t):
                copy.start()

    for t in range(slots):

        @pl.when(t < count[0])
        def _():
            copies, leaving = arrivals(t), departures(t)
            g = assembled(pieces, t, block)
            for copy in copies:
                copy.wait()
            square = square_sum(g)
            left_scale = quarter_scale(traces[t, 0], square, gain, n)
            right_scale = quarter_scale(traces[t, 1], square, gain, n)
            made[t, 0] = decay_rate * singles[t, 0] + gain * mul_t(g, g)
            leaving[0].start()
            made[t, 1] = decay_rate * singles[t, 1] + gain * t_mul(g, g)
            leaving[1].start()
            high, low = halves(mul(fives[t, 0], g) + mul(fives[t, 1], g))
            m = mul_t(high, g) + mul_t(low, g)
            made[t, 2] = 1.25 * singles[t, 2] - left_scale * (singles[t, 4] + gain * m)
            leaving[2].start()
            high, low = halves(mul_t(fives[t, 2], g) + mul_t(fives[t, 3], g))
            m = mul(high, g) + mul(low, g)
            made[t, 3] = 1.25 * singles[t, 3] - right_scale * (singles[t, 5] + gain * m)
            leaving[3].start()

        @pl.when(t >= count[0])
        def _():
            for came, leaves in zip(carried(t), departures(t)):
                came.wait()
                leaves.start()

    for t in range(slots):
        for copy in departures(t):
            copy.wait()


def new_state(gain, count, pieces, left, right, xl, xr, ready):
    slots, n, _ = left.shape
    inputs = [hbm(x) for sides in ready for made in sides for x in made]
    return pl.pallas_call(
        functools.partial(state_kernel, gain, slots),
        out_shape=(stored(slots, n, n),) * 4,
        in_specs=[scalars, whole] + [in_place] * (4 + len(inputs)),
        out_specs=(in_place,) * 4,
        scratch_shapes=[
            pltpu.VMEM((n, n), bf16),
            pltpu.VMEM((slots, 4, n, n), bf16),
            pltpu.VMEM((slots, 6, n, n), f32),
            pltpu.VMEM((slots, 2, 8, 128), f32),
            pltpu.VMEM((slots, 4, n, n), f32),
            pltpu.SemaphoreType.DMA((slots, 12)),
            pltpu.SemaphoreType.DMA((slots, 4)),
        ],
        compiler_params=params(40),
        cost_estimate=pl.CostEstimate(
            flops=slots * 10 * 2 * n**3,
            bytes_accessed=slots * 48 * n * n,
            transcendentals=0,
        ),
        name="new_state",
    )(count, vmem(pieces), *[hbm(x) for x in (left, right, xl, xr)], *inputs)


def body(
    gradients, owner_list, row_offset, col_offset, left_factor, right_factor, left_root, right_root
):
    replicas = lax.axis_size("dp")
    shards = lax.axis_size("shard")
    slots, n, _ = left_factor.shape
    _, row_blocks, rows, cols, _ = gradients.shape
    width = n // replicas
    gain = (1.0 - decay_rate) / n
    mine = gradients[0]

    def hop(x, step):
        return lax.ppermute(x, "dp", [(i, (i + step) % replicas) for i in range(replicas)])

    half = row_blocks // 2
    far_low, far_high = windows(mine, width, ((0, 2), (half, 2)))
    far_low, far_high = hop(far_low, 1), hop(far_high, -1)
    near_high, near_low = windows(mine, width, ((half, 1), (0, 3)))
    near_high, near_low = hop(near_high, 1), hop(near_low, -1)

    entries = jnp.arange(owner_list.shape[0], dtype=jnp.int32)
    same = owner_list[None, :] == owner_list[:, None]
    earlier = jnp.sum(same & (entries[None, :] < entries[:, None]), axis=1)
    slot_of = owner_list * slots + earlier.astype(jnp.int32)
    block_of = row_offset // n * cols + col_offset // n
    table = jnp.sum(
        jnp.where(block_of[None, :] == entries[:, None], slot_of[None, :], 0), axis=1
    ).astype(jnp.int32)
    owner = lax.axis_index(("dp", "shard"))
    count = jnp.sum((owner_list == owner).astype(jnp.int32)).reshape(1)

    far_low, far_high = merged(mine, (1, 3), far_low, far_high)
    far_low, far_high = hop(far_low, 1), hop(far_high, -1)
    (first,) = early(count, (0, left_root, left_factor))
    arrived = (near_high, near_low, far_low, far_high)
    arrived, first = lax.optimization_barrier((arrived, first))

    all_slots = replicas * shards * slots
    outgoing = gather_pieces(table, mine, arrived, all_slots)
    incoming = lax.all_to_all(outgoing, ("dp", "shard"), split_axis=0, concat_axis=0, tiled=True)
    sides = ((left_root, left_factor), (right_root, right_factor))
    rest = [(t, *side) for t in range(slots) for side in sides][1:]
    ready = [first, *early(count, *rest)]
    incoming, ready = lax.optimization_barrier((incoming, ready))
    ready = [ready[2 * t : 2 * t + 2] for t in range(slots)]
    pieces = incoming.reshape(replicas, shards, slots, rows, width)
    outbound = update_pieces(gain, count, pieces, left_root, right_root, ready)
    returned = lax.all_to_all(
        outbound.reshape(all_slots, rows, width),
        ("dp", "shard"), split_axis=0, concat_axis=0, tiled=True,
    )
    new_left, new_right, new_xl, new_xr = new_state(
        gain, count, pieces, left_factor, right_factor, left_root, right_root, ready
    )
    update = place_pieces(table, returned, row_blocks, cols)
    return update, new_left, new_right, new_xl, new_xr


def solution(mesh):
    slots = P(("dp", "shard"), None, None)
    in_specs = (P("dp", None, "shard", None, None), P(), P(), P(), slots, slots, slots, slots)
    out_specs = (P(None, "shard", None, "dp"), slots, slots, slots, slots)
    return jax.shard_map(body, mesh=mesh, in_specs=in_specs, out_specs=out_specs, check_vma=False)
```

```python
import functools

import jax
import jax.numpy as jnp
from jax import lax
from jax.experimental import pallas as pl
from jax.experimental.pallas import tpu as pltpu
from jax.sharding import PartitionSpec as P

decay_rate = 0.9
f32 = jnp.float32
bf16 = jnp.bfloat16
MIB = 1 << 20


def params(mib):
    return pltpu.CompilerParams(vmem_limit_bytes=mib * MIB)


def halves(x):
    high = x.astype(bf16)
    return high, (x - high.astype(f32)).astype(bf16)


def mul(a, b):
    return jnp.dot(a, b, preferred_element_type=f32)


def mul_t(a, b):
    return lax.dot_general(a, b, (((1,), (1,)), ((), ())), preferred_element_type=f32)


def t_mul(a, b):
    return lax.dot_general(a, b, (((0,), (0,)), ((), ())), preferred_element_type=f32)


def mul3(a, b):
    return mul(a[0], b[0]) + (mul(a[0], b[1]) + mul(a[1], b[0]))


def vmem(x):
    return pltpu.with_memory_space_constraint(x, pltpu.VMEM)


def hbm(x):
    return pltpu.with_memory_space_constraint(x, pltpu.HBM)


def stored(*shape, dtype=f32):
    return pltpu.HBM(shape, dtype)


whole = pl.BlockSpec(memory_space=pltpu.VMEM)
scalars = pl.BlockSpec(memory_space=pltpu.SMEM)
in_place = pl.BlockSpec(memory_space=pl.ANY)


def column_at(hop, width):
    replicas = lax.axis_size("dp")
    z = lax.rem(lax.axis_index("dp").astype(jnp.int32) + hop, replicas)
    return pl.ds(pl.multiple_of(z * width, width), width)


def window_kernel(parts, mine, *refs):
    outs, sem = refs[:-1], refs[-1]
    copies = []
    for k, ((low, hop), out) in enumerate(zip(parts, outs)):
        half, width = out.shape[0], out.shape[-1]
        source = mine.at[low : low + half, :, :, column_at(hop, width)]
        copies.append(pltpu.make_async_copy(source, out, sem.at[k]))
    for copy in copies:
        copy.start()
    for copy in copies:
        copy.wait()


def windows(mine, width, parts):
    row_blocks, rows, cols, _ = mine.shape
    return pl.pallas_call(
        functools.partial(window_kernel, parts),
        out_shape=(pltpu.VMEM((row_blocks // 2, rows, cols, width), bf16),) * len(parts),
        in_specs=[in_place],
        out_specs=(whole,) * len(parts),
        scratch_shapes=[pltpu.SemaphoreType.DMA((len(parts),))],
        compiler_params=params(4),
        name="windows",
    )(hbm(mine))


def merge_kernel(hops, mine, low_in, high_in, low_out, high_out):
    half, width = low_in.shape[0], low_in.shape[-1]
    for k, (came, out) in enumerate(((low_in, low_out), (high_in, high_out))):
        column = column_at(hops[k], width)
        for b in range(half):
            own = mine[k * half + b, :, :, column].astype(f32)
            out[b] = (own + came[b].astype(f32)).astype(bf16)


def merged(mine, hops, low_in, high_in):
    return pl.pallas_call(
        functools.partial(merge_kernel, hops),
        out_shape=(pltpu.VMEM(low_in.shape, bf16),) * 2,
        in_specs=[whole] * 3,
        out_specs=(whole, whole),
        compiler_params=params(4),
        name="merge_far_part",
    )(vmem(mine), vmem(low_in), vmem(high_in))


def gather_kernel(table, mine, ups, downs, ups_more, downs_more, out, held):
    row_blocks, rows, cols, _ = mine.shape
    width = ups.shape[-1]
    half = row_blocks // 2
    column = column_at(0, width)
    out[...] = jnp.zeros_like(out)
    for b in range(row_blocks):
        near, far = (downs, ups_more) if b < half else (ups, downs_more)
        total = mine[b, :, :, column].astype(f32) + near[b % half].astype(f32)
        total = total + far[b % half].astype(f32)
        held[b] = total.reshape(rows * cols, width)
        for c in range(cols):
            piece = held[b, pl.ds(c, rows, stride=cols), :]
            out[table[b * cols + c]] = piece.astype(out.dtype)


def gather_pieces(table, mine, arrived, slots):
    half, rows, cols, width = arrived[0].shape
    return pl.pallas_call(
        gather_kernel,
        out_shape=jax.ShapeDtypeStruct((slots, rows, width), bf16),
        in_specs=[scalars] + [whole] * 5,
        out_specs=whole,
        scratch_shapes=[pltpu.VMEM((2 * half, rows * cols, width), f32)],
        compiler_params=params(6),
        name="sum_and_gather",
    )(table, vmem(mine), *[vmem(a) for a in arrived])


def place_kernel(per_step, rows, cols, table, arrived, out, held):
    step = pl.program_id(0)
    for b in range(per_step):
        for c in range(cols):
            slot = table[(step * per_step + b) * cols + c]
            held[b, pl.ds(c, rows, stride=cols), :] = arrived[slot].astype(f32)
        out[b] = held[b].reshape(rows, cols, held.shape[-1]).astype(out.dtype)


def place_pieces(table, arrived, row_blocks, cols):
    slots, rows, width = arrived.shape
    per_step = 4
    return pl.pallas_call(
        functools.partial(place_kernel, per_step, rows, cols),
        out_shape=jax.ShapeDtypeStruct((row_blocks, rows, cols, width), bf16),
        grid=(row_blocks // per_step,),
        in_specs=[scalars, whole],
        out_specs=pl.BlockSpec((per_step, rows, cols, width), lambda i: (i, 0, 0, 0)),
        scratch_shapes=[pltpu.VMEM((per_step, rows * cols, width), f32)],
        compiler_params=params(4),
        name="place_pieces",
    )(table, vmem(arrived))


def early_kernel(slots, count, *refs):
    items = len(slots)
    ins, outs = refs[:items], refs[items : 3 * items]
    roots, lows, in_sem, out_sem = refs[3 * items :]

    def arrival(k):
        return pltpu.make_async_copy(ins[k].at[slots[k]], roots.at[k], in_sem.at[k])

    def departure(k):
        return pltpu.make_async_copy(lows.at[k], outs[2 * k + 1], out_sem.at[k])

    for k in range(items):

        @pl.when(slots[k] < count[0])
        def _():
            arrival(k).start()

    for k in range(items):

        @pl.when(slots[k] < count[0])
        def _():
            arrival(k).wait()
            x = halves(roots[k])
            square = halves(mul3(x, x))
            fourth = halves(mul3(square, square))
            outs[2 * k][...], lows[k] = halves(mul3(x, fourth))
            departure(k).start()

    for k in range(items):

        @pl.when(slots[k] < count[0])
        def _():
            departure(k).wait()


def early(count, *items):
    n = items[0][1].shape[1]
    many = len(items)
    made = pl.pallas_call(
        functools.partial(early_kernel, [t for t, _ in items]),
        out_shape=(pltpu.VMEM((n, n), bf16), stored(n, n, dtype=bf16)) * many,
        in_specs=[scalars] + [in_place] * many,
        out_specs=(whole, in_place) * many,
        scratch_shapes=[
            pltpu.VMEM((many, n, n), f32),
            pltpu.VMEM((many, n, n), bf16),
            pltpu.SemaphoreType.DMA((many,)),
            pltpu.SemaphoreType.DMA((many,)),
        ],
        compiler_params=params(20),
        cost_estimate=pl.CostEstimate(
            flops=many * 9 * 2 * n**3,
            bytes_accessed=many * 8 * n * n,
            transcendentals=0,
        ),
        name="early_products",
    )(count, *[hbm(root) for _, root in items])
    return [made[2 * k : 2 * k + 2] for k in range(many)]


def assembled(pieces, t, block):
    parts, shards, _, rows, width = pieces.shape
    for z in range(parts):
        block[:, z * width : (z + 1) * width] = pieces[z, :, t].reshape(
            shards * rows, width
        )
    return block[...]


def quarter_scale(factor):
    n, tile = factor.shape[0], 128
    on = lax.broadcasted_iota(jnp.int32, (tile, tile), 0)
    on = on == lax.broadcasted_iota(jnp.int32, (tile, tile), 1)
    total = factor[:tile, :tile]
    for d in range(tile, n, tile):
        total = total + factor[d : d + tile, d : d + tile]
    return (0.25 * n) / jnp.sum(jnp.where(on, total, 0.0))


def update_kernel(gain, slots, count, pieces, left, right, xl, xr, *refs):
    fives, refs = refs[: 2 * slots], refs[2 * slots :]
    out, blocks, singles, made, in_sem, out_sem = refs
    parts, shards, _, rows, width = made.shape
    n = parts * width
    olds = (left, xl, right, xr)

    def arrivals(t):
        return [
            pltpu.make_async_copy(old.at[t], singles.at[t, k], in_sem.at[t, k])
            for k, old in enumerate(olds)
        ]

    def departure(h):
        span = pl.ds(h * parts // 2, parts // 2)
        return pltpu.make_async_copy(made.at[span], out.at[span], out_sem.at[h])

    def root(t, k, gram, copies):
        copies[2 * k].wait()
        factor = singles[t, 2 * k] + (gain / decay_rate) * gram
        scale = quarter_scale(factor)
        product = mul(fives[2 * t + k][...], factor.astype(bf16))
        copies[2 * k + 1].wait()
        return (1.25 * singles[t, 2 * k + 1] - scale * product).astype(bf16)

    def work(ts):
        copies = {t: arrivals(t) for t in ts}
        for k in range(4):
            for t in ts:
                copies[t][k].start()
        g, part, side = {}, {}, {}
        for t in ts:
            g[t] = assembled(pieces, t, blocks.at[t])
        grams = {t: (mul_t(g[t], g[t]), t_mul(g[t], g[t])) for t in ts}
        for t in ts:
            side[t] = root(t, 0, grams[t][0], copies[t])
            part[t] = mul(side[t], g[t]).astype(bf16)
        for t in ts:
            side[t] = root(t, 1, grams[t][1], copies[t])
        for h in range(2):
            for t in ts:
                done = mul(part[t], side[t][:, h * n // 2 : (h + 1) * n // 2]).astype(bf16)
                for k in range(parts // 2):
                    made[h * parts // 2 + k, :, t] = done[
                        :, k * width : (k + 1) * width
                    ].reshape(shards, rows, width)
            departure(h).start()

    for live in range(slots + 1):

        @pl.when(count[0] == live)
        def _():
            for t in range(live, slots):
                made[:, :, t] = jnp.zeros_like(made[:, :, t])
            if live:
                work(range(live))
            else:
                departure(0).start()
                departure(1).start()

    departure(0).wait()
    departure(1).wait()


def update_pieces(gain, count, pieces, state, ready):
    slots = pieces.shape[2]
    n = state[0].shape[1]
    fives = [vmem(high) for sides in ready for high, _ in sides]
    return pl.pallas_call(
        functools.partial(update_kernel, gain, slots),
        out_shape=stored(*pieces.shape, dtype=bf16),
        in_specs=[scalars, whole] + [in_place] * 4 + [whole] * len(fives),
        out_specs=in_place,
        scratch_shapes=[
            pltpu.VMEM((slots, n, n), bf16),
            pltpu.VMEM((slots, 4, n, n), f32),
            pltpu.VMEM(pieces.shape, bf16),
            pltpu.SemaphoreType.DMA((slots, 4)),
            pltpu.SemaphoreType.DMA((2,)),
        ],
        compiler_params=params(36),
        name="update_pieces",
    )(count, vmem(pieces), *[hbm(x) for x in state], *fives)


def state_kernel(gain, slots, count, pieces, left, right, xl, xr, *refs):
    ready, refs = refs[: 4 * slots], refs[4 * slots :]
    outs, refs = refs[:4], refs[4:]
    block, fives, made, in_sem, out_sem = refs
    olds = (left, right, xl, xr)

    def arrivals(t):
        sources = [(a.at[t], made.at[t, k]) for k, a in enumerate(olds)]
        sources += [(a, fives.at[t, k]) for k, a in enumerate(ready[4 * t : 4 * t + 4])]
        return [
            pltpu.make_async_copy(a, b, in_sem.at[t, k]) for k, (a, b) in enumerate(sources)
        ]

    def departures(t):
        return [
            pltpu.make_async_copy(made.at[t, k], out.at[t], out_sem.at[t, k])
            for k, out in enumerate(outs)
        ]

    for t in range(slots):
        for copy in arrivals(t)[:4]:
            copy.start()

        @pl.when(t < count[0])
        def _():
            for copy in arrivals(t)[4:]:
                copy.start()

    for t in range(slots):
        for copy in arrivals(t)[:4]:
            copy.wait()

        @pl.when(t < count[0])
        def _():
            g = assembled(pieces, t, block)
            for copy in arrivals(t)[4:]:
                copy.wait()
            for k in range(2):
                gram = t_mul(g, g) if k else mul_t(g, g)
                made[t, k] = decay_rate * made[t, k] + gain * gram
                departures(t)[k].start()
                factor = made[t, k]
                product = mul3((fives[t, 2 * k], fives[t, 2 * k + 1]), halves(factor))
                made[t, 2 + k] = 1.25 * made[t, 2 + k] - quarter_scale(factor) * product
                departures(t)[2 + k].start()

        @pl.when(t >= count[0])
        def _():
            for copy in departures(t):
                copy.start()

    for t in range(slots):
        for copy in departures(t):
            copy.wait()


def new_state(gain, count, pieces, state, ready):
    slots, n, _ = state[0].shape
    inputs = [hbm(x) for sides in ready for made in sides for x in made]
    return pl.pallas_call(
        functools.partial(state_kernel, gain, slots),
        out_shape=(stored(slots, n, n),) * 4,
        in_specs=[scalars, whole] + [in_place] * (4 + len(inputs)),
        out_specs=(in_place,) * 4,
        scratch_shapes=[
            pltpu.VMEM((n, n), bf16),
            pltpu.VMEM((slots, 4, n, n), bf16),
            pltpu.VMEM((slots, 4, n, n), f32),
            pltpu.SemaphoreType.DMA((slots, 8)),
            pltpu.SemaphoreType.DMA((slots, 4)),
        ],
        compiler_params=params(36),
        cost_estimate=pl.CostEstimate(
            flops=slots * 8 * 2 * n**3,
            bytes_accessed=slots * 36 * n * n,
            transcendentals=0,
        ),
        name="new_state",
    )(count, vmem(pieces), *[hbm(x) for x in state], *inputs)


def body(
    gradients, owner_list, row_offset, col_offset, left_factor, right_factor, left_root, right_root
):
    replicas = lax.axis_size("dp")
    shards = lax.axis_size("shard")
    slots, n, _ = left_factor.shape
    _, row_blocks, rows, cols, _ = gradients.shape
    width = n // replicas
    gain = (1.0 - decay_rate) / n
    mine = gradients[0]

    def hop(x, step):
        return lax.ppermute(x, "dp", [(i, (i + step) % replicas) for i in range(replicas)])

    half = row_blocks // 2
    far = lax.rem(lax.axis_index("dp") + 2, replicas) * width
    far = lax.dynamic_slice_in_dim(mine, far, width, axis=3)
    far_low, far_high = far[:half], far[half:]
    far_low, far_high = hop(far_low, 1), hop(far_high, -1)
    near_high, near_low = windows(mine, width, ((half, 1), (0, 3)))
    near_high, near_low = hop(near_high, 1), hop(near_low, -1)

    entries = jnp.arange(owner_list.shape[0], dtype=jnp.int32)
    same = owner_list[None, :] == owner_list[:, None]
    earlier = jnp.sum(same & (entries[None, :] < entries[:, None]), axis=1)
    slot_of = owner_list * slots + earlier.astype(jnp.int32)
    block_of = row_offset // n * cols + col_offset // n
    table = jnp.sum(
        jnp.where(block_of[None, :] == entries[:, None], slot_of[None, :], 0), axis=1
    ).astype(jnp.int32)
    owner = lax.axis_index(("dp", "shard"))
    count = jnp.sum((owner_list == owner).astype(jnp.int32)).reshape(1)

    far_low, far_high = merged(mine, (1, 3), far_low, far_high)
    far_low, far_high = hop(far_low, 1), hop(far_high, -1)
    (first,) = early(count, (0, left_root))
    arrived = (near_high, near_low, far_low, far_high)
    arrived, first = lax.optimization_barrier((arrived, first))

    all_slots = replicas * shards * slots
    outgoing = gather_pieces(table, mine, arrived, all_slots)
    incoming = lax.all_to_all(outgoing, ("dp", "shard"), split_axis=0, concat_axis=0, tiled=True)
    rest = [(t, side) for t in range(slots) for side in (left_root, right_root)][1:]
    ready = [first, *early(count, *rest)]
    incoming, ready = lax.optimization_barrier((incoming, ready))
    ready = [ready[2 * t : 2 * t + 2] for t in range(slots)]
    pieces = incoming.reshape(replicas, shards, slots, rows, width)
    state = (left_factor, right_factor, left_root, right_root)
    outbound = update_pieces(gain, count, pieces, state, ready)
    returned = lax.all_to_all(
        outbound.reshape(all_slots, rows, width),
        ("dp", "shard"), split_axis=0, concat_axis=0, tiled=True,
    )
    new_left, new_right, new_xl, new_xr = new_state(gain, count, pieces, state, ready)
    update = place_pieces(table, returned, row_blocks, cols)
    return update, new_left, new_right, new_xl, new_xr


def solution(mesh):
    slots = P(("dp", "shard"), None, None)
    in_specs = (P("dp", None, "shard", None, None), P(), P(), P(), slots, slots, slots, slots)
    out_specs = (P(None, "shard", None, "dp"), slots, slots, slots, slots)
    return jax.shard_map(body, mesh=mesh, in_specs=in_specs, out_specs=out_specs, check_vma=False)
```

```python
import functools

import jax
import jax.numpy as jnp
from jax import lax
from jax.experimental import pallas as pl
from jax.experimental.pallas import tpu as pltpu
from jax.sharding import PartitionSpec as P

decay_rate = 0.9
f32 = jnp.float32
bf16 = jnp.bfloat16
MIB = 1 << 20


def params(mib):
    return pltpu.CompilerParams(vmem_limit_bytes=mib * MIB)


def halves(x):
    high = x.astype(bf16)
    return high, (x - high.astype(f32)).astype(bf16)


def mul(a, b):
    return jnp.dot(a, b, preferred_element_type=f32)


def mul_t(a, b):
    return lax.dot_general(a, b, (((1,), (1,)), ((), ())), preferred_element_type=f32)


def t_mul(a, b):
    return lax.dot_general(a, b, (((0,), (0,)), ((), ())), preferred_element_type=f32)


def mul3(a, b):
    return mul(a[0], b[0]) + (mul(a[0], b[1]) + mul(a[1], b[0]))


def vmem(x):
    return pltpu.with_memory_space_constraint(x, pltpu.VMEM)


def hbm(x):
    return pltpu.with_memory_space_constraint(x, pltpu.HBM)


def stored(*shape, dtype=f32):
    return pltpu.HBM(shape, dtype)


whole = pl.BlockSpec(memory_space=pltpu.VMEM)
scalars = pl.BlockSpec(memory_space=pltpu.SMEM)
in_place = pl.BlockSpec(memory_space=pl.ANY)


def column_at(hop, width):
    replicas = lax.axis_size("dp")
    z = lax.rem(lax.axis_index("dp").astype(jnp.int32) + hop, replicas)
    return pl.ds(pl.multiple_of(z * width, width), width)


def window_kernel(parts, mine, *refs):
    outs, sem = refs[:-1], refs[-1]
    copies = []
    for k, ((low, hop), out) in enumerate(zip(parts, outs)):
        half, width = out.shape[0], out.shape[-1]
        source = mine.at[low : low + half, :, :, column_at(hop, width)]
        copies.append(pltpu.make_async_copy(source, out, sem.at[k]))
    for copy in copies:
        copy.start()
    for copy in copies:
        copy.wait()


def windows(mine, width, parts):
    row_blocks, rows, cols, _ = mine.shape
    return pl.pallas_call(
        functools.partial(window_kernel, parts),
        out_shape=(pltpu.VMEM((row_blocks // 2, rows, cols, width), bf16),) * len(parts),
        in_specs=[in_place],
        out_specs=(whole,) * len(parts),
        scratch_shapes=[pltpu.SemaphoreType.DMA((len(parts),))],
        compiler_params=params(4),
        name="windows",
    )(hbm(mine))


def merge_kernel(low, hop, mine, came, out):
    column = column_at(hop, out.shape[-1])
    for b in range(out.shape[0]):
        own = mine[low + b, :, :, column].astype(f32)
        out[b] = (own + came[b].astype(f32)).astype(bf16)


def merged(mine, low, hop, came):
    return pl.pallas_call(
        functools.partial(merge_kernel, low, hop),
        out_shape=pltpu.VMEM(came.shape, bf16),
        in_specs=[whole] * 2,
        out_specs=whole,
        compiler_params=params(4),
        name="merge_far_part",
    )(vmem(mine), vmem(came))


def gather_kernel(table, mine, ups, downs, ups_more, downs_more, out, held):
    row_blocks, rows, cols, _ = mine.shape
    width = ups.shape[-1]
    half = row_blocks // 2
    column = column_at(0, width)
    out[...] = jnp.zeros_like(out)
    for b in range(row_blocks):
        near, far = (downs, ups_more) if b < half else (ups, downs_more)
        total = mine[b, :, :, column].astype(f32) + near[b % half].astype(f32)
        total = total + far[b % half].astype(f32)
        held[b] = total.reshape(rows * cols, width)
        for c in range(cols):
            piece = held[b, pl.ds(c, rows, stride=cols), :]
            out[table[b * cols + c]] = piece.astype(out.dtype)


def gather_pieces(table, mine, arrived, slots):
    half, rows, cols, width = arrived[0].shape
    return pl.pallas_call(
        gather_kernel,
        out_shape=jax.ShapeDtypeStruct((slots, rows, width), bf16),
        in_specs=[scalars] + [whole] * 5,
        out_specs=whole,
        scratch_shapes=[pltpu.VMEM((2 * half, rows * cols, width), f32)],
        compiler_params=params(6),
        name="sum_and_gather",
    )(table, vmem(mine), *[vmem(a) for a in arrived])


def place_kernel(per_step, rows, cols, table, arrived, out, held):
    step = pl.program_id(0)
    for b in range(per_step):
        for c in range(cols):
            slot = table[(step * per_step + b) * cols + c]
            held[b, pl.ds(c, rows, stride=cols), :] = arrived[slot].astype(f32)
        out[b] = held[b].reshape(rows, cols, held.shape[-1]).astype(out.dtype)


def place_pieces(table, arrived, row_blocks, cols):
    slots, rows, width = arrived.shape
    per_step = 4
    return pl.pallas_call(
        functools.partial(place_kernel, per_step, rows, cols),
        out_shape=jax.ShapeDtypeStruct((row_blocks, rows, cols, width), bf16),
        grid=(row_blocks // per_step,),
        in_specs=[scalars, whole],
        out_specs=pl.BlockSpec((per_step, rows, cols, width), lambda i: (i, 0, 0, 0)),
        scratch_shapes=[pltpu.VMEM((per_step, rows * cols, width), f32)],
        compiler_params=params(4),
        name="place_pieces",
    )(table, vmem(arrived))


def early_kernel(slots, count, *refs):
    items = len(slots)
    ins, outs = refs[: 2 * items], refs[2 * items : 5 * items]
    roots, factors, lows, short, in_sem, out_sem = refs[5 * items :]

    def arrivals(k):
        return [
            pltpu.make_async_copy(ins[2 * k + i].at[slots[k]], held.at[k], in_sem.at[k, i])
            for i, held in enumerate((roots, factors))
        ]

    def departures(k):
        return [
            pltpu.make_async_copy(held.at[k], outs[3 * k + 1 + i], out_sem.at[k, i])
            for i, held in enumerate((lows, short))
        ]

    for i in range(2):
        for k in range(items):

            @pl.when(slots[k] < count[0])
            def _():
                arrivals(k)[i].start()

    for k in range(items):

        @pl.when(slots[k] < count[0])
        def _():
            (root_in, factor_in), going = arrivals(k), departures(k)
            root_in.wait()
            x = halves(roots[k])
            square = halves(mul3(x, x))
            fourth = halves(mul3(square, square))
            factor_in.wait()
            short[k] = factors[k].astype(bf16)
            going[1].start()
            outs[3 * k][...], lows[k] = halves(mul3(x, fourth))
            going[0].start()

    for k in range(items):

        @pl.when(slots[k] < count[0])
        def _():
            for copy in departures(k):
                copy.wait()


def early(count, *items):
    n = items[0][1].shape[1]
    many = len(items)
    made = pl.pallas_call(
        functools.partial(early_kernel, [t for t, _, _ in items]),
        out_shape=(
            pltpu.VMEM((n, n), bf16),
            stored(n, n, dtype=bf16),
            stored(n, n, dtype=bf16),
        )
        * many,
        in_specs=[scalars] + [in_place] * (2 * many),
        out_specs=(whole, in_place, in_place) * many,
        scratch_shapes=[
            pltpu.VMEM((many, n, n), f32),
            pltpu.VMEM((many, n, n), f32),
            pltpu.VMEM((many, n, n), bf16),
            pltpu.VMEM((many, n, n), bf16),
            pltpu.SemaphoreType.DMA((many, 2)),
            pltpu.SemaphoreType.DMA((many, 2)),
        ],
        compiler_params=params(24),
        cost_estimate=pl.CostEstimate(
            flops=many * 9 * 2 * n**3,
            bytes_accessed=many * 12 * n * n,
            transcendentals=0,
        ),
        name="early_products",
    )(count, *[hbm(x) for _, *pair in items for x in pair])
    return [made[3 * k : 3 * k + 3] for k in range(many)]


def assembled(pieces, t, block):
    parts, shards, _, rows, width = pieces.shape
    for z in range(parts):
        block[:, z * width : (z + 1) * width] = pieces[z, :, t].reshape(
            shards * rows, width
        )
    return block[...]


def quarter_scale(factor):
    n, tile = factor.shape[0], 128
    on = lax.broadcasted_iota(jnp.int32, (tile, tile), 0)
    on = on == lax.broadcasted_iota(jnp.int32, (tile, tile), 1)
    total = factor[:tile, :tile]
    for d in range(tile, n, tile):
        total = total + factor[d : d + tile, d : d + tile]
    return (0.25 * n) / jnp.sum(jnp.where(on, total, 0.0))


def update_kernel(gain, slots, count, pieces, xl, xr, *refs):
    ready, refs = refs[: 4 * slots], refs[4 * slots :]
    out, blocks, roots, factors, made, in_sem, out_sem = refs
    parts, shards, _, rows, width = made.shape
    n = parts * width
    roots_in = (xl, xr)

    def arrivals(t):
        copies = []
        for k in range(2):
            sources = (
                (ready[4 * t + 2 * k + 1], factors.at[t, k]),
                (roots_in[k].at[t], roots.at[t, k]),
            )
            for a, b in sources:
                copies.append(pltpu.make_async_copy(a, b, in_sem.at[t, len(copies)]))
        return copies

    def departure(h):
        span = pl.ds(h * parts // 2, parts // 2)
        return pltpu.make_async_copy(made.at[span], out.at[span], out_sem.at[h])

    def root(t, k, gram, copies):
        copies[2 * k].wait()
        factor = factors[t, k].astype(f32) + (gain / decay_rate) * gram
        scale = quarter_scale(factor)
        product = mul(ready[4 * t + 2 * k][...], factor.astype(bf16))
        copies[2 * k + 1].wait()
        return (1.25 * roots[t, k] - scale * product).astype(bf16)

    def work(ts):
        copies = {t: arrivals(t) for t in ts}
        for k in range(4):
            for t in ts:
                copies[t][k].start()
        g, part, side = {}, {}, {}
        for t in ts:
            g[t] = assembled(pieces, t, blocks.at[t])
        grams = {t: (mul_t(g[t], g[t]), t_mul(g[t], g[t])) for t in ts}
        for t in ts:
            side[t] = root(t, 0, grams[t][0], copies[t])
            part[t] = mul(side[t], g[t]).astype(bf16)
        for t in ts:
            side[t] = root(t, 1, grams[t][1], copies[t])
        for h in range(2):
            for t in ts:
                done = mul(part[t], side[t][:, h * n // 2 : (h + 1) * n // 2]).astype(bf16)
                for k in range(parts // 2):
                    made[h * parts // 2 + k, :, t] = done[
                        :, k * width : (k + 1) * width
                    ].reshape(shards, rows, width)
            departure(h).start()

    for live in range(slots + 1):

        @pl.when(count[0] == live)
        def _():
            for t in range(live, slots):
                made[:, :, t] = jnp.zeros_like(made[:, :, t])
            if live:
                work(range(live))
            else:
                departure(0).start()
                departure(1).start()

    departure(0).wait()
    departure(1).wait()


def update_pieces(gain, count, pieces, xl, xr, ready):
    slots = pieces.shape[2]
    n = xl.shape[1]
    inputs = []
    for sides in ready:
        for high, _, factor in sides:
            inputs += [vmem(high), hbm(factor)]
    return pl.pallas_call(
        functools.partial(update_kernel, gain, slots),
        out_shape=stored(*pieces.shape, dtype=bf16),
        in_specs=[scalars, whole] + [in_place] * 2 + [whole, in_place] * (2 * slots),
        out_specs=in_place,
        scratch_shapes=[
            pltpu.VMEM((slots, n, n), bf16),
            pltpu.VMEM((slots, 2, n, n), f32),
            pltpu.VMEM((slots, 2, n, n), bf16),
            pltpu.VMEM(pieces.shape, bf16),
            pltpu.SemaphoreType.DMA((slots, 4)),
            pltpu.SemaphoreType.DMA((2,)),
        ],
        compiler_params=params(36),
        name="update_pieces",
    )(count, vmem(pieces), hbm(xl), hbm(xr), *inputs)


def state_kernel(gain, slots, count, pieces, left, right, xl, xr, *refs):
    ready, refs = refs[: 4 * slots], refs[4 * slots :]
    outs, refs = refs[:4], refs[4:]
    block, fives, made, in_sem, out_sem = refs
    olds = (left, right, xl, xr)

    def arrivals(t):
        sources = [(a.at[t], made.at[t, k]) for k, a in enumerate(olds)]
        sources += [(a, fives.at[t, k]) for k, a in enumerate(ready[4 * t : 4 * t + 4])]
        return [
            pltpu.make_async_copy(a, b, in_sem.at[t, k]) for k, (a, b) in enumerate(sources)
        ]

    def departures(t):
        return [
            pltpu.make_async_copy(made.at[t, k], out.at[t], out_sem.at[t, k])
            for k, out in enumerate(outs)
        ]

    for t in range(slots):
        for copy in arrivals(t)[:4]:
            copy.start()

        @pl.when(t < count[0])
        def _():
            for copy in arrivals(t)[4:]:
                copy.start()

    for t in range(slots):
        for copy in arrivals(t)[:4]:
            copy.wait()

        @pl.when(t < count[0])
        def _():
            g = assembled(pieces, t, block)
            for copy in arrivals(t)[4:]:
                copy.wait()
            for k in range(2):
                gram = t_mul(g, g) if k else mul_t(g, g)
                made[t, k] = decay_rate * made[t, k] + gain * gram
                departures(t)[k].start()
                factor = made[t, k]
                product = mul3((fives[t, 2 * k], fives[t, 2 * k + 1]), halves(factor))
                made[t, 2 + k] = 1.25 * made[t, 2 + k] - quarter_scale(factor) * product
                departures(t)[2 + k].start()

        @pl.when(t >= count[0])
        def _():
            for copy in departures(t):
                copy.start()

    for t in range(slots):
        for copy in departures(t):
            copy.wait()


def new_state(gain, count, pieces, state, ready):
    slots, n, _ = state[0].shape
    inputs = [hbm(x) for sides in ready for made in sides for x in made[:2]]
    return pl.pallas_call(
        functools.partial(state_kernel, gain, slots),
        out_shape=(stored(slots, n, n),) * 4,
        in_specs=[scalars, whole] + [in_place] * (4 + len(inputs)),
        out_specs=(in_place,) * 4,
        scratch_shapes=[
            pltpu.VMEM((n, n), bf16),
            pltpu.VMEM((slots, 4, n, n), bf16),
            pltpu.VMEM((slots, 4, n, n), f32),
            pltpu.SemaphoreType.DMA((slots, 8)),
            pltpu.SemaphoreType.DMA((slots, 4)),
        ],
        compiler_params=params(36),
        cost_estimate=pl.CostEstimate(
            flops=slots * 8 * 2 * n**3,
            bytes_accessed=slots * 36 * n * n,
            transcendentals=0,
        ),
        name="new_state",
    )(count, vmem(pieces), *[hbm(x) for x in state], *inputs)


def body(
    gradients, owner_list, row_offset, col_offset, left_factor, right_factor, left_root, right_root
):
    replicas = lax.axis_size("dp")
    shards = lax.axis_size("shard")
    slots, n, _ = left_factor.shape
    _, row_blocks, rows, cols, _ = gradients.shape
    width = n // replicas
    gain = (1.0 - decay_rate) / n
    mine = gradients[0]

    def hop(x, step):
        return lax.ppermute(x, "dp", [(i, (i + step) % replicas) for i in range(replicas)])

    half = row_blocks // 2
    far = lax.rem(lax.axis_index("dp") + 2, replicas) * width
    far = lax.dynamic_slice_in_dim(mine, far, width, axis=3)
    far_low, far_high = far[:half], far[half:]
    far_low, far_high = hop(far_low, 1), hop(far_high, -1)
    near_high, near_low = windows(mine, width, ((half, 1), (0, 3)))
    near_high, near_low = hop(near_high, 1), hop(near_low, -1)

    entries = jnp.arange(owner_list.shape[0], dtype=jnp.int32)
    same = owner_list[None, :] == owner_list[:, None]
    earlier = jnp.sum(same & (entries[None, :] < entries[:, None]), axis=1)
    slot_of = owner_list * slots + earlier.astype(jnp.int32)
    block_of = row_offset // n * cols + col_offset // n
    table = jnp.sum(
        jnp.where(block_of[None, :] == entries[:, None], slot_of[None, :], 0), axis=1
    ).astype(jnp.int32)
    owner = lax.axis_index(("dp", "shard"))
    count = jnp.sum((owner_list == owner).astype(jnp.int32)).reshape(1)

    far_low = hop(merged(mine, 0, 1, far_low), 1)
    far_high = hop(merged(mine, half, 3, far_high), -1)
    (first,) = early(count, (0, left_root, left_factor))
    arrived = (near_high, near_low, far_low, far_high)
    arrived, first = lax.optimization_barrier((arrived, first))

    all_slots = replicas * shards * slots
    outgoing = gather_pieces(table, mine, arrived, all_slots)
    incoming = lax.all_to_all(outgoing, ("dp", "shard"), split_axis=0, concat_axis=0, tiled=True)
    sides = ((left_root, left_factor), (right_root, right_factor))
    rest = [(t, *side) for t in range(slots) for side in sides][1:]
    ready = [first, *early(count, *rest)]
    incoming, ready = lax.optimization_barrier((incoming, ready))
    ready = [ready[2 * t : 2 * t + 2] for t in range(slots)]
    pieces = incoming.reshape(replicas, shards, slots, rows, width)
    state = (left_factor, right_factor, left_root, right_root)
    outbound = update_pieces(gain, count, pieces, left_root, right_root, ready)
    returned = lax.all_to_all(
        outbound.reshape(all_slots, rows, width),
        ("dp", "shard"), split_axis=0, concat_axis=0, tiled=True,
    )
    new_left, new_right, new_xl, new_xr = new_state(gain, count, pieces, state, ready)
    update = place_pieces(table, returned, row_blocks, cols)
    return update, new_left, new_right, new_xl, new_xr


def solution(mesh):
    slots = P(("dp", "shard"), None, None)
    in_specs = (P("dp", None, "shard", None, None), P(), P(), P(), slots, slots, slots, slots)
    out_specs = (P(None, "shard", None, "dp"), slots, slots, slots, slots)
    return jax.shard_map(body, mesh=mesh, in_specs=in_specs, out_specs=out_specs, check_vma=False)
```

```python
import functools

import jax
import jax.numpy as jnp
from jax import lax
from jax.experimental import pallas as pl
from jax.experimental.pallas import tpu as pltpu
from jax.sharding import PartitionSpec as P

decay_rate = 0.9
f32 = jnp.float32
bf16 = jnp.bfloat16
MIB = 1 << 20


def params(mib):
    return pltpu.CompilerParams(vmem_limit_bytes=mib * MIB)


def halves(x):
    high = x.astype(bf16)
    return high, (x - high.astype(f32)).astype(bf16)


def mul(a, b):
    return jnp.dot(a, b, preferred_element_type=f32)


def mul_t(a, b):
    return lax.dot_general(a, b, (((1,), (1,)), ((), ())), preferred_element_type=f32)


def t_mul(a, b):
    return lax.dot_general(a, b, (((0,), (0,)), ((), ())), preferred_element_type=f32)


def mul3(a, b):
    return mul(a[0], b[0]) + (mul(a[0], b[1]) + mul(a[1], b[0]))


def vmem(x):
    return pltpu.with_memory_space_constraint(x, pltpu.VMEM)


def hbm(x):
    return pltpu.with_memory_space_constraint(x, pltpu.HBM)


def stored(*shape, dtype=f32):
    return pltpu.HBM(shape, dtype)


whole = pl.BlockSpec(memory_space=pltpu.VMEM)
scalars = pl.BlockSpec(memory_space=pltpu.SMEM)
in_place = pl.BlockSpec(memory_space=pl.ANY)


def column_at(hop, width):
    replicas = lax.axis_size("dp")
    z = lax.rem(lax.axis_index("dp").astype(jnp.int32) + hop, replicas)
    return pl.ds(pl.multiple_of(z * width, width), width)


def window_kernel(parts, mine, *refs):
    outs, sem = refs[:-1], refs[-1]
    copies = []
    for k, ((low, hop), out) in enumerate(zip(parts, outs)):
        half, width = out.shape[0], out.shape[-1]
        source = mine.at[low : low + half, :, :, column_at(hop, width)]
        copies.append(pltpu.make_async_copy(source, out, sem.at[k]))
    for copy in copies:
        copy.start()
    for copy in copies:
        copy.wait()


def windows(mine, width, parts):
    row_blocks, rows, cols, _ = mine.shape
    return pl.pallas_call(
        functools.partial(window_kernel, parts),
        out_shape=(pltpu.VMEM((row_blocks // 2, rows, cols, width), bf16),) * len(parts),
        in_specs=[in_place],
        out_specs=(whole,) * len(parts),
        scratch_shapes=[pltpu.SemaphoreType.DMA((len(parts),))],
        compiler_params=params(4),
        name="windows",
    )(hbm(mine))


def merge_kernel(low, hop, mine, came, out):
    column = column_at(hop, out.shape[-1])
    for b in range(out.shape[0]):
        own = mine[low + b, :, :, column].astype(f32)
        out[b] = (own + came[b].astype(f32)).astype(bf16)


def merged(mine, low, hop, came):
    return pl.pallas_call(
        functools.partial(merge_kernel, low, hop),
        out_shape=pltpu.VMEM(came.shape, bf16),
        in_specs=[whole] * 2,
        out_specs=whole,
        compiler_params=params(4),
        name="merge_far_part",
    )(vmem(mine), vmem(came))


def gather_kernel(table, mine, ups, downs, ups_more, downs_more, out, held):
    row_blocks, rows, cols, _ = mine.shape
    width = ups.shape[-1]
    half = row_blocks // 2
    column = column_at(0, width)
    out[...] = jnp.zeros_like(out)
    for b in range(row_blocks):
        near, far = (downs, ups_more) if b < half else (ups, downs_more)
        total = mine[b, :, :, column].astype(f32) + near[b % half].astype(f32)
        total = total + far[b % half].astype(f32)
        held[b] = total.reshape(rows * cols, width)
        for c in range(cols):
            piece = held[b, pl.ds(c, rows, stride=cols), :]
            out[table[b * cols + c]] = piece.astype(out.dtype)


def gather_pieces(table, mine, arrived, slots):
    half, rows, cols, width = arrived[0].shape
    return pl.pallas_call(
        gather_kernel,
        out_shape=jax.ShapeDtypeStruct((slots, rows, width), bf16),
        in_specs=[scalars] + [whole] * 5,
        out_specs=whole,
        scratch_shapes=[pltpu.VMEM((2 * half, rows * cols, width), f32)],
        compiler_params=params(6),
        name="sum_and_gather",
    )(table, vmem(mine), *[vmem(a) for a in arrived])


def place_kernel(per_step, rows, cols, table, arrived, out, held):
    step = pl.program_id(0)
    for b in range(per_step):
        for c in range(cols):
            slot = table[(step * per_step + b) * cols + c]
            held[b, pl.ds(c, rows, stride=cols), :] = arrived[slot].astype(f32)
        out[b] = held[b].reshape(rows, cols, held.shape[-1]).astype(out.dtype)


def place_pieces(table, arrived, row_blocks, cols):
    slots, rows, width = arrived.shape
    per_step = 4
    return pl.pallas_call(
        functools.partial(place_kernel, per_step, rows, cols),
        out_shape=jax.ShapeDtypeStruct((row_blocks, rows, cols, width), bf16),
        grid=(row_blocks // per_step,),
        in_specs=[scalars, whole],
        out_specs=pl.BlockSpec((per_step, rows, cols, width), lambda i: (i, 0, 0, 0)),
        scratch_shapes=[pltpu.VMEM((per_step, rows * cols, width), f32)],
        compiler_params=params(4),
        name="place_pieces",
    )(table, vmem(arrived))


def early_kernel(slots, count, *refs):
    items = len(slots)
    ins, outs = refs[: 2 * items], refs[2 * items : 5 * items]
    roots, factors, lows, short, in_sem, out_sem = refs[5 * items :]

    def arrivals(k):
        return [
            pltpu.make_async_copy(ins[2 * k + i].at[slots[k]], held.at[k], in_sem.at[k, i])
            for i, held in enumerate((roots, factors))
        ]

    def departures(k):
        return [
            pltpu.make_async_copy(held.at[k], outs[3 * k + 1 + i], out_sem.at[k, i])
            for i, held in enumerate((lows, short))
        ]

    for i in range(2):
        for k in range(items):

            @pl.when(slots[k] < count[0])
            def _():
                arrivals(k)[i].start()

    for k in range(items):

        @pl.when(slots[k] < count[0])
        def _():
            (root_in, factor_in), going = arrivals(k), departures(k)
            root_in.wait()
            x = halves(roots[k])
            square = halves(mul3(x, x))
            fourth = halves(mul3(square, square))
            factor_in.wait()
            short[k] = factors[k].astype(bf16)
            going[1].start()
            outs[3 * k][...], lows[k] = halves(mul3(x, fourth))
            going[0].start()

    for k in range(items):

        @pl.when(slots[k] < count[0])
        def _():
            for copy in departures(k):
                copy.wait()


def early(count, *items):
    n = items[0][1].shape[1]
    many = len(items)
    made = pl.pallas_call(
        functools.partial(early_kernel, [t for t, _, _ in items]),
        out_shape=(
            pltpu.VMEM((n, n), bf16),
            stored(n, n, dtype=bf16),
            stored(n, n, dtype=bf16),
        )
        * many,
        in_specs=[scalars] + [in_place] * (2 * many),
        out_specs=(whole, in_place, in_place) * many,
        scratch_shapes=[
            pltpu.VMEM((many, n, n), f32),
            pltpu.VMEM((many, n, n), f32),
            pltpu.VMEM((many, n, n), bf16),
            pltpu.VMEM((many, n, n), bf16),
            pltpu.SemaphoreType.DMA((many, 2)),
            pltpu.SemaphoreType.DMA((many, 2)),
        ],
        compiler_params=params(24),
        cost_estimate=pl.CostEstimate(
            flops=many * 9 * 2 * n**3,
            bytes_accessed=many * 12 * n * n,
            transcendentals=0,
        ),
        name="early_products",
    )(count, *[hbm(x) for _, *pair in items for x in pair])
    return [made[3 * k : 3 * k + 3] for k in range(many)]


def assembled(pieces, t, block):
    parts, shards, _, rows, width = pieces.shape
    for z in range(parts):
        block[:, z * width : (z + 1) * width] = pieces[z, :, t].reshape(
            shards * rows, width
        )
    return block[...]


def quarter_scale(factor):
    n, tile = factor.shape[0], 128
    on = lax.broadcasted_iota(jnp.int32, (tile, tile), 0)
    on = on == lax.broadcasted_iota(jnp.int32, (tile, tile), 1)
    total = factor[:tile, :tile]
    for d in range(tile, n, tile):
        total = total + factor[d : d + tile, d : d + tile]
    return (0.25 * n) / jnp.sum(jnp.where(on, total, 0.0))


def update_kernel(gain, slots, count, pieces, xl, xr, *refs):
    ready, refs = refs[: 4 * slots], refs[4 * slots :]
    out, blocks, roots, factors, made, in_sem, out_sem = refs
    parts, shards, _, rows, width = made.shape
    n = parts * width
    roots_in = (xl, xr)

    def arrivals(t):
        copies = []
        for k in range(2):
            sources = (
                (ready[4 * t + 2 * k + 1], factors.at[t, k]),
                (roots_in[k].at[t], roots.at[t, k]),
            )
            for a, b in sources:
                copies.append(pltpu.make_async_copy(a, b, in_sem.at[t, len(copies)]))
        return copies

    def departure(h):
        span = pl.ds(h * parts // 2, parts // 2)
        return pltpu.make_async_copy(made.at[span], out.at[span], out_sem.at[h])

    def root(t, k, gram, copies):
        copies[2 * k].wait()
        factor = factors[t, k].astype(f32) + (gain / decay_rate) * gram
        scale = quarter_scale(factor)
        product = mul(ready[4 * t + 2 * k][...], factor.astype(bf16))
        copies[2 * k + 1].wait()
        return (1.25 * roots[t, k] - scale * product).astype(bf16)

    def work(ts):
        copies = {t: arrivals(t) for t in ts}
        for k in range(4):
            for t in ts:
                copies[t][k].start()
        g, part, side = {}, {}, {}
        for t in ts:
            g[t] = assembled(pieces, t, blocks.at[t])
        grams = {t: (mul_t(g[t], g[t]), t_mul(g[t], g[t])) for t in ts}
        for t in ts:
            side[t] = root(t, 0, grams[t][0], copies[t])
            part[t] = mul(side[t], g[t]).astype(bf16)
        for t in ts:
            side[t] = root(t, 1, grams[t][1], copies[t])
        for h in range(2):
            for t in ts:
                done = mul(part[t], side[t][:, h * n // 2 : (h + 1) * n // 2]).astype(bf16)
                for k in range(parts // 2):
                    made[h * parts // 2 + k, :, t] = done[
                        :, k * width : (k + 1) * width
                    ].reshape(shards, rows, width)
            departure(h).start()

    for live in range(slots + 1):

        @pl.when(count[0] == live)
        def _():
            for t in range(live, slots):
                made[:, :, t] = jnp.zeros_like(made[:, :, t])
            if live:
                work(range(live))
            else:
                departure(0).start()
                departure(1).start()

    departure(0).wait()
    departure(1).wait()


def update_pieces(gain, count, pieces, xl, xr, ready):
    slots = pieces.shape[2]
    n = xl.shape[1]
    inputs = []
    for sides in ready:
        for high, _, factor in sides:
            inputs += [vmem(high), hbm(factor)]
    return pl.pallas_call(
        functools.partial(update_kernel, gain, slots),
        out_shape=stored(*pieces.shape, dtype=bf16),
        in_specs=[scalars, whole] + [in_place] * 2 + [whole, in_place] * (2 * slots),
        out_specs=in_place,
        scratch_shapes=[
            pltpu.VMEM((slots, n, n), bf16),
            pltpu.VMEM((slots, 2, n, n), f32),
            pltpu.VMEM((slots, 2, n, n), bf16),
            pltpu.VMEM(pieces.shape, bf16),
            pltpu.SemaphoreType.DMA((slots, 4)),
            pltpu.SemaphoreType.DMA((2,)),
        ],
        compiler_params=params(36),
        name="update_pieces",
    )(count, vmem(pieces), hbm(xl), hbm(xr), *inputs)


def state_kernel(gain, slots, count, pieces, left, right, xl, xr, *refs):
    ready, refs = refs[: 4 * slots], refs[4 * slots :]
    outs, refs = refs[:4], refs[4:]
    block, fives, made, in_sem, out_sem = refs
    olds = (left, right, xl, xr)

    def arrivals(t):
        sources = [(a.at[t], made.at[t, k]) for k, a in enumerate(olds)]
        sources += [(a, fives.at[t, k]) for k, a in enumerate(ready[4 * t : 4 * t + 4])]
        return [
            pltpu.make_async_copy(a, b, in_sem.at[t, k]) for k, (a, b) in enumerate(sources)
        ]

    def departures(t):
        return [
            pltpu.make_async_copy(made.at[t, k], out.at[t], out_sem.at[t, k])
            for k, out in enumerate(outs)
        ]

    for t in range(slots):
        for copy in arrivals(t)[:4]:
            copy.start()

        @pl.when(t < count[0])
        def _():
            for copy in arrivals(t)[4:]:
                copy.start()

    for t in range(slots):
        for copy in arrivals(t)[:4]:
            copy.wait()

        @pl.when(t < count[0])
        def _():
            g = assembled(pieces, t, block)
            for copy in arrivals(t)[4:]:
                copy.wait()
            for k in range(2):
                gram = t_mul(g, g) if k else mul_t(g, g)
                made[t, k] = decay_rate * made[t, k] + gain * gram
                departures(t)[k].start()
                factor = made[t, k]
                product = mul3((fives[t, 2 * k], fives[t, 2 * k + 1]), halves(factor))
                made[t, 2 + k] = 1.25 * made[t, 2 + k] - quarter_scale(factor) * product
                departures(t)[2 + k].start()

        @pl.when(t >= count[0])
        def _():
            for copy in departures(t):
                copy.start()

    for t in range(slots):
        for copy in departures(t):
            copy.wait()


def new_state(gain, count, pieces, state, ready):
    slots, n, _ = state[0].shape
    inputs = [hbm(x) for sides in ready for made in sides for x in made[:2]]
    return pl.pallas_call(
        functools.partial(state_kernel, gain, slots),
        out_shape=(stored(slots, n, n),) * 4,
        in_specs=[scalars, whole] + [in_place] * (4 + len(inputs)),
        out_specs=(in_place,) * 4,
        scratch_shapes=[
            pltpu.VMEM((n, n), bf16),
            pltpu.VMEM((slots, 4, n, n), bf16),
            pltpu.VMEM((slots, 4, n, n), f32),
            pltpu.SemaphoreType.DMA((slots, 8)),
            pltpu.SemaphoreType.DMA((slots, 4)),
        ],
        compiler_params=params(36),
        cost_estimate=pl.CostEstimate(
            flops=slots * 8 * 2 * n**3,
            bytes_accessed=slots * 36 * n * n,
            transcendentals=0,
        ),
        name="new_state",
    )(count, vmem(pieces), *[hbm(x) for x in state], *inputs)


def body(
    gradients, owner_list, row_offset, col_offset, left_factor, right_factor, left_root, right_root
):
    replicas = lax.axis_size("dp")
    shards = lax.axis_size("shard")
    slots, n, _ = left_factor.shape
    _, row_blocks, rows, cols, _ = gradients.shape
    width = n // replicas
    gain = (1.0 - decay_rate) / n
    mine = gradients[0]

    def hop(x, step):
        return lax.ppermute(x, "dp", [(i, (i + step) % replicas) for i in range(replicas)])

    half = row_blocks // 2
    far = lax.rem(lax.axis_index("dp") + 2, replicas) * width
    far = lax.dynamic_slice_in_dim(mine, far, width, axis=3)
    far_low, far_high = far[:half], far[half:]
    far_low, far_high = hop(far_low, 1), hop(far_high, -1)
    near_high, near_low = windows(mine, width, ((half, 1), (0, 3)))

    entries = jnp.arange(owner_list.shape[0], dtype=jnp.int32)
    same = owner_list[None, :] == owner_list[:, None]
    earlier = jnp.sum(same & (entries[None, :] < entries[:, None]), axis=1)
    slot_of = owner_list * slots + earlier.astype(jnp.int32)
    block_of = row_offset // n * cols + col_offset // n
    table = jnp.sum(
        jnp.where(block_of[None, :] == entries[:, None], slot_of[None, :], 0), axis=1
    ).astype(jnp.int32)
    owner = lax.axis_index(("dp", "shard"))
    count = jnp.sum((owner_list == owner).astype(jnp.int32)).reshape(1)

    far_low, far_high = merged(mine, 0, 1, far_low), merged(mine, half, 3, far_high)
    far_low, near_high = lax.optimization_barrier((far_low, near_high))
    far_high, near_low = lax.optimization_barrier((far_high, near_low))
    far_low, far_high = hop(far_low, 1), hop(far_high, -1)
    near_high, near_low = hop(near_high, 1), hop(near_low, -1)
    (first,) = early(count, (0, left_root, left_factor))
    arrived = (near_high, near_low, far_low, far_high)
    arrived, first = lax.optimization_barrier((arrived, first))

    all_slots = replicas * shards * slots
    outgoing = gather_pieces(table, mine, arrived, all_slots)
    incoming = lax.all_to_all(outgoing, ("dp", "shard"), split_axis=0, concat_axis=0, tiled=True)
    sides = ((left_root, left_factor), (right_root, right_factor))
    rest = [(t, *side) for t in range(slots) for side in sides][1:]
    ready = [first, *early(count, *rest)]
    incoming, ready = lax.optimization_barrier((incoming, ready))
    ready = [ready[2 * t : 2 * t + 2] for t in range(slots)]
    pieces = incoming.reshape(replicas, shards, slots, rows, width)
    state = (left_factor, right_factor, left_root, right_root)
    outbound = update_pieces(gain, count, pieces, left_root, right_root, ready)
    returned = lax.all_to_all(
        outbound.reshape(all_slots, rows, width),
        ("dp", "shard"), split_axis=0, concat_axis=0, tiled=True,
    )
    new_left, new_right, new_xl, new_xr = new_state(gain, count, pieces, state, ready)
    update = place_pieces(table, returned, row_blocks, cols)
    return update, new_left, new_right, new_xl, new_xr


def solution(mesh):
    slots = P(("dp", "shard"), None, None)
    in_specs = (P("dp", None, "shard", None, None), P(), P(), P(), slots, slots, slots, slots)
    out_specs = (P(None, "shard", None, "dp"), slots, slots, slots, slots)
    return jax.shard_map(body, mesh=mesh, in_specs=in_specs, out_specs=out_specs, check_vma=False)
```

```python
import functools

import jax
import jax.numpy as jnp
from jax import lax
from jax.experimental import pallas as pl
from jax.experimental.pallas import tpu as pltpu
from jax.sharding import PartitionSpec as P

decay_rate = 0.9
f32 = jnp.float32
bf16 = jnp.bfloat16
MIB = 1 << 20


def params(mib):
    return pltpu.CompilerParams(vmem_limit_bytes=mib * MIB)


def halves(x):
    high = x.astype(bf16)
    return high, (x - high.astype(f32)).astype(bf16)


def mul(a, b):
    return jnp.dot(a, b, preferred_element_type=f32)


def mul_t(a, b):
    return lax.dot_general(a, b, (((1,), (1,)), ((), ())), preferred_element_type=f32)


def t_mul(a, b):
    return lax.dot_general(a, b, (((0,), (0,)), ((), ())), preferred_element_type=f32)


def mul3(a, b):
    return mul(a[0], b[0]) + (mul(a[0], b[1]) + mul(a[1], b[0]))


def vmem(x):
    return pltpu.with_memory_space_constraint(x, pltpu.VMEM)


def hbm(x):
    return pltpu.with_memory_space_constraint(x, pltpu.HBM)


def stored(*shape, dtype=f32):
    return pltpu.HBM(shape, dtype)


whole = pl.BlockSpec(memory_space=pltpu.VMEM)
scalars = pl.BlockSpec(memory_space=pltpu.SMEM)
in_place = pl.BlockSpec(memory_space=pl.ANY)


def column_at(hop, width):
    replicas = lax.axis_size("dp")
    z = lax.rem(lax.axis_index("dp").astype(jnp.int32) + hop, replicas)
    return pl.ds(pl.multiple_of(z * width, width), width)


def window_kernel(parts, mine, *refs):
    outs, sem = refs[:-1], refs[-1]
    copies = []
    for k, ((low, hop), out) in enumerate(zip(parts, outs)):
        half, width = out.shape[0], out.shape[-1]
        source = mine.at[low : low + half, :, :, column_at(hop, width)]
        copies.append(pltpu.make_async_copy(source, out, sem.at[k]))
    for copy in copies:
        copy.start()
    for copy in copies:
        copy.wait()


def windows(mine, width, parts):
    row_blocks, rows, cols, _ = mine.shape
    return pl.pallas_call(
        functools.partial(window_kernel, parts),
        out_shape=(pltpu.VMEM((row_blocks // 2, rows, cols, width), bf16),) * len(parts),
        in_specs=[in_place],
        out_specs=(whole,) * len(parts),
        scratch_shapes=[pltpu.SemaphoreType.DMA((len(parts),))],
        compiler_params=params(4),
        name="windows",
    )(hbm(mine))


def merge_kernel(own, came, out):
    for b in range(out.shape[0]):
        out[b] = (own[b].astype(f32) + came[b].astype(f32)).astype(bf16)


def merged(own, came):
    return pl.pallas_call(
        merge_kernel,
        out_shape=pltpu.VMEM(came.shape, bf16),
        in_specs=[whole] * 2,
        out_specs=whole,
        compiler_params=params(4),
        name="merge_far_part",
    )(vmem(own), vmem(came))


def gather_kernel(table, *refs):
    parts, (out, held) = refs[:6], refs[6:]
    half, rows, cols, width = parts[0].shape
    out[...] = jnp.zeros_like(out)
    for b in range(2 * half):
        own, near, far = parts[b // half * 3 : b // half * 3 + 3]
        total = own[b % half].astype(f32) + near[b % half].astype(f32)
        total = total + far[b % half].astype(f32)
        held[b] = total.reshape(rows * cols, width)
        for c in range(cols):
            piece = held[b, pl.ds(c, rows, stride=cols), :]
            out[table[b * cols + c]] = piece.astype(out.dtype)


def gather_pieces(table, parts, slots):
    half, rows, cols, width = parts[0].shape
    return pl.pallas_call(
        gather_kernel,
        out_shape=jax.ShapeDtypeStruct((slots, rows, width), bf16),
        in_specs=[scalars] + [whole] * len(parts),
        out_specs=whole,
        scratch_shapes=[pltpu.VMEM((2 * half, rows * cols, width), f32)],
        compiler_params=params(6),
        name="sum_and_gather",
    )(table, *[vmem(x) for x in parts])


def place_kernel(per_step, rows, cols, table, arrived, out, held):
    step = pl.program_id(0)
    for b in range(per_step):
        for c in range(cols):
            slot = table[(step * per_step + b) * cols + c]
            held[b, pl.ds(c, rows, stride=cols), :] = arrived[slot].astype(f32)
        out[b] = held[b].reshape(rows, cols, held.shape[-1]).astype(out.dtype)


def place_pieces(table, arrived, row_blocks, cols):
    slots, rows, width = arrived.shape
    per_step = 4
    return pl.pallas_call(
        functools.partial(place_kernel, per_step, rows, cols),
        out_shape=jax.ShapeDtypeStruct((row_blocks, rows, cols, width), bf16),
        grid=(row_blocks // per_step,),
        in_specs=[scalars, whole],
        out_specs=pl.BlockSpec((per_step, rows, cols, width), lambda i: (i, 0, 0, 0)),
        scratch_shapes=[pltpu.VMEM((per_step, rows * cols, width), f32)],
        compiler_params=params(4),
        name="place_pieces",
    )(table, vmem(arrived))


def early_kernel(slots, count, *refs):
    items = len(slots)
    ins, outs = refs[: 2 * items], refs[2 * items : 5 * items]
    roots, factors, lows, short, in_sem, out_sem = refs[5 * items :]

    def arrivals(k):
        return [
            pltpu.make_async_copy(ins[2 * k + i].at[slots[k]], held.at[k], in_sem.at[k, i])
            for i, held in enumerate((roots, factors))
        ]

    def departures(k):
        return [
            pltpu.make_async_copy(held.at[k], outs[3 * k + 1 + i], out_sem.at[k, i])
            for i, held in enumerate((lows, short))
        ]

    for i in range(2):
        for k in range(items):

            @pl.when(slots[k] < count[0])
            def _():
                arrivals(k)[i].start()

    for k in range(items):

        @pl.when(slots[k] < count[0])
        def _():
            (root_in, factor_in), going = arrivals(k), departures(k)
            root_in.wait()
            x = halves(roots[k])
            square = halves(mul3(x, x))
            fourth = halves(mul3(square, square))
            factor_in.wait()
            short[k] = factors[k].astype(bf16)
            going[1].start()
            outs[3 * k][...], lows[k] = halves(mul3(x, fourth))
            going[0].start()

    for k in range(items):

        @pl.when(slots[k] < count[0])
        def _():
            for copy in departures(k):
                copy.wait()


def early(count, *items):
    n = items[0][1].shape[1]
    many = len(items)
    made = pl.pallas_call(
        functools.partial(early_kernel, [t for t, _, _ in items]),
        out_shape=(
            pltpu.VMEM((n, n), bf16),
            stored(n, n, dtype=bf16),
            stored(n, n, dtype=bf16),
        )
        * many,
        in_specs=[scalars] + [in_place] * (2 * many),
        out_specs=(whole, in_place, in_place) * many,
        scratch_shapes=[
            pltpu.VMEM((many, n, n), f32),
            pltpu.VMEM((many, n, n), f32),
            pltpu.VMEM((many, n, n), bf16),
            pltpu.VMEM((many, n, n), bf16),
            pltpu.SemaphoreType.DMA((many, 2)),
            pltpu.SemaphoreType.DMA((many, 2)),
        ],
        compiler_params=params(24),
        cost_estimate=pl.CostEstimate(
            flops=many * 9 * 2 * n**3,
            bytes_accessed=many * 12 * n * n,
            transcendentals=0,
        ),
        name="early_products",
    )(count, *[hbm(x) for _, *pair in items for x in pair])
    return [made[3 * k : 3 * k + 3] for k in range(many)]


def assembled(pieces, t, block):
    parts, shards, _, rows, width = pieces.shape
    for z in range(parts):
        block[:, z * width : (z + 1) * width] = pieces[z, :, t].reshape(
            shards * rows, width
        )
    return block[...]


def quarter_scale(factor):
    n, tile = factor.shape[0], 128
    on = lax.broadcasted_iota(jnp.int32, (tile, tile), 0)
    on = on == lax.broadcasted_iota(jnp.int32, (tile, tile), 1)
    total = factor[:tile, :tile]
    for d in range(tile, n, tile):
        total = total + factor[d : d + tile, d : d + tile]
    return (0.25 * n) / jnp.sum(jnp.where(on, total, 0.0))


def update_kernel(gain, slots, count, pieces, xl, xr, *refs):
    ready, refs = refs[: 4 * slots], refs[4 * slots :]
    out, blocks, roots, factors, made, in_sem, out_sem = refs
    parts, shards, _, rows, width = made.shape
    n = parts * width
    roots_in = (xl, xr)

    def arrivals(t):
        copies = []
        for k in range(2):
            sources = (
                (ready[4 * t + 2 * k + 1], factors.at[t, k]),
                (roots_in[k].at[t], roots.at[t, k]),
            )
            for a, b in sources:
                copies.append(pltpu.make_async_copy(a, b, in_sem.at[t, len(copies)]))
        return copies

    def departure(h):
        span = pl.ds(h * parts // 2, parts // 2)
        return pltpu.make_async_copy(made.at[span], out.at[span], out_sem.at[h])

    def root(t, k, gram, copies):
        copies[2 * k].wait()
        factor = factors[t, k].astype(f32) + (gain / decay_rate) * gram
        scale = quarter_scale(factor)
        product = mul(ready[4 * t + 2 * k][...], factor.astype(bf16))
        copies[2 * k + 1].wait()
        return (1.25 * roots[t, k] - scale * product).astype(bf16)

    def work(ts):
        copies = {t: arrivals(t) for t in ts}
        for k in range(4):
            for t in ts:
                copies[t][k].start()
        g, part, side = {}, {}, {}
        for t in ts:
            g[t] = assembled(pieces, t, blocks.at[t])
        grams = {t: (mul_t(g[t], g[t]), t_mul(g[t], g[t])) for t in ts}
        for t in ts:
            side[t] = root(t, 0, grams[t][0], copies[t])
            part[t] = mul(side[t], g[t]).astype(bf16)
        for t in ts:
            side[t] = root(t, 1, grams[t][1], copies[t])
        for h in range(2):
            for t in ts:
                done = mul(part[t], side[t][:, h * n // 2 : (h + 1) * n // 2]).astype(bf16)
                for k in range(parts // 2):
                    made[h * parts // 2 + k, :, t] = done[
                        :, k * width : (k + 1) * width
                    ].reshape(shards, rows, width)
            departure(h).start()

    for live in range(slots + 1):

        @pl.when(count[0] == live)
        def _():
            for t in range(live, slots):
                made[:, :, t] = jnp.zeros_like(made[:, :, t])
            if live:
                work(range(live))
            else:
                departure(0).start()
                departure(1).start()

    departure(0).wait()
    departure(1).wait()


def update_pieces(gain, count, pieces, xl, xr, ready):
    slots = pieces.shape[2]
    n = xl.shape[1]
    inputs = []
    for sides in ready:
        for high, _, factor in sides:
            inputs += [vmem(high), hbm(factor)]
    return pl.pallas_call(
        functools.partial(update_kernel, gain, slots),
        out_shape=stored(*pieces.shape, dtype=bf16),
        in_specs=[scalars, whole] + [in_place] * 2 + [whole, in_place] * (2 * slots),
        out_specs=in_place,
        scratch_shapes=[
            pltpu.VMEM((slots, n, n), bf16),
            pltpu.VMEM((slots, 2, n, n), f32),
            pltpu.VMEM((slots, 2, n, n), bf16),
            pltpu.VMEM(pieces.shape, bf16),
            pltpu.SemaphoreType.DMA((slots, 4)),
            pltpu.SemaphoreType.DMA((2,)),
        ],
        compiler_params=params(36),
        name="update_pieces",
    )(count, vmem(pieces), hbm(xl), hbm(xr), *inputs)


def state_kernel(gain, slots, count, pieces, left, right, xl, xr, *refs):
    ready, refs = refs[: 4 * slots], refs[4 * slots :]
    outs, refs = refs[:4], refs[4:]
    block, fives, made, in_sem, out_sem = refs
    olds = (left, right, xl, xr)

    def arrivals(t):
        sources = [(a.at[t], made.at[t, k]) for k, a in enumerate(olds)]
        sources += [(a, fives.at[t, k]) for k, a in enumerate(ready[4 * t : 4 * t + 4])]
        return [
            pltpu.make_async_copy(a, b, in_sem.at[t, k]) for k, (a, b) in enumerate(sources)
        ]

    def departures(t):
        return [
            pltpu.make_async_copy(made.at[t, k], out.at[t], out_sem.at[t, k])
            for k, out in enumerate(outs)
        ]

    for t in range(slots):
        for copy in arrivals(t)[:4]:
            copy.start()

        @pl.when(t < count[0])
        def _():
            for copy in arrivals(t)[4:]:
                copy.start()

    for t in range(slots):
        for copy in arrivals(t)[:4]:
            copy.wait()

        @pl.when(t < count[0])
        def _():
            g = assembled(pieces, t, block)
            for copy in arrivals(t)[4:]:
                copy.wait()
            for k in range(2):
                gram = t_mul(g, g) if k else mul_t(g, g)
                made[t, k] = decay_rate * made[t, k] + gain * gram
                departures(t)[k].start()
                factor = made[t, k]
                product = mul3((fives[t, 2 * k], fives[t, 2 * k + 1]), halves(factor))
                made[t, 2 + k] = 1.25 * made[t, 2 + k] - quarter_scale(factor) * product
                departures(t)[2 + k].start()

        @pl.when(t >= count[0])
        def _():
            for copy in departures(t):
                copy.start()

    for t in range(slots):
        for copy in departures(t):
            copy.wait()


def new_state(gain, count, pieces, state, ready):
    slots, n, _ = state[0].shape
    inputs = [hbm(x) for sides in ready for made in sides for x in made[:2]]
    return pl.pallas_call(
        functools.partial(state_kernel, gain, slots),
        out_shape=(stored(slots, n, n),) * 4,
        in_specs=[scalars, whole] + [in_place] * (4 + len(inputs)),
        out_specs=(in_place,) * 4,
        scratch_shapes=[
            pltpu.VMEM((n, n), bf16),
            pltpu.VMEM((slots, 4, n, n), bf16),
            pltpu.VMEM((slots, 4, n, n), f32),
            pltpu.SemaphoreType.DMA((slots, 8)),
            pltpu.SemaphoreType.DMA((slots, 4)),
        ],
        compiler_params=params(36),
        cost_estimate=pl.CostEstimate(
            flops=slots * 8 * 2 * n**3,
            bytes_accessed=slots * 36 * n * n,
            transcendentals=0,
        ),
        name="new_state",
    )(count, vmem(pieces), *[hbm(x) for x in state], *inputs)


def body(
    gradients, owner_list, row_offset, col_offset, left_factor, right_factor, left_root, right_root
):
    replicas = lax.axis_size("dp")
    shards = lax.axis_size("shard")
    slots, n, _ = left_factor.shape
    _, row_blocks, rows, cols, _ = gradients.shape
    width = n // replicas
    gain = (1.0 - decay_rate) / n
    mine = gradients[0]

    def hop(x, step):
        return lax.ppermute(x, "dp", [(i, (i + step) % replicas) for i in range(replicas)])

    half = row_blocks // 2
    far = lax.rem(lax.axis_index("dp") + 2, replicas) * width
    far = lax.dynamic_slice_in_dim(mine, far, width, axis=3)
    far_low, far_high = far[:half], far[half:]
    far_low, far_high = hop(far_low, 1), hop(far_high, -1)
    near_high, near_low, own_low, own_high, last_low, last_high = windows(
        mine, width, ((half, 1), (0, 3), (0, 1), (half, 3), (0, 0), (half, 0))
    )
    near_high, near_low = hop(near_high, 1), hop(near_low, -1)

    entries = jnp.arange(owner_list.shape[0], dtype=jnp.int32)
    same = owner_list[None, :] == owner_list[:, None]
    earlier = jnp.sum(same & (entries[None, :] < entries[:, None]), axis=1)
    slot_of = owner_list * slots + earlier.astype(jnp.int32)
    block_of = row_offset // n * cols + col_offset // n
    table = jnp.sum(
        jnp.where(block_of[None, :] == entries[:, None], slot_of[None, :], 0), axis=1
    ).astype(jnp.int32)
    owner = lax.axis_index(("dp", "shard"))
    count = jnp.sum((owner_list == owner).astype(jnp.int32)).reshape(1)

    far_low = hop(merged(own_low, far_low), 1)
    far_high = hop(merged(own_high, far_high), -1)
    (first,) = early(count, (0, left_root, left_factor))
    arrived = (last_low, near_low, far_low, last_high, near_high, far_high)
    arrived, first = lax.optimization_barrier((arrived, first))

    all_slots = replicas * shards * slots
    outgoing = gather_pieces(table, arrived, all_slots)
    incoming = lax.all_to_all(outgoing, ("dp", "shard"), split_axis=0, concat_axis=0, tiled=True)
    sides = ((left_root, left_factor), (right_root, right_factor))
    rest = [(t, *side) for t in range(slots) for side in sides][1:]
    ready = [first, *early(count, *rest)]
    incoming, ready = lax.optimization_barrier((incoming, ready))
    ready = [ready[2 * t : 2 * t + 2] for t in range(slots)]
    pieces = incoming.reshape(replicas, shards, slots, rows, width)
    state = (left_factor, right_factor, left_root, right_root)
    outbound = update_pieces(gain, count, pieces, left_root, right_root, ready)
    returned = lax.all_to_all(
        outbound.reshape(all_slots, rows, width),
        ("dp", "shard"), split_axis=0, concat_axis=0, tiled=True,
    )
    new_left, new_right, new_xl, new_xr = new_state(gain, count, pieces, state, ready)
    update = place_pieces(table, returned, row_blocks, cols)
    return update, new_left, new_right, new_xl, new_xr


def solution(mesh):
    slots = P(("dp", "shard"), None, None)
    in_specs = (P("dp", None, "shard", None, None), P(), P(), P(), slots, slots, slots, slots)
    out_specs = (P(None, "shard", None, "dp"), slots, slots, slots, slots)
    return jax.shard_map(body, mesh=mesh, in_specs=in_specs, out_specs=out_specs, check_vma=False)
```

```python
import functools

import jax
import jax.numpy as jnp
from jax import lax
from jax.experimental import pallas as pl
from jax.experimental.pallas import tpu as pltpu
from jax.sharding import PartitionSpec as P

decay_rate = 0.9
f32 = jnp.float32
bf16 = jnp.bfloat16
MIB = 1 << 20


def params(mib):
    return pltpu.CompilerParams(vmem_limit_bytes=mib * MIB)


def halves(x):
    high = x.astype(bf16)
    return high, (x - high.astype(f32)).astype(bf16)


def mul(a, b):
    return jnp.dot(a, b, preferred_element_type=f32)


def mul_t(a, b):
    return lax.dot_general(a, b, (((1,), (1,)), ((), ())), preferred_element_type=f32)


def t_mul(a, b):
    return lax.dot_general(a, b, (((0,), (0,)), ((), ())), preferred_element_type=f32)


def mul3(a, b):
    return mul(a[0], b[0]) + (mul(a[0], b[1]) + mul(a[1], b[0]))


def vmem(x):
    return pltpu.with_memory_space_constraint(x, pltpu.VMEM)


def hbm(x):
    return pltpu.with_memory_space_constraint(x, pltpu.HBM)


def stored(*shape, dtype=f32):
    return pltpu.HBM(shape, dtype)


whole = pl.BlockSpec(memory_space=pltpu.VMEM)
scalars = pl.BlockSpec(memory_space=pltpu.SMEM)
in_place = pl.BlockSpec(memory_space=pl.ANY)


def direction(index):
    return 1 - 2 * lax.rem(index, 2)


def column_at(hop, width):
    replicas = lax.axis_size("dp")
    way = direction(lax.axis_index("shard").astype(jnp.int32))
    z = lax.rem(lax.axis_index("dp").astype(jnp.int32) + way * hop + replicas, replicas)
    return pl.ds(pl.multiple_of(z * width, width), width)


def window_kernel(hops, mine, *refs):
    outs, sem = refs[:-1], refs[-1]
    copies = []
    for k, (hop, out) in enumerate(zip(hops, outs)):
        source = mine.at[:, :, :, column_at(hop, out.shape[-1])]
        copies.append(pltpu.make_async_copy(source, out, sem.at[k]))
    for copy in copies:
        copy.start()
    for copy in copies:
        copy.wait()


def windows(mine, width, hops):
    row_blocks, rows, cols, _ = mine.shape
    return pl.pallas_call(
        functools.partial(window_kernel, hops),
        out_shape=(pltpu.VMEM((row_blocks, rows, cols, width), bf16),) * len(hops),
        in_specs=[in_place],
        out_specs=(whole,) * len(hops),
        scratch_shapes=[pltpu.SemaphoreType.DMA((len(hops),))],
        compiler_params=params(4),
        name="windows",
    )(hbm(mine))


def merge_kernel(own, came, out):
    for b in range(out.shape[0]):
        out[b] = (own[b].astype(f32) + came[b].astype(f32)).astype(bf16)


def merged(own, came):
    return pl.pallas_call(
        merge_kernel,
        out_shape=pltpu.VMEM(came.shape, bf16),
        in_specs=[whole] * 2,
        out_specs=whole,
        compiler_params=params(4),
        name="merge_far_part",
    )(vmem(own), vmem(came))


def gather_kernel(table, own, near, far, out, held):
    row_blocks, rows, cols, width = own.shape
    out[...] = jnp.zeros_like(out)
    for b in range(row_blocks):
        total = own[b].astype(f32) + near[b].astype(f32) + far[b].astype(f32)
        held[b] = total.reshape(rows * cols, width)
        for c in range(cols):
            piece = held[b, pl.ds(c, rows, stride=cols), :]
            out[table[b * cols + c]] = piece.astype(out.dtype)


def gather_pieces(table, parts, slots):
    row_blocks, rows, cols, width = parts[0].shape
    return pl.pallas_call(
        gather_kernel,
        out_shape=jax.ShapeDtypeStruct((slots, rows, width), bf16),
        in_specs=[scalars] + [whole] * len(parts),
        out_specs=whole,
        scratch_shapes=[pltpu.VMEM((row_blocks, rows * cols, width), f32)],
        compiler_params=params(6),
        name="sum_and_gather",
    )(table, *[vmem(x) for x in parts])


def place_kernel(per_step, rows, cols, table, arrived, out, held):
    step = pl.program_id(0)
    for b in range(per_step):
        for c in range(cols):
            slot = table[(step * per_step + b) * cols + c]
            held[b, pl.ds(c, rows, stride=cols), :] = arrived[slot].astype(f32)
        out[b] = held[b].reshape(rows, cols, held.shape[-1]).astype(out.dtype)


def place_pieces(table, arrived, row_blocks, cols):
    slots, rows, width = arrived.shape
    per_step = 4
    return pl.pallas_call(
        functools.partial(place_kernel, per_step, rows, cols),
        out_shape=jax.ShapeDtypeStruct((row_blocks, rows, cols, width), bf16),
        grid=(row_blocks // per_step,),
        in_specs=[scalars, whole],
        out_specs=pl.BlockSpec((per_step, rows, cols, width), lambda i: (i, 0, 0, 0)),
        scratch_shapes=[pltpu.VMEM((per_step, rows * cols, width), f32)],
        compiler_params=params(4),
        name="place_pieces",
    )(table, vmem(arrived))


def early_kernel(slots, count, *refs):
    items = len(slots)
    ins, outs = refs[: 2 * items], refs[2 * items : 5 * items]
    roots, factors, lows, short, in_sem, out_sem = refs[5 * items :]

    def arrivals(k):
        return [
            pltpu.make_async_copy(ins[2 * k + i].at[slots[k]], held.at[k], in_sem.at[k, i])
            for i, held in enumerate((roots, factors))
        ]

    def departures(k):
        return [
            pltpu.make_async_copy(held.at[k], outs[3 * k + 1 + i], out_sem.at[k, i])
            for i, held in enumerate((lows, short))
        ]

    for i in range(2):
        for k in range(items):

            @pl.when(slots[k] < count[0])
            def _():
                arrivals(k)[i].start()

    for k in range(items):

        @pl.when(slots[k] < count[0])
        def _():
            (root_in, factor_in), going = arrivals(k), departures(k)
            root_in.wait()
            x = halves(roots[k])
            square = halves(mul3(x, x))
            fourth = halves(mul3(square, square))
            factor_in.wait()
            short[k] = factors[k].astype(bf16)
            going[1].start()
            outs[3 * k][...], lows[k] = halves(mul3(x, fourth))
            going[0].start()

    for k in range(items):

        @pl.when(slots[k] < count[0])
        def _():
            for copy in departures(k):
                copy.wait()


def early(count, *items):
    n = items[0][1].shape[1]
    many = len(items)
    made = pl.pallas_call(
        functools.partial(early_kernel, [t for t, _, _ in items]),
        out_shape=(
            pltpu.VMEM((n, n), bf16),
            stored(n, n, dtype=bf16),
            stored(n, n, dtype=bf16),
        )
        * many,
        in_specs=[scalars] + [in_place] * (2 * many),
        out_specs=(whole, in_place, in_place) * many,
        scratch_shapes=[
            pltpu.VMEM((many, n, n), f32),
            pltpu.VMEM((many, n, n), f32),
            pltpu.VMEM((many, n, n), bf16),
            pltpu.VMEM((many, n, n), bf16),
            pltpu.SemaphoreType.DMA((many, 2)),
            pltpu.SemaphoreType.DMA((many, 2)),
        ],
        compiler_params=params(24),
        cost_estimate=pl.CostEstimate(
            flops=many * 9 * 2 * n**3,
            bytes_accessed=many * 12 * n * n,
            transcendentals=0,
        ),
        name="early_products",
    )(count, *[hbm(x) for _, *pair in items for x in pair])
    return [made[3 * k : 3 * k + 3] for k in range(many)]


def assembled(pieces, t, block):
    parts, shards, _, rows, width = pieces.shape
    for z in range(parts):
        block[:, z * width : (z + 1) * width] = pieces[z, :, t].reshape(
            shards * rows, width
        )
    return block[...]


def quarter_scale(factor):
    n, tile = factor.shape[0], 128
    on = lax.broadcasted_iota(jnp.int32, (tile, tile), 0)
    on = on == lax.broadcasted_iota(jnp.int32, (tile, tile), 1)
    total = factor[:tile, :tile]
    for d in range(tile, n, tile):
        total = total + factor[d : d + tile, d : d + tile]
    return (0.25 * n) / jnp.sum(jnp.where(on, total, 0.0))


def update_kernel(gain, slots, count, pieces, xl, xr, *refs):
    ready, refs = refs[: 4 * slots], refs[4 * slots :]
    out, blocks, roots, factors, made, in_sem, out_sem = refs
    parts, shards, _, rows, width = made.shape
    n = parts * width
    roots_in = (xl, xr)

    def arrivals(t):
        copies = []
        for k in range(2):
            sources = (
                (ready[4 * t + 2 * k + 1], factors.at[t, k]),
                (roots_in[k].at[t], roots.at[t, k]),
            )
            for a, b in sources:
                copies.append(pltpu.make_async_copy(a, b, in_sem.at[t, len(copies)]))
        return copies

    def departure(h):
        span = pl.ds(h * parts // 2, parts // 2)
        return pltpu.make_async_copy(made.at[span], out.at[span], out_sem.at[h])

    def root(t, k, gram, copies):
        copies[2 * k].wait()
        factor = factors[t, k].astype(f32) + (gain / decay_rate) * gram
        scale = quarter_scale(factor)
        product = mul(ready[4 * t + 2 * k][...], factor.astype(bf16))
        copies[2 * k + 1].wait()
        return (1.25 * roots[t, k] - scale * product).astype(bf16)

    def work(ts):
        copies = {t: arrivals(t) for t in ts}
        for k in range(4):
            for t in ts:
                copies[t][k].start()
        g, part, side = {}, {}, {}
        for t in ts:
            g[t] = assembled(pieces, t, blocks.at[t])
        grams = {t: (mul_t(g[t], g[t]), t_mul(g[t], g[t])) for t in ts}
        for t in ts:
            side[t] = root(t, 0, grams[t][0], copies[t])
            part[t] = mul(side[t], g[t]).astype(bf16)
        for t in ts:
            side[t] = root(t, 1, grams[t][1], copies[t])
        for h in range(2):
            for t in ts:
                done = mul(part[t], side[t][:, h * n // 2 : (h + 1) * n // 2]).astype(bf16)
                for k in range(parts // 2):
                    made[h * parts // 2 + k, :, t] = done[
                        :, k * width : (k + 1) * width
                    ].reshape(shards, rows, width)
            departure(h).start()

    for live in range(slots + 1):

        @pl.when(count[0] == live)
        def _():
            for t in range(live, slots):
                made[:, :, t] = jnp.zeros_like(made[:, :, t])
            if live:
                work(range(live))
            else:
                departure(0).start()
                departure(1).start()

    departure(0).wait()
    departure(1).wait()


def update_pieces(gain, count, pieces, xl, xr, ready):
    slots = pieces.shape[2]
    n = xl.shape[1]
    inputs = []
    for sides in ready:
        for high, _, factor in sides:
            inputs += [vmem(high), hbm(factor)]
    return pl.pallas_call(
        functools.partial(update_kernel, gain, slots),
        out_shape=stored(*pieces.shape, dtype=bf16),
        in_specs=[scalars, whole] + [in_place] * 2 + [whole, in_place] * (2 * slots),
        out_specs=in_place,
        scratch_shapes=[
            pltpu.VMEM((slots, n, n), bf16),
            pltpu.VMEM((slots, 2, n, n), f32),
            pltpu.VMEM((slots, 2, n, n), bf16),
            pltpu.VMEM(pieces.shape, bf16),
            pltpu.SemaphoreType.DMA((slots, 4)),
            pltpu.SemaphoreType.DMA((2,)),
        ],
        compiler_params=params(36),
        name="update_pieces",
    )(count, vmem(pieces), hbm(xl), hbm(xr), *inputs)


def state_kernel(gain, slots, count, pieces, left, right, xl, xr, *refs):
    ready, refs = refs[: 4 * slots], refs[4 * slots :]
    outs, refs = refs[:4], refs[4:]
    block, fives, made, in_sem, out_sem = refs
    olds = (left, right, xl, xr)

    def arrivals(t):
        sources = [(a.at[t], made.at[t, k]) for k, a in enumerate(olds)]
        sources += [(a, fives.at[t, k]) for k, a in enumerate(ready[4 * t : 4 * t + 4])]
        return [
            pltpu.make_async_copy(a, b, in_sem.at[t, k]) for k, (a, b) in enumerate(sources)
        ]

    def departures(t):
        return [
            pltpu.make_async_copy(made.at[t, k], out.at[t], out_sem.at[t, k])
            for k, out in enumerate(outs)
        ]

    for t in range(slots):
        for copy in arrivals(t)[:4]:
            copy.start()

        @pl.when(t < count[0])
        def _():
            for copy in arrivals(t)[4:]:
                copy.start()

    for t in range(slots):
        for copy in arrivals(t)[:4]:
            copy.wait()

        @pl.when(t < count[0])
        def _():
            g = assembled(pieces, t, block)
            for copy in arrivals(t)[4:]:
                copy.wait()
            for k in range(2):
                gram = t_mul(g, g) if k else mul_t(g, g)
                made[t, k] = decay_rate * made[t, k] + gain * gram
                departures(t)[k].start()
                factor = made[t, k]
                product = mul3((fives[t, 2 * k], fives[t, 2 * k + 1]), halves(factor))
                made[t, 2 + k] = 1.25 * made[t, 2 + k] - quarter_scale(factor) * product
                departures(t)[2 + k].start()

        @pl.when(t >= count[0])
        def _():
            for copy in departures(t):
                copy.start()

    for t in range(slots):
        for copy in departures(t):
            copy.wait()


def new_state(gain, count, pieces, state, ready):
    slots, n, _ = state[0].shape
    inputs = [hbm(x) for sides in ready for made in sides for x in made[:2]]
    return pl.pallas_call(
        functools.partial(state_kernel, gain, slots),
        out_shape=(stored(slots, n, n),) * 4,
        in_specs=[scalars, whole] + [in_place] * (4 + len(inputs)),
        out_specs=(in_place,) * 4,
        scratch_shapes=[
            pltpu.VMEM((n, n), bf16),
            pltpu.VMEM((slots, 4, n, n), bf16),
            pltpu.VMEM((slots, 4, n, n), f32),
            pltpu.SemaphoreType.DMA((slots, 8)),
            pltpu.SemaphoreType.DMA((slots, 4)),
        ],
        compiler_params=params(36),
        cost_estimate=pl.CostEstimate(
            flops=slots * 8 * 2 * n**3,
            bytes_accessed=slots * 36 * n * n,
            transcendentals=0,
        ),
        name="new_state",
    )(count, vmem(pieces), *[hbm(x) for x in state], *inputs)


def body(
    gradients, owner_list, row_offset, col_offset, left_factor, right_factor, left_root, right_root
):
    replicas = lax.axis_size("dp")
    shards = lax.axis_size("shard")
    slots, n, _ = left_factor.shape
    _, row_blocks, rows, cols, _ = gradients.shape
    width = n // replicas
    gain = (1.0 - decay_rate) / n
    mine = gradients[0]

    def hop(x, way):
        pairs = []
        for z in range(replicas):
            for shard in range(shards):
                to = (z + way * direction_of[shard % 2]) % replicas
                pairs.append((z * shards + shard, to * shards + shard))
        return lax.ppermute(x, ("dp", "shard"), pairs)

    direction_of = (1, -1)
    column = lax.rem(lax.axis_index("dp") + replicas // 2, replicas) * width
    far = hop(lax.dynamic_slice_in_dim(mine, column, width, axis=3), 1)
    near, ahead, own = windows(mine, width, (-1, 1, 0))
    near = hop(near, -1)

    entries = jnp.arange(owner_list.shape[0], dtype=jnp.int32)
    same = owner_list[None, :] == owner_list[:, None]
    earlier = jnp.sum(same & (entries[None, :] < entries[:, None]), axis=1)
    slot_of = owner_list * slots + earlier.astype(jnp.int32)
    block_of = row_offset // n * cols + col_offset // n
    table = jnp.sum(
        jnp.where(block_of[None, :] == entries[:, None], slot_of[None, :], 0), axis=1
    ).astype(jnp.int32)
    owner = lax.axis_index(("dp", "shard"))
    count = jnp.sum((owner_list == owner).astype(jnp.int32)).reshape(1)

    far = hop(merged(ahead, far), 1)
    (first,) = early(count, (0, left_root, left_factor))
    arrived, first = lax.optimization_barrier(((own, near, far), first))

    all_slots = replicas * shards * slots
    outgoing = gather_pieces(table, arrived, all_slots)
    incoming = lax.all_to_all(outgoing, ("dp", "shard"), split_axis=0, concat_axis=0, tiled=True)
    sides = ((left_root, left_factor), (right_root, right_factor))
    rest = [(t, *side) for t in range(slots) for side in sides][1:]
    ready = [first, *early(count, *rest)]
    incoming, ready = lax.optimization_barrier((incoming, ready))
    ready = [ready[2 * t : 2 * t + 2] for t in range(slots)]
    pieces = incoming.reshape(replicas, shards, slots, rows, width)
    state = (left_factor, right_factor, left_root, right_root)
    outbound = update_pieces(gain, count, pieces, left_root, right_root, ready)
    returned = lax.all_to_all(
        outbound.reshape(all_slots, rows, width),
        ("dp", "shard"), split_axis=0, concat_axis=0, tiled=True,
    )
    new_left, new_right, new_xl, new_xr = new_state(gain, count, pieces, state, ready)
    update = place_pieces(table, returned, row_blocks, cols)
    return update, new_left, new_right, new_xl, new_xr


def solution(mesh):
    slots = P(("dp", "shard"), None, None)
    in_specs = (P("dp", None, "shard", None, None), P(), P(), P(), slots, slots, slots, slots)
    out_specs = (P(None, "shard", None, "dp"), slots, slots, slots, slots)
    return jax.shard_map(body, mesh=mesh, in_specs=in_specs, out_specs=out_specs, check_vma=False)
```

```python
import functools

import jax
import jax.numpy as jnp
from jax import lax
from jax.experimental import pallas as pl
from jax.experimental.pallas import tpu as pltpu
from jax.sharding import PartitionSpec as P

decay_rate = 0.9
f32 = jnp.float32
bf16 = jnp.bfloat16
MIB = 1 << 20


def params(mib):
    return pltpu.CompilerParams(vmem_limit_bytes=mib * MIB)


def halves(x):
    high = x.astype(bf16)
    return high, (x - high.astype(f32)).astype(bf16)


def mul(a, b):
    return jnp.dot(a, b, preferred_element_type=f32)


def mul_t(a, b):
    return lax.dot_general(a, b, (((1,), (1,)), ((), ())), preferred_element_type=f32)


def t_mul(a, b):
    return lax.dot_general(a, b, (((0,), (0,)), ((), ())), preferred_element_type=f32)


def mul3(a, b):
    return mul(a[0], b[0]) + (mul(a[0], b[1]) + mul(a[1], b[0]))


def vmem(x):
    return pltpu.with_memory_space_constraint(x, pltpu.VMEM)


def hbm(x):
    return pltpu.with_memory_space_constraint(x, pltpu.HBM)


def stored(*shape, dtype=f32):
    return pltpu.HBM(shape, dtype)


whole = pl.BlockSpec(memory_space=pltpu.VMEM)
scalars = pl.BlockSpec(memory_space=pltpu.SMEM)
in_place = pl.BlockSpec(memory_space=pl.ANY)


def column_at(hop, width):
    replicas = lax.axis_size("dp")
    z = lax.rem(lax.axis_index("dp").astype(jnp.int32) + hop, replicas)
    return pl.ds(pl.multiple_of(z * width, width), width)


def window_kernel(parts, mine, *refs):
    outs, sem = refs[:-1], refs[-1]
    copies = []
    for k, ((low, hop), out) in enumerate(zip(parts, outs)):
        half, width = out.shape[0], out.shape[-1]
        source = mine.at[low : low + half, :, :, column_at(hop, width)]
        copies.append(pltpu.make_async_copy(source, out, sem.at[k]))
    for copy in copies:
        copy.start()
    for copy in copies:
        copy.wait()


def windows(mine, width, parts):
    row_blocks, rows, cols, _ = mine.shape
    return pl.pallas_call(
        functools.partial(window_kernel, parts),
        out_shape=(pltpu.VMEM((row_blocks // 2, rows, cols, width), bf16),) * len(parts),
        in_specs=[in_place],
        out_specs=(whole,) * len(parts),
        scratch_shapes=[pltpu.SemaphoreType.DMA((len(parts),))],
        compiler_params=params(4),
        name="windows",
    )(hbm(mine))


def merge_kernel(own, came, out):
    for b in range(out.shape[0]):
        out[b] = (own[b].astype(f32) + came[b].astype(f32)).astype(bf16)


def merged(own, came):
    return pl.pallas_call(
        merge_kernel,
        out_shape=pltpu.VMEM(came.shape, bf16),
        in_specs=[whole] * 2,
        out_specs=whole,
        compiler_params=params(4),
        name="merge_far_part",
    )(vmem(own), vmem(came))


def gather_kernel(table, *refs):
    parts, (out, held, slots, sem) = refs[:6], refs[6:]
    copy = pltpu.make_async_copy(table, slots, sem)
    copy.start()
    half, rows, cols, width = parts[0].shape
    out[...] = jnp.zeros_like(out)
    for b in range(2 * half):
        own, near, far = parts[b // half * 3 : b // half * 3 + 3]
        total = own[b % half].astype(f32) + near[b % half].astype(f32)
        total = total + far[b % half].astype(f32)
        held[b] = total.reshape(rows * cols, width)
    copy.wait()
    for b in range(2 * half):
        for c in range(cols):
            piece = held[b, pl.ds(c, rows, stride=cols), :]
            out[slots[b * cols + c]] = piece.astype(out.dtype)


def gather_pieces(table, parts, slots):
    half, rows, cols, width = parts[0].shape
    return pl.pallas_call(
        gather_kernel,
        out_shape=jax.ShapeDtypeStruct((slots, rows, width), bf16),
        in_specs=[whole] + [whole] * len(parts),
        out_specs=whole,
        scratch_shapes=[
            pltpu.VMEM((2 * half, rows * cols, width), f32),
            pltpu.SMEM(table.shape, jnp.int32),
            pltpu.SemaphoreType.DMA(()),
        ],
        compiler_params=params(6),
        name="sum_and_gather",
    )(vmem(table), *[vmem(x) for x in parts])


def place_kernel(per_step, rows, cols, table, arrived, out, held):
    step = pl.program_id(0)
    for b in range(per_step):
        for c in range(cols):
            slot = table[(step * per_step + b) * cols + c]
            held[b, pl.ds(c, rows, stride=cols), :] = arrived[slot].astype(f32)
        out[b] = held[b].reshape(rows, cols, held.shape[-1]).astype(out.dtype)


def place_pieces(table, arrived, row_blocks, cols):
    slots, rows, width = arrived.shape
    per_step = 4
    return pl.pallas_call(
        functools.partial(place_kernel, per_step, rows, cols),
        out_shape=jax.ShapeDtypeStruct((row_blocks, rows, cols, width), bf16),
        grid=(row_blocks // per_step,),
        in_specs=[scalars, whole],
        out_specs=pl.BlockSpec((per_step, rows, cols, width), lambda i: (i, 0, 0, 0)),
        scratch_shapes=[pltpu.VMEM((per_step, rows * cols, width), f32)],
        compiler_params=params(4),
        name="place_pieces",
    )(table, vmem(arrived))


def early_kernel(slots, count, *refs):
    items = len(slots)
    ins, outs = refs[: 2 * items], refs[2 * items : 5 * items]
    roots, factors, lows, short, in_sem, out_sem = refs[5 * items :]

    def arrivals(k):
        return [
            pltpu.make_async_copy(ins[2 * k + i].at[slots[k]], held.at[k], in_sem.at[k, i])
            for i, held in enumerate((roots, factors))
        ]

    def departures(k):
        return [
            pltpu.make_async_copy(held.at[k], outs[3 * k + 1 + i], out_sem.at[k, i])
            for i, held in enumerate((lows, short))
        ]

    for i in range(2):
        for k in range(items):

            @pl.when(slots[k] < count[0])
            def _():
                arrivals(k)[i].start()

    for k in range(items):

        @pl.when(slots[k] < count[0])
        def _():
            (root_in, factor_in), going = arrivals(k), departures(k)
            root_in.wait()
            x = halves(roots[k])
            square = halves(mul3(x, x))
            fourth = halves(mul3(square, square))
            factor_in.wait()
            short[k] = factors[k].astype(bf16)
            going[1].start()
            outs[3 * k][...], lows[k] = halves(mul3(x, fourth))
            going[0].start()

    for k in range(items):

        @pl.when(slots[k] < count[0])
        def _():
            for copy in departures(k):
                copy.wait()


def early(count, *items):
    n = items[0][1].shape[1]
    many = len(items)
    made = pl.pallas_call(
        functools.partial(early_kernel, [t for t, _, _ in items]),
        out_shape=(
            pltpu.VMEM((n, n), bf16),
            stored(n, n, dtype=bf16),
            stored(n, n, dtype=bf16),
        )
        * many,
        in_specs=[scalars] + [in_place] * (2 * many),
        out_specs=(whole, in_place, in_place) * many,
        scratch_shapes=[
            pltpu.VMEM((many, n, n), f32),
            pltpu.VMEM((many, n, n), f32),
            pltpu.VMEM((many, n, n), bf16),
            pltpu.VMEM((many, n, n), bf16),
            pltpu.SemaphoreType.DMA((many, 2)),
            pltpu.SemaphoreType.DMA((many, 2)),
        ],
        compiler_params=params(24),
        cost_estimate=pl.CostEstimate(
            flops=many * 9 * 2 * n**3,
            bytes_accessed=many * 12 * n * n,
            transcendentals=0,
        ),
        name="early_products",
    )(count, *[hbm(x) for _, *pair in items for x in pair])
    return [made[3 * k : 3 * k + 3] for k in range(many)]


def assembled(pieces, t, block):
    parts, shards, _, rows, width = pieces.shape
    for z in range(parts):
        block[:, z * width : (z + 1) * width] = pieces[z, :, t].reshape(
            shards * rows, width
        )
    return block[...]


def quarter_scale(factor):
    n, tile = factor.shape[0], 128
    on = lax.broadcasted_iota(jnp.int32, (tile, tile), 0)
    on = on == lax.broadcasted_iota(jnp.int32, (tile, tile), 1)
    total = factor[:tile, :tile]
    for d in range(tile, n, tile):
        total = total + factor[d : d + tile, d : d + tile]
    return (0.25 * n) / jnp.sum(jnp.where(on, total, 0.0))


def update_kernel(gain, slots, count, pieces, xl, xr, *refs):
    ready, refs = refs[: 4 * slots], refs[4 * slots :]
    out, blocks, roots, factors, made, in_sem, out_sem = refs
    parts, shards, _, rows, width = made.shape
    n = parts * width
    roots_in = (xl, xr)

    def arrivals(t):
        copies = []
        for k in range(2):
            sources = (
                (ready[4 * t + 2 * k + 1], factors.at[t, k]),
                (roots_in[k].at[t], roots.at[t, k]),
            )
            for a, b in sources:
                copies.append(pltpu.make_async_copy(a, b, in_sem.at[t, len(copies)]))
        return copies

    def departure(h):
        span = pl.ds(h * parts // 2, parts // 2)
        return pltpu.make_async_copy(made.at[span], out.at[span], out_sem.at[h])

    def root(t, k, gram, copies):
        copies[2 * k].wait()
        factor = factors[t, k].astype(f32) + (gain / decay_rate) * gram
        scale = quarter_scale(factor)
        product = mul(ready[4 * t + 2 * k][...], factor.astype(bf16))
        copies[2 * k + 1].wait()
        return (1.25 * roots[t, k] - scale * product).astype(bf16)

    def work(ts):
        copies = {t: arrivals(t) for t in ts}
        for k in range(4):
            for t in ts:
                copies[t][k].start()
        g, part, side = {}, {}, {}
        for t in ts:
            g[t] = assembled(pieces, t, blocks.at[t])
        grams = {t: (mul_t(g[t], g[t]), t_mul(g[t], g[t])) for t in ts}
        for t in ts:
            side[t] = root(t, 0, grams[t][0], copies[t])
            part[t] = mul(side[t], g[t]).astype(bf16)
        for t in ts:
            side[t] = root(t, 1, grams[t][1], copies[t])
        for h in range(2):
            for t in ts:
                done = mul(part[t], side[t][:, h * n // 2 : (h + 1) * n // 2]).astype(bf16)
                for k in range(parts // 2):
                    made[h * parts // 2 + k, :, t] = done[
                        :, k * width : (k + 1) * width
                    ].reshape(shards, rows, width)
            departure(h).start()

    for live in range(slots + 1):

        @pl.when(count[0] == live)
        def _():
            for t in range(live, slots):
                made[:, :, t] = jnp.zeros_like(made[:, :, t])
            if live:
                work(range(live))
            else:
                departure(0).start()
                departure(1).start()

    departure(0).wait()
    departure(1).wait()


def update_pieces(gain, count, pieces, xl, xr, ready):
    slots = pieces.shape[2]
    n = xl.shape[1]
    inputs = []
    for sides in ready:
        for high, _, factor in sides:
            inputs += [vmem(high), hbm(factor)]
    return pl.pallas_call(
        functools.partial(update_kernel, gain, slots),
        out_shape=stored(*pieces.shape, dtype=bf16),
        in_specs=[scalars, whole] + [in_place] * 2 + [whole, in_place] * (2 * slots),
        out_specs=in_place,
        scratch_shapes=[
            pltpu.VMEM((slots, n, n), bf16),
            pltpu.VMEM((slots, 2, n, n), f32),
            pltpu.VMEM((slots, 2, n, n), bf16),
            pltpu.VMEM(pieces.shape, bf16),
            pltpu.SemaphoreType.DMA((slots, 4)),
            pltpu.SemaphoreType.DMA((2,)),
        ],
        compiler_params=params(36),
        name="update_pieces",
    )(count, vmem(pieces), hbm(xl), hbm(xr), *inputs)


def state_kernel(gain, slots, count, pieces, left, right, xl, xr, *refs):
    ready, refs = refs[: 4 * slots], refs[4 * slots :]
    outs, refs = refs[:4], refs[4:]
    block, fives, made, in_sem, out_sem = refs
    olds = (left, right, xl, xr)

    def arrivals(t):
        sources = [(a.at[t], made.at[t, k]) for k, a in enumerate(olds)]
        sources += [(a, fives.at[t, k]) for k, a in enumerate(ready[4 * t : 4 * t + 4])]
        return [
            pltpu.make_async_copy(a, b, in_sem.at[t, k]) for k, (a, b) in enumerate(sources)
        ]

    def departures(t):
        return [
            pltpu.make_async_copy(made.at[t, k], out.at[t], out_sem.at[t, k])
            for k, out in enumerate(outs)
        ]

    for t in range(slots):
        for copy in arrivals(t)[:4]:
            copy.start()

        @pl.when(t < count[0])
        def _():
            for copy in arrivals(t)[4:]:
                copy.start()

    for t in range(slots):
        for copy in arrivals(t)[:4]:
            copy.wait()

        @pl.when(t < count[0])
        def _():
            g = assembled(pieces, t, block)
            for copy in arrivals(t)[4:]:
                copy.wait()
            for k in range(2):
                gram = t_mul(g, g) if k else mul_t(g, g)
                made[t, k] = decay_rate * made[t, k] + gain * gram
                departures(t)[k].start()
                factor = made[t, k]
                product = mul3((fives[t, 2 * k], fives[t, 2 * k + 1]), halves(factor))
                made[t, 2 + k] = 1.25 * made[t, 2 + k] - quarter_scale(factor) * product
                departures(t)[2 + k].start()

        @pl.when(t >= count[0])
        def _():
            for copy in departures(t):
                copy.start()

    for t in range(slots):
        for copy in departures(t):
            copy.wait()


def new_state(gain, count, pieces, state, ready):
    slots, n, _ = state[0].shape
    inputs = [hbm(x) for sides in ready for made in sides for x in made[:2]]
    return pl.pallas_call(
        functools.partial(state_kernel, gain, slots),
        out_shape=(stored(slots, n, n),) * 4,
        in_specs=[scalars, whole] + [in_place] * (4 + len(inputs)),
        out_specs=(in_place,) * 4,
        scratch_shapes=[
            pltpu.VMEM((n, n), bf16),
            pltpu.VMEM((slots, 4, n, n), bf16),
            pltpu.VMEM((slots, 4, n, n), f32),
            pltpu.SemaphoreType.DMA((slots, 8)),
            pltpu.SemaphoreType.DMA((slots, 4)),
        ],
        compiler_params=params(36),
        cost_estimate=pl.CostEstimate(
            flops=slots * 8 * 2 * n**3,
            bytes_accessed=slots * 36 * n * n,
            transcendentals=0,
        ),
        name="new_state",
    )(count, vmem(pieces), *[hbm(x) for x in state], *inputs)


def body(
    gradients, owner_list, row_offset, col_offset, left_factor, right_factor, left_root, right_root
):
    replicas = lax.axis_size("dp")
    shards = lax.axis_size("shard")
    slots, n, _ = left_factor.shape
    _, row_blocks, rows, cols, _ = gradients.shape
    width = n // replicas
    gain = (1.0 - decay_rate) / n
    mine = gradients[0]

    def hop(x, step):
        return lax.ppermute(x, "dp", [(i, (i + step) % replicas) for i in range(replicas)])

    half = row_blocks // 2
    far = lax.rem(lax.axis_index("dp") + 2, replicas) * width
    far = lax.dynamic_slice_in_dim(mine, far, width, axis=3)
    far_low, far_high = far[:half], far[half:]
    far_low, far_high = hop(far_low, 1), hop(far_high, -1)
    near_high, near_low, own_low, own_high, last_low, last_high = windows(
        mine, width, ((half, 1), (0, 3), (0, 1), (half, 3), (0, 0), (half, 0))
    )
    near_high, near_low = hop(near_high, 1), hop(near_low, -1)

    entries = jnp.arange(owner_list.shape[0], dtype=jnp.int32)
    same = owner_list[None, :] == owner_list[:, None]
    earlier = jnp.sum(same & (entries[None, :] < entries[:, None]), axis=1)
    slot_of = owner_list * slots + earlier.astype(jnp.int32)
    block_of = row_offset // n * cols + col_offset // n
    table = jnp.sum(
        jnp.where(block_of[None, :] == entries[:, None], slot_of[None, :], 0), axis=1
    ).astype(jnp.int32)
    owner = lax.axis_index(("dp", "shard"))
    count = jnp.sum((owner_list == owner).astype(jnp.int32)).reshape(1)

    far_low = hop(merged(own_low, far_low), 1)
    far_high = hop(merged(own_high, far_high), -1)
    (first,) = early(count, (0, left_root, left_factor))
    arrived = (last_low, near_low, far_low, last_high, near_high, far_high)
    arrived, first = lax.optimization_barrier((arrived, first))

    all_slots = replicas * shards * slots
    outgoing = gather_pieces(table, arrived, all_slots)
    incoming = lax.all_to_all(outgoing, ("dp", "shard"), split_axis=0, concat_axis=0, tiled=True)
    sides = ((left_root, left_factor), (right_root, right_factor))
    rest = [(t, *side) for t in range(slots) for side in sides][1:]
    ready = [first, *early(count, *rest)]
    incoming, ready = lax.optimization_barrier((incoming, ready))
    ready = [ready[2 * t : 2 * t + 2] for t in range(slots)]
    pieces = incoming.reshape(replicas, shards, slots, rows, width)
    state = (left_factor, right_factor, left_root, right_root)
    outbound = update_pieces(gain, count, pieces, left_root, right_root, ready)
    returned = lax.all_to_all(
        outbound.reshape(all_slots, rows, width),
        ("dp", "shard"), split_axis=0, concat_axis=0, tiled=True,
    )
    new_left, new_right, new_xl, new_xr = new_state(gain, count, pieces, state, ready)
    update = place_pieces(table, returned, row_blocks, cols)
    return update, new_left, new_right, new_xl, new_xr


def solution(mesh):
    slots = P(("dp", "shard"), None, None)
    in_specs = (P("dp", None, "shard", None, None), P(), P(), P(), slots, slots, slots, slots)
    out_specs = (P(None, "shard", None, "dp"), slots, slots, slots, slots)
    return jax.shard_map(body, mesh=mesh, in_specs=in_specs, out_specs=out_specs, check_vma=False)
```
